32 devices in a mesh: shard: 4 (over z), ctx: 2 (over x), tp: 4 (over y, core).
Axes of the slice: x: 2, y: 2, z: 4, core: 2. Of those that a mesh axis runs over, the one named last changes fastest.
Arguments:
- inputs: bfloat16 [8, 1024, 1024], P('shard', 'ctx', 'tp'), may hold values from -6 to 6
- adapter_id: int32 [8], P('shard'), may hold values from 0 to 7
- cotangent: bfloat16 [8, 1024, 1024], P('shard', 'ctx', 'tp'), may hold values from -6 to 6
- ffn1_in: bfloat16 [1024, 4096], P('shard', 'tp'), may hold values from -0.1875 to 0.1875
- ffn1_out: bfloat16 [1024, 4096], P('shard', 'tp'), may hold values from -0.09375 to 0.09375
- query_w: bfloat16 [1024, 1024], P('shard', 'tp'), may hold values from -0.1875 to 0.1875
- key_w: bfloat16 [1024, 1024], P('shard', 'tp'), may hold values from -0.1875 to 0.1875
- value_w: bfloat16 [1024, 1024], P('shard', 'tp'), may hold values from -0.1875 to 0.1875
- out_w: bfloat16 [1024, 1024], P('shard', 'tp'), may hold values from -0.75 to 0.75
- conv_in_w: bfloat16 [1024, 2, 1024], P('shard', None, 'tp'), may hold values from -0.1875 to 0.1875
- conv_kernel: bfloat16 [31, 1024], P(None, 'tp'), may hold values from -1 to 1
- conv_out_w: bfloat16 [1024, 1024], P('shard', 'tp'), may hold values from -0.1875 to 0.1875
- ffn2_in: bfloat16 [1024, 4096], P('shard', 'tp'), may hold values from -0.1875 to 0.1875
- ffn2_out: bfloat16 [1024, 4096], P('shard', 'tp'), may hold values from -0.09375 to 0.09375
- distance_table: bfloat16 [73, 64], replicated, may hold values from -6 to 6
- adapt_down: bfloat16 [8, 1024, 128], replicated, may hold values from -0.1875 to 0.1875
- adapt_down_ff: bfloat16 [2, 4096, 128], replicated, may hold values from -0.09375 to 0.09375
- adapt_up: bfloat16 [9, 128, 1024], replicated, may hold values from -1.5 to 1.5
- adapt_up_ff: bfloat16 [2, 128, 4096], replicated, may hold values from -1.5 to 1.5
Outputs:
- output: bfloat16 [8, 1024, 1024], P('shard', 'ctx', 'tp')
- input_grad: float32 [8, 1024, 1024], P('shard', 'ctx', 'tp')
- down_grad: float32 [8, 1024, 128], replicated
- down_ff_grad: float32 [2, 4096, 128], replicated
- up_grad: float32 [9, 128, 1024], replicated
- up_ff_grad: float32 [2, 128, 4096], replicated
The draws below stay inside these ranges and needn't reach their ends.
Inputs may be any that keep to these rules, and one draw needn't show every extreme that they name: adapter_id names one adapter for each sequence.
All inputs are finite; a program needn't handle non-finite values.
Results may differ from the reference program's by a relative error of at most 0.02.
Values may be sent and summed in bfloat16 or wider, within the bound.
No kernel may reach another device: no remote copies, remote signals or barrier semaphores. Data moves between devices by JAX's collectives and lax.ppermute only.
A program may use at most 256 MiB of HBM per device.

```python
import jax
import jax.numpy as jnp
from jax import lax

D = 1024
HEADS = 16
HEAD = 64
FF = 4096
KERNEL = 31
LEFT = 64
RIGHT = 8
NADAPT = 8
RANK = 16
LEN = 1024
NR = 128
NREL = 73
SEQS = 8
N_TP = 4


def set_ends(drawn, rng, low, top_value):
    place = [jax.random.randint(jax.random.fold_in(rng, axis), (), 0, length) for axis, length in enumerate(drawn.shape)]
    longest = drawn.shape.index(max(drawn.shape))
    next_to = place[:longest] + [(place[longest] + 1) % drawn.shape[longest]] + place[longest + 1:]
    return drawn.at[tuple(place)].set(low).at[tuple(next_to)].set(top_value)


def shard_levels(stream_key, shape, cuts, least, high):
    level, own = 1.0, jax.random.fold_in(stream_key, 6)
    for axis_at, shards_of in cuts:
        steps = jnp.exp(jax.random.uniform(jax.random.fold_in(own, axis_at), (shards_of,), jnp.float32, least / len(cuts), high / len(cuts)))
        level = level * jnp.repeat(steps, shape[axis_at] // shards_of).reshape([-1 if axis == axis_at else 1 for axis in range(len(shape))])
    return level


def gaussian(own_key, dims, deviation, limit, cuts=(), kind=jnp.bfloat16):
    values = deviation * jax.random.normal(own_key, dims, jnp.float32)
    if cuts:
        values = values * shard_levels(own_key, dims, cuts, -0.22, 0.18)
    return jnp.clip(values, -limit, limit).astype(kind)


def setup_inputs(seed: int = 0) -> dict:
    splits = jax.random.split(jax.random.key(seed), 20)
    return {
        "inputs": gaussian(splits[0], (SEQS, LEN, D), 1.0, 6.0, ((0, 4), (1, 2), (2, 4))),
        "adapter_id": set_ends(jax.random.randint(splits[1], (SEQS,), 0, NADAPT), jax.random.fold_in(splits[1], 1), 0, NADAPT - 1).astype(jnp.int32),
        "cotangent": gaussian(splits[2], (SEQS, LEN, D), 1.0, 6.0, ((0, 4), (1, 2), (2, 4))),
        "ffn1_in": gaussian(splits[3], (D, FF), D ** -0.5, 0.1875, ((0, 4), (1, 4))),
        "ffn1_out": gaussian(splits[4], (D, FF), FF ** -0.5, 0.09375, ((0, 4), (1, 4))),
        "query_w": gaussian(splits[5], (D, D), D ** -0.5, 0.1875, ((0, 4), (1, 4))),
        "key_w": gaussian(splits[6], (D, D), D ** -0.5, 0.1875, ((0, 4), (1, 4))),
        "value_w": gaussian(splits[7], (D, D), D ** -0.5, 0.1875, ((0, 4), (1, 4))),
        "out_w": gaussian(splits[8], (D, D), HEAD ** -0.5, 0.75, ((0, 4), (1, 4))),
        "conv_in_w": gaussian(splits[9], (D, 2, D), D ** -0.5, 0.1875, ((0, 4), (2, 4))),
        "conv_kernel": gaussian(splits[10], (KERNEL, D), KERNEL ** -0.5, 1.0, ((1, 4),)),
        "conv_out_w": gaussian(splits[11], (D, D), D ** -0.5, 0.1875, ((0, 4), (1, 4))),
        "ffn2_in": gaussian(splits[12], (D, FF), D ** -0.5, 0.1875, ((0, 4), (1, 4))),
        "ffn2_out": gaussian(splits[13], (D, FF), FF ** -0.5, 0.09375, ((0, 4), (1, 4))),
        "distance_table": gaussian(splits[14], (NREL, HEAD), 1.0, 6.0),
        "adapt_down": gaussian(splits[15], (8, D, NR), D ** -0.5, 0.1875),
        "adapt_down_ff": gaussian(splits[16], (2, FF, NR), FF ** -0.5, 0.09375),
        "adapt_up": gaussian(splits[17], (9, NR, D), RANK ** -0.5, 1.5),
        "adapt_up_ff": gaussian(splits[18], (2, NR, FF), RANK ** -0.5, 1.5),
    }


HIGH = lax.Precision.HIGHEST
eps = 1e-05

@jax.custom_vjp
def low(v):
    return lax.optimization_barrier(v.astype(jnp.bfloat16)).astype(jnp.float32)

@jax.custom_vjp
def low_back(v):
    return v

def low_keep(v):
    return (low(v), None)

def low_pass(kept, grad):
    return (grad,)

def back_keep(v):
    return (v, None)

def back_low(kept, grad):
    return (low(grad),)
low.defvjp(low_keep, low_pass)
low_back.defvjp(back_keep, back_low)

def product(first, second):
    return jnp.dot(first, second, precision=HIGH)

def normalize(value):
    mean = lax.optimization_barrier(jnp.mean(value, axis=-1, keepdims=True))
    square = lax.optimization_barrier(jnp.mean(value * value, axis=-1, keepdims=True))
    return (value - mean) * lax.rsqrt(square - mean * mean + eps)

def swish(value):
    return value * jax.nn.sigmoid(value)

def column_adapter(rows, down, up, mask):
    reduced = low(product(rows, down) * mask)
    copies = low_back(jnp.broadcast_to(reduced, (N_TP,) + reduced.shape))
    rank_all, halves, width = up.shape
    groups = up.reshape(rank_all, halves, N_TP, width // N_TP)
    result = jnp.einsum('glr,rhgo->lhgo', copies, groups, precision=HIGH)
    return result.reshape(rows.shape[0], halves, width)

def row_adapter(pieces, down, up, mask):
    count, width = pieces.shape
    split = pieces.reshape(count, N_TP, width // N_TP)
    downs = down.reshape(N_TP, width // N_TP, down.shape[1])
    reduced = jnp.einsum('lgi,gir->glr', split, downs, precision=HIGH)
    reduced = low(low_back(reduced * mask))
    return jnp.einsum('glr,ro->lo', reduced, up, precision=HIGH)

def column(rows, weight, down, up, mask):
    return product(rows, weight) + column_adapter(rows, down, up[:, None, :], mask)[:, 0, :]

def row(pieces, weight, down, up, mask):
    return product(pieces, weight.T) + row_adapter(pieces, down, up, mask)

def feed_forward(resid, weight_in, weight_out, down_in, up_in, down_out, up_out, mask):
    rows = low(normalize(resid))
    pre = low_back(column(rows, weight_in, down_in, up_in, mask))
    active = low(swish(pre))
    branch = low_back(row(active, weight_out, down_out, up_out, mask))
    return resid + 0.5 * branch

def attention(resid, query_w, key_w, value_w, out_w, table, down, up, mask):
    rows = low(normalize(resid))
    count = rows.shape[0]

    def project(weight, index):
        raw = column(rows, weight, down[index], up[index - 1], mask)
        return low(low_back(raw)).reshape(count, HEADS, HEAD)
    queries = project(query_w, 1)
    keys = project(key_w, 2)
    values = project(value_w, 3)
    near = jnp.einsum('lhe,re->hlr', queries, table, precision=HIGH)
    places = jnp.arange(count, dtype=jnp.int32)
    distance = jnp.clip(places[None, :] - places[:, None], -LEFT, RIGHT) + LEFT
    index = jnp.broadcast_to(distance, (HEADS, count, count))
    gathered = jnp.take_along_axis(near, index, axis=2)
    direct = jnp.einsum('lhe,mhe->hlm', queries, keys, precision=HIGH)
    scores = (direct + gathered) * HEAD ** (-0.5)
    probs = low(jax.nn.softmax(low_back(scores), axis=-1))
    mixed = jnp.einsum('hlm,mhe->lhe', probs, values, precision=HIGH).reshape(count, HEADS * HEAD)
    mixed = low(low_back(mixed))
    branch = low_back(row(mixed, out_w, down[6], up[5], mask))
    return resid + branch

def convolve(resid, conv_in_w, conv_kernel, conv_out_w, down, up, mask):
    rows = low(normalize(resid))
    count = rows.shape[0]
    pair_up = jnp.transpose(up[3:5], (1, 0, 2))
    pair = product(rows, conv_in_w.reshape(D, 2 * D)).reshape(count, 2, D)
    pair = low_back(pair + column_adapter(rows, down[4], pair_up, mask))
    gated = pair[:, 0] * jax.nn.sigmoid(pair[:, 1])
    padded = jnp.concatenate([jnp.zeros((KERNEL - 1, D), jnp.float32), gated], axis=0)
    mixed = conv_kernel[0] * padded[0:count]
    for tap in range(1, KERNEL):
        mixed = mixed + conv_kernel[tap] * padded[tap:tap + count]
    active = low(swish(normalize(mixed)))
    branch = low_back(row(active, conv_out_w, down[7], up[6], mask))
    return resid + branch

def layer(resid, down, down_ff, up, up_ff, frozen, mask):
    ffn1_in, ffn1_out, query_w, key_w, value_w, out_w, conv_in_w, conv_kernel, conv_out_w, ffn2_in, ffn2_out, distance_table = frozen
    first = feed_forward(resid, ffn1_in, ffn1_out, down[0], up_ff[0], down_ff[0], up[7], mask)
    second = attention(first, query_w, key_w, value_w, out_w, distance_table, down, up, mask)
    third = convolve(second, conv_in_w, conv_kernel, conv_out_w, down, up, mask)
    fourth = feed_forward(third, ffn2_in, ffn2_out, down[5], up_ff[1], down_ff[1], up[8], mask)
    return normalize(fourth)

def reference(inputs, adapter_id, cotangent, ffn1_in, ffn1_out, query_w, key_w, value_w, out_w, conv_in_w, conv_kernel, conv_out_w, ffn2_in, ffn2_out, distance_table, adapt_down, adapt_down_ff, adapt_up, adapt_up_ff):
    frozen = tuple((weight.astype(jnp.float32) for weight in (ffn1_in, ffn1_out, query_w, key_w, value_w, out_w, conv_in_w, conv_kernel, conv_out_w, ffn2_in, ffn2_out, distance_table)))
    trained = tuple((weight.astype(jnp.float32) for weight in (adapt_down, adapt_down_ff, adapt_up, adapt_up_ff)))
    numbers = jnp.arange(NADAPT, dtype=jnp.int32)

    def per_sequence(totals, item):
        resid, ident, grad_out = item
        mask = jnp.repeat((numbers == ident).astype(jnp.float32), RANK)

        def run(value, down, down_ff, up, up_ff):
            return layer(value, down, down_ff, up, up_ff, frozen, mask)
        result, pull = jax.vjp(run, resid, *trained)
        grads = pull(grad_out)
        totals = tuple((total + grad for total, grad in zip(totals, grads[1:])))
        return (totals, (result.astype(jnp.bfloat16), grads[0]))
    zeros = tuple((jnp.zeros_like(weight) for weight in trained))
    totals, (output, input_grad) = lax.scan(per_sequence, zeros, (inputs.astype(jnp.float32), adapter_id, cotangent.astype(jnp.float32)))
    return (output, input_grad, totals[0], totals[1], totals[2], totals[3])
```

```python
import jax
import jax.numpy as jnp
from jax import lax
from jax.experimental import pallas as pl
from jax.experimental.pallas import tpu as pltpu
from jax.sharding import PartitionSpec as P

LEFT = 64
RIGHT = 8
NADAPT = 8
RANK = 16
HEAD = 64
LANES = 128
eps = 1e-05
BF = jnp.bfloat16
F32 = jnp.float32

CORE = [(0, 1), (1, 0), (2, 3), (3, 2)]
PAIR = [(0, 2), (2, 0), (1, 3), (3, 1)]
SIDE = [(0, 1), (1, 0)]
ACROSS = [(s * 4 + t, (1 - s) * 4 + (t ^ 2)) for s in range(2) for t in range(4)]


def block_at(block, core):
    return (block // 2) * 4 + (block % 2) * 2 + core


NEXT = [(block_at(n, k), block_at(n + 1, k)) for n in range(3) for k in range(2)]
BEFORE = [(block_at(n + 1, k), block_at(n, k)) for n in range(3) for k in range(2)]


def by_core(value):
    return lax.ppermute(value, "tp", CORE)


def by_pair(value):
    return lax.ppermute(value, "tp", PAIR)


def by_side(value):
    return lax.ppermute(value, "ctx", SIDE)


def across(value):
    return lax.ppermute(value, ("ctx", "tp"), ACROSS)


def wide_table(table):
    place = jnp.arange(4*LANES, dtype=jnp.int32)
    index = jnp.where(place < 3*LANES, jnp.clip(place - LEFT, 0, LEFT+RIGHT), 0)
    pick = (index[:, None] == jnp.arange(table.shape[0], dtype=jnp.int32)[None, :]).astype(BF)
    rows = jnp.dot(pick, table, preferred_element_type=F32).astype(BF)
    return jnp.concatenate([rows, rows], axis=1)

def load_blocks(b_ref, sources, target, sems, parts):
    copies=[]
    for j, source in enumerate(sources):
        rows = source.shape[0]; cols = source.shape[1]//parts
        for part in range(parts):
            copies.append(pltpu.make_async_copy(
                source.at[:, part*cols:(part+1)*cols],
                target.at[part, pl.ds(pl.multiple_of((b_ref[0] ^ j)*rows, rows), rows), :],
                sems.at[j*parts+part]))
    for c in copies: c.start()
    for c in copies: c.wait()

def window(r0, length):
    lo=max(r0-LANES,0); hi=min(r0+2*LANES,length)
    return lo,hi

def biased(s, near, p, rows, length):
    parts=[]
    for sub in range(rows//LANES):
        r0=p*rows+sub*LANES
        e=near[sub*LANES:(sub+1)*LANES]
        band=pltpu.roll(e, 0, 1, stride=1, stride_axis=0)
        lo,hi=window(r0,length)
        pieces=[]
        if lo>0: pieces.append(jnp.broadcast_to(e[:,0:1],(LANES,lo)))
        pieces.append(band[:, lo-r0+LANES:hi-r0+LANES])
        if hi<length: pieces.append(jnp.broadcast_to(e[:,2*LANES-1:2*LANES],(LANES,length-hi)))
        parts.append(jnp.concatenate(pieces,axis=1))
    return s+jnp.concatenate(parts,axis=0)


def fwd_kernel(b_ref, s0,s1,s2,s3, text_ref, o_ref, lse_ref, qkv, sems):
    dc=pl.program_id(0); k=pl.program_id(1)
    @pl.when((dc==0)&(k==0))
    def _(): load_blocks(b_ref,(s0,s1,s2,s3),qkv,sems,2)
    rows=o_ref.shape[1]; length=qkv.shape[1]
    own=(lax.broadcasted_iota(jnp.int32,(rows,LANES),1)//64)==k
    key=qkv[dc,:,LANES:2*LANES]; val=qkv[dc,:,2*LANES:]
    for p in range(length//rows):
        q=qkv[dc,p*rows:(p+1)*rows,0:LANES].astype(F32)*0.125
        q=jnp.where(own,q,0.0).astype(BF)
        s=biased(nt(q,key),nt(q,text_ref[...]),p,rows,length)
        top=jnp.max(s,axis=-1,keepdims=True)
        e=jnp.exp(s-top)
        tot=jnp.sum(e,axis=-1,keepdims=True)
        o=jnp.dot(e.astype(BF),val,preferred_element_type=F32)/tot
        o=o.astype(BF)
        slot=p^b_ref[0]
        @pl.when(k==0)
        def _(): o_ref[slot]=o
        @pl.when(k==1)
        def _(): o_ref[slot]=jnp.where(own,o,o_ref[slot])
        lse_ref[0,p*rows:(p+1)*rows,:]=top+jnp.log(tot)

def attend(b, slots, text):
    rows=slots[0].shape[0]; n=len(slots); length=rows*n
    anys=[pl.BlockSpec(memory_space=pl.ANY)]*n
    return pl.pallas_call(
        fwd_kernel,
        grid_spec=pltpu.PrefetchScalarGridSpec(
            num_scalar_prefetch=1, grid=(2,2),
            in_specs=anys+[pl.BlockSpec(text.shape,lambda d,k,b:(0,0))],
            out_specs=(pl.BlockSpec((n,rows,LANES),lambda d,k,b:(0,0,d)),
                       pl.BlockSpec((1,length,1),lambda d,k,b:(2*d+k,0,0))),
            scratch_shapes=[pltpu.VMEM((2,length,3*LANES),BF),pltpu.SemaphoreType.DMA((2*n,))]),
        out_shape=(jax.ShapeDtypeStruct((n,rows,2*LANES),BF),jax.ShapeDtypeStruct((4,length,1),F32)),
        compiler_params=pltpu.CompilerParams(vmem_limit_bytes=48<<20),
        name="attend",
        cost_estimate=pl.CostEstimate(flops=4*4*length*length*64,bytes_accessed=length*8*LANES*2,transcendentals=4*length*length),
    )(b,*slots,text)

def bwd_kernel(b_ref, s0,s1,s2,s3, g0,g1,g2,g3, text_ref, lse_ref, out_ref, qkv, gout, dq_acc, dk_acc, dv_acc, sems, gsems):
    dc=pl.program_id(0); k=pl.program_id(1)
    @pl.when((dc==0)&(k==0))
    def _():
        load_blocks(b_ref,(s0,s1,s2,s3),qkv,sems,2)
        load_blocks(b_ref,(g0,g1,g2,g3),gout,gsems,2)
    rows=out_ref.shape[1]; length=qkv.shape[1]
    own=(lax.broadcasted_iota(jnp.int32,(rows,LANES),1)//64)==k
    key=qkv[dc,:,LANES:2*LANES]; val=qkv[dc,:,2*LANES:]
    text=text_ref[...]
    turn=((lax.broadcasted_iota(jnp.int32,(LANES,LANES),0)+lax.broadcasted_iota(jnp.int32,(LANES,LANES),1))==LANES-1).astype(BF)
    @pl.when(k==0)
    def _():
        dk_acc[...]=jnp.zeros_like(dk_acc); dv_acc[...]=jnp.zeros_like(dv_acc)
    for p in range(length//rows):
        span=slice(p*rows,(p+1)*rows)
        q=qkv[dc,span,0:LANES].astype(F32)*0.125
        q=jnp.where(own,q,0.0).astype(BF)
        g=jnp.where(own,gout[dc,span,:].astype(F32),0.0).astype(BF)
        s=biased(nt(q,key),nt(q,text),p,rows,length)
        pr=jnp.exp(s-lse_ref[0,span,:])
        dp=nt(g,val)
        w=pr*dp
        ds=(w-pr*jnp.sum(w,axis=-1,keepdims=True)).astype(BF)
        dv_acc[...]+=tn(g,pr.astype(BF))
        dk_acc[...]+=tn(q,ds)
        dq=jnp.dot(ds,key,preferred_element_type=F32)
        extra=[]
        t_lo=text[0:1,:].astype(F32); t_hi=text[2*LANES-1:2*LANES,:].astype(F32)
        for sub in range(rows//LANES):
            r0=p*rows+sub*LANES
            lo,hi=window(r0,length)
            d=ds[sub*LANES:(sub+1)*LANES].astype(F32)
            pieces=[]
            if lo-r0+LANES>0: pieces.append(jnp.zeros((LANES,lo-r0+LANES),F32))
            pieces.append(d[:,lo:hi])
            pieces.append(jnp.zeros((LANES,4*LANES-(hi-r0+LANES)),F32))
            w=jnp.concatenate(pieces,axis=1)
            w=jnp.dot(turn,w.astype(BF),preferred_element_type=F32)
            w=pltpu.roll(w,3*LANES+1,1,stride=1,stride_axis=0)
            w=jnp.dot(turn,w.astype(BF),preferred_element_type=F32)
            x=jnp.dot(w.astype(BF),text,preferred_element_type=F32)
            if lo>0: x+=jnp.sum(d[:,:lo],axis=-1,keepdims=True)*t_lo
            if hi<length: x+=jnp.sum(d[:,hi:],axis=-1,keepdims=True)*t_hi
            extra.append(x)
        dq=(dq+jnp.concatenate(extra,axis=0))*0.125
        dq_acc[span,:]=jnp.where(own,dq,dq_acc[span,:])
    @pl.when(k==1)
    def _():
        for p in range(length//rows):
            slot=p^b_ref[0]; span=slice(p*rows,(p+1)*rows)
            out_ref[slot,:,0:LANES]=dq_acc[span,:].astype(BF)
            out_ref[slot,:,LANES:2*LANES]=dk_acc[:,span].T.astype(BF)
            out_ref[slot,:,2*LANES:]=dv_acc[:,span].T.astype(BF)

def attend_back(b, slots, grads, text, lse):
    rows=slots[0].shape[0]; n=len(slots); length=rows*n
    anys=[pl.BlockSpec(memory_space=pl.ANY)]*(2*n)
    return pl.pallas_call(
        bwd_kernel,
        grid_spec=pltpu.PrefetchScalarGridSpec(
            num_scalar_prefetch=1, grid=(2,2),
            in_specs=anys+[pl.BlockSpec(text.shape,lambda d,k,b:(0,0)),pl.BlockSpec((1,length,1),lambda d,k,b:(2*d+k,0,0))],
            out_specs=pl.BlockSpec((n,rows,3*LANES),lambda d,k,b:(0,0,d)),
            scratch_shapes=[pltpu.VMEM((2,length,3*LANES),BF),pltpu.VMEM((2,length,LANES),BF),
              pltpu.VMEM((length,LANES),F32),pltpu.VMEM((LANES,length),F32),pltpu.VMEM((LANES,length),F32),
              pltpu.SemaphoreType.DMA((2*n,)),pltpu.SemaphoreType.DMA((2*n,))]),
        out_shape=jax.ShapeDtypeStruct((n,rows,6*LANES),BF),
        compiler_params=pltpu.CompilerParams(vmem_limit_bytes=56<<20),
        name="attend_back",
        cost_estimate=pl.CostEstimate(flops=10*4*length*length*64,bytes_accessed=length*14*LANES*2,transcendentals=4*length*length),
    )(b,*slots,*grads,text,lse)


def nn(first, second):
    return jnp.dot(first, second, preferred_element_type=F32)


def nt(first, second):
    return lax.dot_general(first, second, (((1,), (1,)), ((), ())), preferred_element_type=F32)


def tn(first, second):
    return lax.dot_general(first, second, (((0,), (0,)), ((), ())), preferred_element_type=F32)


def normalize(value):
    mean = jnp.mean(value, axis=-1, keepdims=True)
    square = jnp.mean(value * value, axis=-1, keepdims=True)
    scale = lax.rsqrt(square - mean * mean + eps)
    return ((value - mean) * scale, scale)


def normalize_back(grad, normed, scale):
    mean = jnp.mean(grad, axis=-1, keepdims=True)
    cross = jnp.mean(grad * normed, axis=-1, keepdims=True)
    return scale * (grad - mean - normed * cross)


def swish_slope(value, sigma):
    return sigma + value * sigma * (1.0 - sigma)


def mask_row(adapter):
    lanes = lax.broadcasted_iota(jnp.int32, (1, NADAPT * RANK), 1)
    return (lanes // RANK == adapter).astype(F32)


def chosen_rows(adapter):
    shape = (RANK, NADAPT * RANK)
    lanes = lax.broadcasted_iota(jnp.int32, shape, 1)
    rows = lax.broadcasted_iota(jnp.int32, shape, 0)
    return (lanes == rows + adapter * RANK).astype(BF)


def compact(pick, value):
    return nt(pick, value).astype(BF)


class Fetches:
    def __init__(self, sems):
        self.sems = sems
        self.used = 0

    def __call__(self, source, target):
        copy = pltpu.make_async_copy(source, target, self.sems.at[self.used])
        self.used += 1
        copy.start()
        return copy


def wait_all(copies):
    for copy in copies:
        copy.wait()


def block_of(where, number):
    side, pair, core = number // 4, (number // 2) % 2, number % 2
    return ((where[0] ^ pair) * 2 + (where[1] ^ core)) * 2 + (where[2] ^ side)


def fetch_columns(fetch, where, source, target):
    found = []
    for number in range(8):
        start = pl.multiple_of(block_of(where, number) * LANES, LANES)
        place = pl.ds(number * LANES, LANES)
        found.append(fetch(source.at[:, pl.ds(start, LANES)], target.at[:, place]))
    return found


def fetch_rows(fetch, where, source, target):
    found = []
    for number in range(8):
        start = pl.multiple_of(block_of(where, number) * LANES, LANES)
        place = pl.ds(number * LANES, LANES)
        found.append(fetch(source.at[pl.ds(start, LANES), :], target.at[place, :]))
    return found


def store_absolute(where, out, first, value):
    rows = value.shape[0]
    for number in range(8):
        pair, side, half = number // 4, (number // 2) % 2, number % 2
        out[side ^ where[2], pair ^ where[0], half, first : first + rows, :] = value[
            :, number * LANES : (number + 1) * LANES
        ]


def store_relative(where, out, first, value, number):
    side, pair, core = number // 4, (number // 2) % 2, number % 2
    out[(where[1] ^ core) ^ where[2], pair, where[2] ^ side, first : first + value.shape[0], :] = value


def store_edge(out, value, flip_side):
    rows = value.shape[0]
    width = value.shape[1] // 4
    for side in range(2):
        for pair in range(2):
            start = (2 * side + pair) * width
            out[side ^ flip_side, 1 - pair] = value[:, start : start + width]


def read_edge(edge):
    return jnp.concatenate([edge[s, p] for s in range(2) for p in range(2)], axis=1)


VMEM_SPEC = pl.BlockSpec(memory_space=pltpu.VMEM)
ANY_SPEC = pl.BlockSpec(memory_space=pltpu.HBM)
SMEM_SPEC = pl.BlockSpec(memory_space=pltpu.SMEM)


def run(body, name, places, outs, scratch, operands, flops=0, room=44, out_specs=None):
    specs = [SMEM_SPEC] + [VMEM_SPEC if p == "v" else ANY_SPEC for p in places]
    moved = sum(o.size * o.dtype.itemsize for o in list(operands[1:]) + list(outs))
    return pl.pallas_call(
        body,
        name=name,
        in_specs=specs,
        out_specs=out_specs or [VMEM_SPEC] * len(outs),
        out_shape=outs,
        scratch_shapes=scratch,
        compiler_params=pltpu.CompilerParams(vmem_limit_bytes=room << 20),
        cost_estimate=pl.CostEstimate(
            flops=flops, bytes_accessed=min(moved, 16 << 20), transcendentals=0
        ),
    )(*operands)


def shape(dims, dtype):
    return jax.ShapeDtypeStruct(dims, dtype)


def fetch_ffn_adapters(fetch, where, which, column, up_ff, down_ff, p_in, q_in, p_out):
    found = []
    for number in range(4):
        side, core = number // 2, number % 2
        start = (2 * where[0] + (where[1] ^ core)) * (2 * column) + (where[2] ^ side) * column
        start = pl.multiple_of(start, column)
        place = pl.ds(number * column, column)
        found.append(fetch(up_ff.at[which, :, pl.ds(start, column)], q_in.at[:, place]))
        found.append(fetch(down_ff.at[which, pl.ds(start, column), :], p_out.at[place, :]))
    return found


def ffn_body(which, down_at, up_at, column, where, own, following, *refs):
    ins, outs, ups = refs[:4], refs[4:8], refs[8:12]
    down, down_ff, up, up_ff = ups
    part, send, pre_out, t_in_out, t_out_out = refs[12:17]
    rows, w_in, w_out, p_in, q_in, p_out, q_out, pre, active, sems = refs[17:]
    fetch = Fetches(sems)
    count = own.shape[0]
    small = [fetch(down.at[down_at], p_in), fetch(up.at[up_at], q_out)]
    small += fetch_ffn_adapters(fetch, where, which, column, up_ff, down_ff, p_in, q_in, p_out)
    first = [
        fetch(r.at[:, pl.ds(0, column)], w_in.at[:, pl.ds(n * column, column)])
        for n, r in enumerate(ins)
    ]
    second = [
        fetch(r.at[:, pl.ds(r.shape[1] - column, column)], w_out.at[:, pl.ds(n * column, column)])
        for n, r in enumerate(outs)
    ]
    mask = mask_row(where[3])
    rows[:count] = own[...]
    rows[count:] = following[...]
    wait_all(small)
    t_in = (nn(rows[...], p_in[...]) * mask).astype(BF)
    t_in_out[...] = t_in
    t_out = jnp.zeros(t_in.shape, F32)
    saved = []
    for n in range(4):
        span = slice(n * column, (n + 1) * column)
        first[n].wait()
        value = nn(rows[...], w_in[:, span]) + nn(t_in, q_in[:, span])
        pre[n] = value
        saved.append(fetch(pre.at[n], pre_out.at[n]))
        act = (value * jax.nn.sigmoid(value)).astype(BF)
        active[:, span] = act
        t_out = t_out + nn(act, p_out[span, :])
    t_out = (t_out * mask).astype(BF)
    t_out_out[...] = t_out
    wait_all(second)
    width = w_out.shape[0] // 2
    for n in range(2):
        span = slice(n * width, (n + 1) * width)
        total = nt(active[...], w_out[span, :]) + nn(t_out, q_out[:, span])
        part[:, span] = total[:count]
        send[:, span] = total[count:].astype(BF)
    wait_all(saved)


def ffn(which, down_at, up_at, where, own, following, w_in, w_out, adapters):
    count, width = own.shape
    column = adapters[3].shape[2] // 8
    hidden = 4 * column
    ranks = NADAPT * RANK

    def body(*refs):
        ffn_body(which, down_at, up_at, column, *refs)

    return run(
        body,
        "hidden_forward",
        "vv" + "a" * 12,
        [
            shape((count, width), F32),
            shape((count, width), BF),
            shape((4, 2 * count, column), F32),
            shape((2 * count, ranks), BF),
            shape((2 * count, ranks), BF),
        ],
        [
            pltpu.VMEM((2 * count, width), BF),
            pltpu.VMEM((width, hidden), BF),
            pltpu.VMEM((width, hidden), BF),
            pltpu.VMEM((width, ranks), BF),
            pltpu.VMEM((ranks, hidden), BF),
            pltpu.VMEM((hidden, ranks), BF),
            pltpu.VMEM((ranks, width), BF),
            pltpu.VMEM((4, 2 * count, column), F32),
            pltpu.VMEM((2 * count, hidden), BF),
            pltpu.SemaphoreType.DMA((22,)),
        ],
        [where, own, following, *w_in, *w_out, *adapters],
        flops=8 * count * width * hidden,
        out_specs=[VMEM_SPEC, VMEM_SPEC, ANY_SPEC, VMEM_SPEC, VMEM_SPEC],
    )


def ffn_back_body(which, down_at, up_at, column, where, own, following, u_own, u_next, t_in, t_out, *refs):
    pre_in = refs[0]
    ins, outs, ups = refs[1:5], refs[5:9], refs[9:13]
    down, down_ff, up, up_ff = ups
    part, send, grads = refs[13:16]
    full, rows, w_in, w_out, p_in, q_in, p_out, q_out, pre, active, slope, sems = refs[16:]
    fetch = Fetches(sems)
    count = own.shape[0]
    small = [fetch(down.at[down_at], p_in), fetch(up.at[up_at], q_out)]
    small += fetch_ffn_adapters(fetch, where, which, column, up_ff, down_ff, p_in, q_in, p_out)
    second = []
    kept = []
    for n, r in enumerate(outs):
        source = r.at[:, pl.ds(r.shape[1] - column, column)]
        second.append(fetch(source, w_out.at[:, pl.ds(n * column, column)]))
        kept.append(fetch(pre_in.at[n], pre.at[n]))
    first = [
        fetch(r.at[:, pl.ds(0, column)], w_in.at[:, pl.ds(n * column, column)])
        for n, r in enumerate(ins)
    ]
    mask = mask_row(where[3])
    pick = chosen_rows(where[3])
    full[:count] = own[...]
    full[count:] = following[...]
    rows[:count] = u_own[...]
    rows[count:] = u_next[...]
    wait_all(small)
    r_out = (nt(full[...], q_out[...]) * mask).astype(BF)
    c_out = compact(pick, r_out)
    c_t_in = compact(pick, t_in[...])
    r_in = jnp.zeros(r_out.shape, F32)
    for n in range(4):
        span = slice(n * column, (n + 1) * column)
        second[n].wait()
        kept[n].wait()
        grad = nn(full[...], w_out[:, span]) + nt(r_out, p_out[span, :])
        value = pre[n]
        sigma = jax.nn.sigmoid(value)
        act = (value * sigma).astype(BF)
        grad = (grad * swish_slope(value, sigma)).astype(BF)
        slope[:, span] = grad
        r_in = r_in + nt(grad, q_in[:, span])
        side, core = n // 2, n % 2
        near = (where[1] ^ core) ^ where[2]
        far = where[2] ^ side
        both = jnp.concatenate([nn(c_out, act), nn(c_t_in, grad)], axis=0)
        for piece in range(column // LANES):
            grads[near, 4 + far * (column // LANES) + piece] = both[
                :, piece * LANES : (piece + 1) * LANES
            ]
    r_in = (r_in * mask).astype(BF)
    wait_all(first)
    width = w_in.shape[0] // 2
    for n in range(2):
        span = slice(n * width, (n + 1) * width)
        total = nt(slope[...], w_in[span, :]) + nt(r_in, p_in[span, :])
        part[:, span] = total[:count]
        send[:, span] = total[count:].astype(BF)
    narrow = jnp.concatenate(
        [nn(compact(pick, r_in), rows[...]), nn(compact(pick, t_out[...]), full[...])], axis=0
    )
    for number in range(8):
        pair, side, half = number // 4, (number // 2) % 2, number % 2
        grads[side ^ where[2], 2 * (pair ^ where[0]) + half] = narrow[
            :, number * LANES : (number + 1) * LANES
        ]


def ffn_back(which, down_at, up_at, where, own, following, u_own, u_next, kept, w_in, w_out, adapters):
    pre, t_in, t_out = kept
    count, width = own.shape
    column = adapters[3].shape[2] // 8
    hidden = 4 * column
    ranks = NADAPT * RANK

    def body(*refs):
        ffn_back_body(which, down_at, up_at, column, *refs)

    return run(
        body,
        "hidden_backward",
        "vvvvvv" + "a" * 13,
        [
            shape((count, width), F32),
            shape((count, width), BF),
            shape((2, 4 + 2 * column // LANES, 2 * RANK, LANES), F32),
        ],
        [
            pltpu.VMEM((2 * count, width), BF),
            pltpu.VMEM((2 * count, width), BF),
            pltpu.VMEM((width, hidden), BF),
            pltpu.VMEM((width, hidden), BF),
            pltpu.VMEM((width, ranks), BF),
            pltpu.VMEM((ranks, hidden), BF),
            pltpu.VMEM((hidden, ranks), BF),
            pltpu.VMEM((ranks, width), BF),
            pltpu.VMEM((4, 2 * count, column), F32),
            pltpu.VMEM((2 * count, hidden), BF),
            pltpu.VMEM((2 * count, hidden), BF),
            pltpu.SemaphoreType.DMA((22,)),
        ],
        [where, own, following, u_own, u_next, t_in, t_out, pre, *w_in, *w_out, *adapters],
        flops=8 * count * width * hidden,
    )


def fetch_heads(fetch, where, pieces, up, wide):
    width = pieces[0].shape[0]
    three = 3 * LANES
    found = []
    for number, piece in enumerate(pieces):
        slot, core = number // 2, number % 2
        found.append(
            fetch(
                piece.at[:, pl.ds(0, three)],
                wide.at[slot, pl.ds(0, width), pl.ds(core * three, three)],
            )
        )
        start = pl.multiple_of(block_of(where, number) * LANES, LANES)
        for kind in range(3):
            found.append(
                fetch(
                    up.at[kind, :, pl.ds(start, LANES)],
                    wide.at[
                        slot,
                        pl.ds(width + kind * LANES, LANES),
                        pl.ds(core * three + kind * LANES, LANES),
                    ],
                )
            )
    return found


def clear_heads(wide, width):
    for kind in range(3):
        span = slice(width + kind * LANES, width + (kind + 1) * LANES)
        for core in range(2):
            for other in range(3):
                if other != kind:
                    at = (core * 3 + other) * LANES
                    for slot in range(4):
                        wide[slot, span, at : at + LANES] = jnp.zeros((LANES, LANES), BF)


def heads_body(where, resid, part, other, *refs):
    pieces = refs[:8]
    down, up = refs[8:10]
    first = refs[10]
    slots = refs[11:15]
    t_out = refs[15]
    wide, thin, sems = refs[16:]
    width = resid.shape[1]
    fetch = Fetches(sems)
    small = [
        fetch(down.at[1 + kind], thin.at[:, pl.ds(kind * LANES, LANES)]) for kind in range(3)
    ]
    large = fetch_heads(fetch, where, pieces, up, wide)
    clear_heads(wide, width)
    value = resid[...] + 0.5 * (part[...] + other[...].astype(F32))
    first[...] = value
    rows = normalize(value)[0].astype(BF)
    mask = jnp.concatenate([mask_row(where[3])] * 3, axis=1)
    wait_all(small)
    reduced = (nn(rows, thin[...]) * mask).astype(BF)
    t_out[...] = reduced
    both = jnp.concatenate([rows, reduced], axis=1)
    for slot in range(4):
        wait_all(large[slot * 8 : slot * 8 + 8])
        slots[slot][...] = nn(both, wide[slot]).astype(BF)


def heads_forward(where, resid, part, other, pieces, down, up):
    count, width = resid.shape
    three = 3 * LANES
    found = run(
        heads_body,
        "heads_forward",
        "vvv" + "a" * 10,
        [shape((count, width), F32)]
        + [shape((count, 2 * three), BF)] * 4
        + [shape((count, three), BF)],
        [
            pltpu.VMEM((4, width + three, 2 * three), BF),
            pltpu.VMEM((width, three), BF),
            pltpu.SemaphoreType.DMA((35,)),
        ],
        [where, resid, part, other, *pieces, down, up],
        flops=2 * count * width * 3 * width,
    )
    return (found[0], found[1:5], found[5])


def heads_back_body(where, grad, first, t_in, g0, g1, g2, g3, partial, *refs):
    pieces = refs[:8]
    down, up = refs[8:10]
    result, half, grads = refs[10:13]
    wide, thin, sems = refs[13:]
    width = grad.shape[1]
    three = 3 * LANES
    fetch = Fetches(sems)
    small = [
        fetch(down.at[1 + kind], thin.at[:, pl.ds(kind * LANES, LANES)]) for kind in range(3)
    ]
    large = fetch_heads(fetch, where, pieces, up, wide)
    clear_heads(wide, width)
    normed, scale = normalize(first[...])
    rows = normed.astype(BF)
    pick = chosen_rows(where[3])
    mask = jnp.concatenate([mask_row(where[3])] * 3, axis=1)
    ranks = [compact(pick, t_in[:, k * LANES : (k + 1) * LANES]) for k in range(3)]
    total = None
    for slot, g in enumerate((g0, g1, g2, g3)):
        wait_all(large[slot * 8 : slot * 8 + 8])
        term = nt(g[...], wide[slot])
        total = term if total is None else total + term
        for core in range(2):
            for kind in range(3):
                at = core * three + kind * LANES
                store_relative(
                    where, grads, (4 + kind) * RANK, nn(ranks[kind], g[:, at : at + LANES]),
                    2 * slot + core,
                )
    reduced = (total[:, width:] * mask).astype(BF)
    wait_all(small)
    total = total[:, :width] + nt(reduced, thin[...])
    value = grad[...] + normalize_back(total, normed, scale)
    result[...] = value
    half[...] = (0.5 * value).astype(BF)
    for kind in range(3):
        found = nn(compact(pick, reduced[:, kind * LANES : (kind + 1) * LANES]), rows)
        store_absolute(where, grads, kind * RANK, found)
    for side in range(2):
        for pair in range(2):
            for piece in range(2):
                grads[side, pair, piece, 3 * RANK : 4 * RANK, :] = partial[
                    side, pair, piece, :RANK, :
                ]
                grads[side, pair, piece, 7 * RANK :, :] = partial[side, pair, piece, RANK:, :]


def heads_back(where, grad, first, t_in, slots, partial, pieces, down, up):
    count, width = grad.shape
    three = 3 * LANES
    return run(
        heads_back_body,
        "heads_backward",
        "v" * 8 + "a" * 10,
        [
            shape((count, width), F32),
            shape((count, width), BF),
            shape((2, 2, 2, 8 * RANK, LANES), F32),
        ],
        [
            pltpu.VMEM((4, width + three, 2 * three), BF),
            pltpu.VMEM((width, three), BF),
            pltpu.SemaphoreType.DMA((35,)),
        ],
        [where, grad, first, t_in, *slots, partial, *pieces, down, up],
        flops=2 * count * width * 3 * width,
    )


def fetch_piece_columns(fetch, pieces, at, target):
    found = []
    for number, piece in enumerate(pieces):
        found.append(
            fetch(piece.at[:, pl.ds(at, LANES)], target.at[:, pl.ds(number * LANES, LANES)])
        )
    return found


def pair_body(where, first, m0, m1, m2, m3, *refs):
    heads, convs = refs[:8], refs[8:16]
    down, up = refs[16:18]
    second, value_out, gate_out, edge, t_mix_out, t_pair_out = refs[18:24]
    w_mix, w_value, w_gate, p_mix, q_mix, p_pair, q_value, q_gate, sems = refs[24:]
    fetch = Fetches(sems)
    mixing = fetch_rows(fetch, where, down.at[6], p_mix) + [fetch(up.at[5], q_mix)]
    mixing += fetch_piece_columns(fetch, heads, 3 * LANES, w_mix)
    pairs = [fetch(down.at[4], p_pair)]
    pairs += fetch_columns(fetch, where, up.at[3], q_value)
    pairs += fetch_columns(fetch, where, up.at[4], q_gate)
    pairs += fetch_piece_columns(fetch, convs, 0, w_value)
    gates = fetch_piece_columns(fetch, convs, LANES, w_gate)
    mask = mask_row(where[3])
    mixed = jnp.concatenate([m0[...], m1[...], m2[...], m3[...]], axis=1)
    wait_all(mixing)
    t_mix = (nn(mixed, p_mix[...]) * mask).astype(BF)
    t_mix_out[...] = t_mix
    value = first[...] + nt(mixed, w_mix[...]) + nn(t_mix, q_mix[...])
    second[...] = value
    rows = normalize(value)[0].astype(BF)
    wait_all(pairs)
    t_pair = (nn(rows, p_pair[...]) * mask).astype(BF)
    t_pair_out[...] = t_pair
    value = nn(rows, w_value[...]) + nn(t_pair, q_value[...])
    value_out[...] = value
    wait_all(gates)
    gate = nn(rows, w_gate[...]) + nn(t_pair, q_gate[...])
    gate_out[...] = gate
    last = value.shape[0] - edge.shape[2]
    store_edge(edge, value[last:] * jax.nn.sigmoid(gate[last:]), where[0])


def pair_forward(where, first, mixed, heads, convs, down, up):
    count, width = first.shape
    ranks = NADAPT * RANK
    square = pltpu.VMEM((width, width), BF)
    return run(
        pair_body,
        "pair_forward",
        "v" * 5 + "a" * 18,
        [
            shape((count, width), F32),
            shape((count, width), F32),
            shape((count, width), F32),
            shape((2, 2, 32, width // 4), F32),
            shape((count, ranks), BF),
            shape((count, ranks), BF),
        ],
        [
            square,
            square,
            square,
            pltpu.VMEM((width, ranks), BF),
            pltpu.VMEM((ranks, width), BF),
            pltpu.VMEM((width, ranks), BF),
            pltpu.VMEM((ranks, width), BF),
            pltpu.VMEM((ranks, width), BF),
            pltpu.SemaphoreType.DMA((50,)),
        ],
        [where, first, *mixed, *heads, *convs, down, up],
        flops=6 * count * width * width,
    )


def tap_sums(padded, taps, kernel, count, starts):
    found = []
    for number in range(padded.shape[0]):
        span = slice(number * LANES, (number + 1) * LANES)
        total = None
        for tap in range(taps):
            term = kernel[tap : tap + 1, span] * padded[number, starts[tap] : starts[tap] + count, :]
            total = term if total is None else total + term
        found.append(total)
    return jnp.concatenate(found, axis=1)


def conv_body(taps, where, second, value, gate, edge, kernel, *refs):
    convs = refs[:8]
    down, up = refs[8:10]
    conv_out, third, rows_out, t_out = refs[10:14]
    w_out, p_out, q_out, padded, sems = refs[14:]
    fetch = Fetches(sems)
    small = fetch_rows(fetch, where, down.at[7], p_out) + [fetch(up.at[6], q_out)]
    small += fetch_piece_columns(fetch, convs, 2 * LANES, w_out)
    count = second.shape[0]
    early = edge.shape[2]
    before = read_edge(edge)
    gated = value[...] * jax.nn.sigmoid(gate[...])
    for number in range(padded.shape[0]):
        span = slice(number * LANES, (number + 1) * LANES)
        padded[number, :early, :] = before[:, span]
        padded[number, early:, :] = gated[:, span]
    conv = tap_sums(padded, taps, kernel, count, [early - taps + 1 + k for k in range(taps)])
    conv_out[...] = conv
    normed = normalize(conv)[0]
    active = (normed * jax.nn.sigmoid(normed)).astype(BF)
    mask = mask_row(where[3])
    wait_all(small)
    reduced = (nn(active, p_out[...]) * mask).astype(BF)
    t_out[...] = reduced
    result = second[...] + nt(active, w_out[...]) + nn(reduced, q_out[...])
    third[...] = result
    rows_out[...] = normalize(result)[0].astype(BF)


def conv_forward(taps, where, second, value, gate, edge, kernel, convs, down, up):
    count, width = second.shape
    ranks = NADAPT * RANK

    def body(*refs):
        conv_body(taps, *refs)

    return run(
        body,
        "conv_forward",
        "v" * 5 + "a" * 10,
        [
            shape((count, width), F32),
            shape((count, width), F32),
            shape((count, width), BF),
            shape((count, ranks), BF),
        ],
        [
            pltpu.VMEM((width, width), BF),
            pltpu.VMEM((width, ranks), BF),
            pltpu.VMEM((ranks, width), BF),
            pltpu.VMEM((width // LANES, count + 32, LANES), F32),
            pltpu.SemaphoreType.DMA((17,)),
        ],
        [where, second, value, gate, edge, kernel, *convs, down, up],
        flops=2 * count * width * width,
    )


def conv_back_body(taps, where, grad, part, other, third, conv, t_in, *refs):
    convs = refs[:8]
    down, up = refs[8:10]
    result, grad_conv, edge, grads = refs[10:14]
    w_out, p_out, q_out, sems = refs[14:]
    fetch = Fetches(sems)
    small = fetch_rows(fetch, where, down.at[7], p_out) + [fetch(up.at[6], q_out)]
    small += fetch_piece_columns(fetch, convs, 2 * LANES, w_out)
    normed, scale = normalize(third[...])
    value = grad[...] + normalize_back(part[...] + other[...].astype(F32), normed, scale)
    result[...] = value
    full = value.astype(BF)
    mask = mask_row(where[3])
    pick = chosen_rows(where[3])
    wait_all(small)
    reduced = (nt(full, q_out[...]) * mask).astype(BF)
    active_grad = nn(full, w_out[...]) + nt(reduced, p_out[...])
    normed, scale = normalize(conv[...])
    sigma = jax.nn.sigmoid(normed)
    active = (normed * sigma).astype(BF)
    inner = normalize_back(active_grad * swish_slope(normed, sigma), normed, scale)
    grad_conv[...] = inner
    store_edge(edge, inner[: edge.shape[2]], 1 - where[0])
    store_absolute(where, grads, 0, nn(compact(pick, t_in[...]), full))
    found = nn(compact(pick, reduced), active)
    for number in range(8):
        store_relative(where, grads, RANK, found[:, number * LANES : (number + 1) * LANES], number)


def conv_back(taps, where, grad, part, other, third, conv, t_in, convs, down, up):
    count, width = grad.shape
    ranks = NADAPT * RANK

    def body(*refs):
        conv_back_body(taps, *refs)

    return run(
        body,
        "conv_backward",
        "v" * 6 + "a" * 10,
        [
            shape((count, width), F32),
            shape((count, width), F32),
            shape((2, 2, 32, width // 4), F32),
            shape((2, 2, 2, 2 * RANK, LANES), F32),
        ],
        [
            pltpu.VMEM((width, width), BF),
            pltpu.VMEM((width, ranks), BF),
            pltpu.VMEM((ranks, width), BF),
            pltpu.SemaphoreType.DMA((17,)),
        ],
        [where, grad, part, other, third, conv, t_in, *convs, down, up],
        flops=2 * count * width * width,
    )


def pair_back_body(
    taps, where, grad, grad_conv, edge, value, gate, kernel, second, t_pair, t_mix,
    m0, m1, m2, m3, partial, *refs
):
    heads, convs = refs[:8], refs[8:16]
    down, up = refs[16:18]
    result = refs[18]
    slots = refs[19:23]
    grads, mix_grads = refs[23:25]
    w_mix, w_value, w_gate, p_mix, q_mix, p_pair, q_value, q_gate, padded, sems = refs[25:]
    fetch = Fetches(sems)
    pairs = [fetch(down.at[4], p_pair)]
    pairs += fetch_columns(fetch, where, up.at[3], q_value)
    pairs += fetch_columns(fetch, where, up.at[4], q_gate)
    pairs += fetch_piece_columns(fetch, convs, 0, w_value)
    pairs += fetch_piece_columns(fetch, convs, LANES, w_gate)
    mixing = fetch_rows(fetch, where, down.at[6], p_mix) + [fetch(up.at[5], q_mix)]
    mixing += fetch_piece_columns(fetch, heads, 3 * LANES, w_mix)
    count = grad.shape[0]
    after = read_edge(edge)
    inner = grad_conv[...]
    for number in range(padded.shape[0]):
        span = slice(number * LANES, (number + 1) * LANES)
        padded[number, :count, :] = inner[:, span]
        padded[number, count:, :] = after[:, span]
    gated = tap_sums(padded, taps, kernel, count, [taps - 1 - k for k in range(taps)])
    sigma = jax.nn.sigmoid(gate[...])
    half = gated * sigma
    g_value = half.astype(BF)
    g_gate = (half * value[...] * (1.0 - sigma)).astype(BF)
    mask = mask_row(where[3])
    pick = chosen_rows(where[3])
    normed, scale = normalize(second[...])
    rows = normed.astype(BF)
    wait_all(pairs)
    reduced = ((nt(g_value, q_value[...]) + nt(g_gate, q_gate[...])) * mask).astype(BF)
    total = nt(g_value, w_value[...]) + nt(g_gate, w_gate[...]) + nt(reduced, p_pair[...])
    value_now = grad[...] + normalize_back(total, normed, scale)
    result[...] = value_now
    store_absolute(where, grads, 0, nn(compact(pick, reduced), rows))
    rank = compact(pick, t_pair[...])
    up_value = nn(rank, g_value)
    up_gate = nn(rank, g_gate)
    for number in range(8):
        span = slice(number * LANES, (number + 1) * LANES)
        store_relative(where, grads, 3 * RANK, up_value[:, span], number)
        store_relative(where, grads, 4 * RANK, up_gate[:, span], number)
    for side in range(2):
        for pair in range(2):
            for piece in range(2):
                grads[side, pair, piece, RANK : 3 * RANK, :] = partial[side, pair, piece]
    full = value_now.astype(BF)
    wait_all(mixing)
    reduced = (nt(full, q_mix[...]) * mask).astype(BF)
    mixed_grad = (nn(full, w_mix[...]) + nt(reduced, p_mix[...])).astype(BF)
    width = mixed_grad.shape[1] // 4
    for slot in range(4):
        slots[slot][...] = mixed_grad[:, slot * width : (slot + 1) * width]
    store_absolute(where, mix_grads, 0, nn(compact(pick, t_mix[...]), full))
    mixed = jnp.concatenate([m0[...], m1[...], m2[...], m3[...]], axis=1)
    found = nn(compact(pick, reduced), mixed)
    for number in range(8):
        span = slice(number * LANES, (number + 1) * LANES)
        store_relative(where, mix_grads, RANK, found[:, span], number)


def pair_back(
    taps, where, grad, grad_conv, edge, value, gate, kernel, second, t_pair, t_mix, mixed,
    partial, heads, convs, down, up
):
    count, width = grad.shape
    ranks = NADAPT * RANK
    square = pltpu.VMEM((width, width), BF)

    def body(*refs):
        pair_back_body(taps, *refs)

    found = run(
        body,
        "pair_backward",
        "v" * 14 + "a" * 18,
        [shape((count, width), F32)]
        + [shape((count, width // 4), BF)] * 4
        + [
            shape((2, 2, 2, 5 * RANK, LANES), F32),
            shape((2, 2, 2, 2 * RANK, LANES), F32),
        ],
        [
            square,
            square,
            square,
            pltpu.VMEM((width, ranks), BF),
            pltpu.VMEM((ranks, width), BF),
            pltpu.VMEM((width, ranks), BF),
            pltpu.VMEM((ranks, width), BF),
            pltpu.VMEM((ranks, width), BF),
            pltpu.VMEM((width // LANES, count + 32, LANES), F32),
            pltpu.SemaphoreType.DMA((50,)),
        ],
        [
            where, grad, grad_conv, edge, value, gate, kernel, second, t_pair, t_mix, *mixed,
            partial, *heads, *convs, down, up,
        ],
        flops=6 * count * width * width,
        room=52,
    )
    return (found[0], found[1:5], found[5], found[6])


def start_body(where, own, following, own_out, next_out):
    own_out[...] = normalize(own[...].astype(F32))[0].astype(BF)
    next_out[...] = normalize(following[...].astype(F32))[0].astype(BF)


def start_rows(where, own, following):
    count, width = own.shape
    return run(
        start_body, "start_rows", "vv", [shape((count, width), BF)] * 2, [], [where, own, following]
    )


def turn_body(where, third, part, other, cotangent, output, grad, half):
    fourth = third[...] + 0.5 * (part[...] + other[...].astype(F32))
    normed, scale = normalize(fourth)
    output[...] = normed.astype(BF)
    value = normalize_back(cotangent[...].astype(F32), normed, scale)
    grad[...] = value
    half[...] = (0.5 * value).astype(BF)


def turn(where, third, part, other, cotangent):
    count, width = third.shape
    return run(
        turn_body,
        "turn",
        "vvvv",
        [shape((count, width), BF), shape((count, width), F32), shape((count, width), BF)],
        [],
        [where, third, part, other, cotangent],
    )


def finish_body(where, grad, part, other, own, result):
    normed, scale = normalize(own[...].astype(F32))
    total = part[...] + other[...].astype(F32)
    result[...] = (grad[...] + normalize_back(total, normed, scale)).astype(BF)


def finish(where, grad, part, other, own):
    count, width = grad.shape
    return run(
        finish_body, "finish", "vvvv", [shape((count, width), BF)], [], [where, grad, part, other, own]
    )[0]


def expand_body(plan, spread, turned, found, *refs):
    kinds = sorted({kind for kind, _, _ in plan})
    outs = refs[-len(kinds) - len(plan) - 1 : -len(plan) - 1]
    held = refs[-len(plan) - 1 : -1]
    sems = refs[-1]
    copies = []
    for item, (kind, slot, starts) in enumerate(plan):
        column = len(starts) * LANES
        for pair in range(2):
            for side in range(2):
                parts = [
                    found[:, side, pair, :, row : row + RANK, :].reshape(-1, LANES)
                    for row in starts
                ]
                value = jnp.concatenate(parts, axis=1)
                start = (2 * pair + side) * column
                if kind % 2 == 0:
                    held[item][start : start + column, :] = tn(value, spread[...])
                else:
                    held[item][:, start : start + column] = nn(turned[...], value)
        copy = pltpu.make_async_copy(held[item], outs[kinds.index(kind)].at[slot], sems.at[item])
        copy.start()
        copies.append(copy)
    wait_all(copies)


def expand_near_body(plan, near_count, where, spread, turned, *refs):
    pieces = refs[: 2 * near_count]
    kinds = len({kind for _, kind, _, _ in plan})
    outs = refs[-kinds - len(plan) - 1 : -len(plan) - 1]
    held = refs[-len(plan) - 1 : -1]
    sems = refs[-1]
    copies = []
    for item, (wide, kind, slot, group) in enumerate(plan):
        rows = slice(group * RANK, (group + 1) * RANK)
        order = [0, 1] if not wide else list(range(2, pieces[0].shape[1]))
        column = len(order) * LANES
        for near in range(near_count):
            parts = [
                jnp.concatenate(
                    [pieces[2 * near + core][:, n, rows, :].reshape(-1, LANES) for core in range(2)],
                    axis=0,
                )
                for n in order
            ]
            value = jnp.concatenate(parts, axis=1)
            pair, side = where[0] ^ (near % 2), where[2] ^ (near // 2)
            place = pl.ds(pl.multiple_of((2 * pair + side) * column, column), column)
            if kind % 2 == 0:
                held[item][place, :] = tn(value, spread[...])
            else:
                held[item][:, place] = nn(turned[...], value)
        at = sorted({k for _, k, _, _ in plan}).index(kind)
        copy = pltpu.make_async_copy(held[item], outs[at].at[slot], sems.at[item])
        copy.start()
        copies.append(copy)
    wait_all(copies)


def expand_near(plan, where, spread, turned, pieces, outs):
    kinds = sorted({kind for _, kind, _, _ in plan})
    held = [outs[kind].shape[1:] for _, kind, _, _ in plan]
    passed = [outs[k] for k in kinds]
    start = 3 + len(pieces)

    def body(*refs):
        expand_near_body(plan, len(pieces) // 2, *refs)

    result = pl.pallas_call(
        body,
        name="expand_near",
        in_specs=[SMEM_SPEC] + [VMEM_SPEC] * (2 + len(pieces)) + [ANY_SPEC] * len(passed),
        out_specs=[ANY_SPEC] * len(kinds),
        out_shape=[shape(outs[k].shape, F32) for k in kinds],
        scratch_shapes=[pltpu.VMEM(h, F32) for h in held]
        + [pltpu.SemaphoreType.DMA((len(plan),))],
        input_output_aliases={start + n: n for n in range(len(kinds))},
        compiler_params=pltpu.CompilerParams(vmem_limit_bytes=44 << 20),
        cost_estimate=pl.CostEstimate(flops=0, bytes_accessed=8 << 20, transcendentals=0),
    )(where, spread, turned, *pieces, *passed)
    outs = list(outs)
    for n, k in enumerate(kinds):
        outs[k] = result[n]
    return outs


def rows_of(base, blocks, rows, group, first=0):
    return [base + n * rows + group * RANK for n in range(first, blocks)]


def expand(plan, spread, turned, found, outs):
    kinds = sorted({kind for kind, _, _ in plan})
    fresh = [isinstance(outs[k], jax.ShapeDtypeStruct) for k in kinds]
    held = [shape(outs[kind].shape[1:], F32) for kind, _, _ in plan]
    passed = [outs[k] for k, f in zip(kinds, fresh) if not f]
    aliases = {}
    for n, k in enumerate(kinds):
        if not fresh[n]:
            aliases[3 + len(aliases)] = n

    def body(*refs):
        expand_body(plan, *refs)

    result = pl.pallas_call(
        body,
        name="expand",
        in_specs=[VMEM_SPEC] * 3 + [ANY_SPEC] * len(passed),
        out_specs=[ANY_SPEC] * len(kinds),
        out_shape=[shape(outs[k].shape, F32) for k in kinds],
        scratch_shapes=[pltpu.VMEM(h.shape, F32) for h in held]
        + [pltpu.SemaphoreType.DMA((len(plan),))],
        input_output_aliases=aliases,
        compiler_params=pltpu.CompilerParams(vmem_limit_bytes=44 << 20),
        cost_estimate=pl.CostEstimate(flops=0, bytes_accessed=8 << 20, transcendentals=0),
    )(spread, turned, found, *passed)
    outs = list(outs)
    for n, k in enumerate(kinds):
        outs[k] = result[n]
    return outs


def join(own, other, bit, axis):
    return jnp.where(
        bit == 0,
        jnp.concatenate([own, other], axis=axis),
        jnp.concatenate([other, own], axis=axis),
    )


def part_of(value, index, count, axis):
    size = value.shape[axis] // count
    return lax.dynamic_slice_in_dim(value, index * size, size, axis)


class Place:
    def __init__(self):
        self.side = lax.axis_index("ctx")
        index = lax.axis_index("tp")
        self.pair = index // 2
        self.core = index % 2
        self.block = 2 * self.side + self.pair


def sequence_rows(value, place):
    own = lax.dynamic_index_in_dim(value, place.core, 0, keepdims=False)
    other = lax.dynamic_index_in_dim(value, 1 - place.core, 0, keepdims=False)
    return join(own, by_core(other), place.core, 1)


def own_rows(value, place):
    half = sequence_rows(value, place)
    mine = part_of(half, place.pair, 2, 0)
    theirs = part_of(half, 1 - place.pair, 2, 0)
    return join(mine, by_pair(theirs), place.pair, 1)


def all_rows(value, place):
    half = sequence_rows(value, place)
    full = join(half, by_pair(half), place.pair, 1)
    return part_of(full, place.pair, 2, 0), part_of(full, 1 - place.pair, 2, 0)


def feature_parts(value, place):
    mine = part_of(value, place.pair, 2, 1)
    theirs = part_of(value, 1 - place.pair, 2, 1)
    half = join(mine, by_pair(theirs), place.pair, 0)
    kept = part_of(half, place.core, 2, 1)[None]
    given = part_of(half, 1 - place.core, 2, 1)[None]
    return join(kept, by_core(given), place.core, 0)


def side_half(weight, place):
    return part_of(weight, place.side, 2, weight.ndim - 1)


def gathered(weight):
    return lax.all_gather(weight, "shard", axis=0, tiled=True)


def hidden_pieces(base):
    over = by_side(base)
    return [base, by_core(base), over, by_core(over)]


def whole_pieces(base):
    over = by_side(base)
    found = []
    for near in (base, over):
        far = by_pair(near)
        found += [near, by_core(near), far, by_core(far)]
    return found


def after(value, other):
    return lax.optimization_barrier((value, other))[0]


def line_order():
    count = lax.axis_size("shard")
    index = jnp.arange(count)
    return index if count > 8 else jnp.mod(lax.axis_index("shard") - index, count)


def around_shard(value):
    count = lax.axis_size("shard")
    if count > 8:
        return lax.all_gather(value, "shard", axis=0, tiled=False)
    found = [value]
    for shift in range(1, count):
        route = [(n, (n + shift) % count) for n in range(count)]
        found.append(lax.ppermute(value, "shard", route))
    return jnp.stack(found, axis=0)


def everywhere(value):
    flat = value.astype(BF).reshape(-1, LANES)
    found = lax.all_gather(flat, ("shard", "ctx", "tp"), axis=0, tiled=True)
    return found.reshape((-1, 2, 2, 2) + flat.shape)


def exchanged(slots):
    return [slots[0], by_pair(slots[1]), by_side(slots[2]), across(slots[3])]


def on_device(
    inputs,
    adapter_id,
    cotangent,
    ffn1_in,
    ffn1_out,
    query_w,
    key_w,
    value_w,
    out_w,
    conv_in_w,
    conv_kernel,
    conv_out_w,
    ffn2_in,
    ffn2_out,
    distance_table,
    adapt_down,
    adapt_down_ff,
    adapt_up,
    adapt_up_ff,
):
    place = Place()
    mine = lax.dynamic_index_in_dim(adapter_id, place.core, 0, keepdims=False)
    where = jnp.stack([place.pair, place.core, place.side, mine]).astype(jnp.int32)
    block = place.block.astype(jnp.int32)[None]
    adapters = (adapt_down, adapt_down_ff, adapt_up, adapt_up_ff)

    taps = conv_kernel.shape[0]
    core_kernel = jnp.concatenate([conv_kernel, by_core(conv_kernel)], axis=1)
    kernel = jnp.stack([core_kernel, by_pair(core_kernel)], axis=1).reshape(taps, 4, 2, -1)
    kernel = join(kernel[:, :, :1], kernel[:, :, 1:], place.side, 2)
    kernel = kernel.transpose(0, 2, 1, 3).reshape(taps, -1).astype(F32)

    ids = lax.all_gather(adapter_id, "shard", axis=0, tiled=True)
    eye = jnp.eye(RANK, dtype=BF)

    def spread_of(order):
        chosen = (order[:, None] == jnp.arange(NADAPT, dtype=jnp.int32)[None, :]).astype(BF)
        return (chosen[:, None, :, None] * eye[None, :, None, :]).reshape(-1, NADAPT * RANK)

    index = line_order()
    picked = index[:, None] == jnp.arange(index.shape[0])[None, :]
    near_ids = jnp.sum(jnp.where(picked[:, :, None], ids.reshape(1, -1, 2), 0), axis=1)
    near_ids = join(near_ids[:, :1], near_ids[:, 1:], place.core, 1).T.reshape(-1)
    spread, spread_near = spread_of(ids), spread_of(near_ids)
    turned, turned_near = spread.T, spread_near.T
    text = wide_table(distance_table)

    turning = own_rows(cotangent, place)
    settled = (kernel, text, spread, spread_near, turned, turned_near, turning)
    (kernel, text, spread, spread_near, turned, turned_near, turning) = lax.optimization_barrier(
        settled
    )

    base_in = gathered(side_half(ffn1_in, place))
    own, following = all_rows(inputs, place)
    rows_own, rows_next = start_rows(where, own, following)
    base_out = gathered(after(side_half(ffn1_out, place), (base_in, rows_own, rows_next)))
    in_side, in_core = by_side(base_in), by_core(base_in)
    local = jnp.concatenate(
        [side_half(w, place) for w in (query_w, key_w, value_w, out_w)], axis=1
    )
    base_heads = gathered(after(local, (base_out, in_side, in_core, turning, spread, kernel)))
    out_side, out_core = by_side(base_out), by_core(base_out)
    w1_in = [base_in, in_core, in_side, by_core(in_side)]
    pair_local = side_half(conv_in_w, place)
    local = jnp.concatenate(
        [pair_local[:, 0], pair_local[:, 1], side_half(conv_out_w, place)], axis=1
    )
    step = local.shape[1]
    local = jnp.concatenate([local, jnp.zeros_like(local[:, : step // 3])], axis=1)
    base_convs = gathered(after(local, (base_heads, out_side, out_core, w1_in[3])))
    w1_out = [base_out, out_core, out_side, by_core(out_side)]
    heads_side, heads_pair = by_side(base_heads), by_pair(base_heads)
    heads_core = by_core(base_heads)
    local = jnp.concatenate([side_half(w, place) for w in (ffn2_in, ffn2_out)], axis=1)
    part, send, pre, t_in, t_out = ffn(
        0, 0, 7, where, rows_own, rows_next, w1_in, w1_out, adapters
    )
    kept_one = (rows_own, rows_next, (pre, t_in, t_out))
    base_two = gathered(after(local, (base_convs, heads_side, heads_pair, heads_core, send)))
    heads_far = by_side(heads_pair)
    heads = [base_heads, heads_core, heads_pair, by_core(heads_pair)]
    heads += [heads_side, by_core(heads_side), heads_far, by_core(heads_far)]
    base_convs = base_convs[:, :step]
    convs_pair = by_pair(after(base_convs, heads_pair))
    convs_side = by_side(after(base_convs, heads_far))

    first, slots, t_heads = heads_forward(
        where, own.astype(F32), part, by_pair(send), heads, adapt_down, adapt_up
    )
    slots = exchanged(slots)
    convs_far = by_pair(after(convs_side, tuple(slots)))
    two_side = by_side(after(base_two, tuple(slots)))
    mixed, logs = attend(block, slots, text)
    convs = [base_convs, convs_pair, convs_side, convs_far]
    convs = [v for piece in convs for v in (piece, by_core(after(piece, mixed)))]
    mixed = exchanged([mixed[n] for n in range(4)])
    second, value, gate, edge, t_mix, t_pair = pair_forward(
        where, first, mixed, heads, convs, adapt_down, adapt_up
    )
    w2 = [base_two, by_core(after(base_two, mixed[0])), two_side, by_core(after(two_side, edge))]
    edge = lax.ppermute(edge, ("ctx", "tp"), NEXT)
    conv, third, rows_own, t_conv = conv_forward(
        taps, where, second, value, gate, edge, kernel, convs, adapt_down, adapt_up
    )
    rows_next = by_pair(rows_own)
    part, send, pre, t_in, t_out = ffn(1, 5, 8, where, rows_own, rows_next, w2, w2, adapters)
    kept_two = (rows_own, rows_next, (pre, t_in, t_out))

    output, grad, half = turn(where, third, part, by_pair(send), turning)
    part, send, sums_two = ffn_back(
        1, 5, 8, where, half, by_pair(half), *kept_two, w2, w2, adapters
    )
    grad, grad_conv, edge, partial = conv_back(
        taps, where, grad, part, by_pair(send), third, conv, t_conv, convs, adapt_down, adapt_up
    )
    came = after(by_side(after(sums_two[1], send)), grad_conv)
    sums_two = sums_two[0] + came
    edge = lax.ppermute(edge, ("ctx", "tp"), BEFORE)
    grad, grad_slots, conv_sums, partial = pair_back(
        taps, where, grad, grad_conv, edge, value, gate, kernel, second, t_pair, t_mix, mixed,
        partial, heads, convs, adapt_down, adapt_up,
    )
    came = after(by_pair(sums_two[2:4]), grad)
    sums_two = jnp.concatenate([sums_two[:2] + came, sums_two[4:]], axis=0)
    grad_slots = exchanged(grad_slots)
    conv_sums = conv_sums[0] + by_side(conv_sums[1])
    conv_sums = conv_sums[0] + by_pair(after(conv_sums[1], grad_slots[1]))
    payload = jnp.concatenate(
        [sums_two.astype(BF).reshape(-1, LANES), conv_sums.astype(BF).reshape(-1, LANES)], axis=0
    )
    found = everywhere(payload)
    back = attend_back(after(block, payload), slots, grad_slots, text, logs)
    output = feature_parts(output, place)
    back = exchanged([back[n] for n in range(4)])
    grad, half, head_sums = heads_back(
        after(where, output), grad, first, t_heads, back, partial, heads, adapt_down, adapt_up
    )
    other_half = by_pair(half)
    head_sums = head_sums[0] + by_side(head_sums[1])
    head_sums = head_sums[0] + by_pair(head_sums[1])
    found_heads = everywhere(after(head_sums, other_half))
    part, send, sums_one = ffn_back(
        0, 0, 7, where, half, other_half, *kept_one, w1_in, w1_out, adapters
    )
    sums_one = sums_one[0] + by_side(sums_one[1].astype(BF)).astype(F32)
    sums_one = jnp.concatenate([sums_one[:2] + by_pair(sums_one[2:4]), sums_one[4:]], axis=0)
    line = around_shard(sums_one.astype(BF))
    pieces = [line, by_pair(line), by_side(line)]
    pieces.append(by_pair(pieces[2]))
    pieces = [v for piece in pieces for v in (piece, by_core(piece))]
    input_grad = finish(where, grad, part, by_pair(send), own)
    input_grad = feature_parts(input_grad, place).astype(F32)

    outs = [shape(v.shape, F32) for v in (adapt_down, adapt_up, adapt_down_ff, adapt_up_ff)]
    ffn_blocks, ffn_rows = sums_two.shape[:2]
    conv_blocks, conv_rows = conv_sums.shape[:2]
    base = ffn_blocks * ffn_rows
    plan = [(kind, slot, rows_of(0, 2, ffn_rows, g)) for kind, slot, g in ((0, 5, 0), (1, 8, 1))]
    plan += [
        (kind, 1, rows_of(0, ffn_blocks, ffn_rows, g, 2)) for kind, g in ((2, 0), (3, 1))
    ]
    plan += [
        (kind, slot, rows_of(base, conv_blocks, conv_rows, g))
        for kind, slot, g in ((0, 4, 0), (1, 6, 1), (0, 7, 2), (1, 3, 3), (1, 4, 4))
    ]
    outs = expand(plan, spread, turned, after(found, send), outs)
    head_blocks, head_rows = head_sums.shape[:2]
    places = ((0, 1), (0, 2), (0, 3), (1, 5), (1, 0), (1, 1), (1, 2), (0, 6))
    plan = [
        (kind, slot, rows_of(0, head_blocks, head_rows, g))
        for g, (kind, slot) in enumerate(places)
    ]
    outs = expand(plan, spread, turned, found_heads, outs)
    outs = expand_near(
        [(False, 0, 0, 0), (False, 1, 7, 1), (True, 2, 0, 0), (True, 3, 0, 1)],
        where, spread_near, turned_near, pieces, outs,
    )
    return (output, input_grad, outs[0], outs[2], outs[1], outs[3])


def solution(mesh):
    placed = (
        P("shard", "ctx", "tp"),
        P("shard"),
        P("shard", "ctx", "tp"),
        P("shard", "tp"),
        P("shard", "tp"),
        P("shard", "tp"),
        P("shard", "tp"),
        P("shard", "tp"),
        P("shard", "tp"),
        P("shard", None, "tp"),
        P(None, "tp"),
        P("shard", "tp"),
        P("shard", "tp"),
        P("shard", "tp"),
        P(),
        P(),
        P(),
        P(),
        P(),
    )
    return jax.shard_map(
        on_device,
        mesh=mesh,
        in_specs=placed,
        out_specs=(P("shard", "ctx", "tp"), P("shard", "ctx", "tp"), P(), P(), P(), P()),
        check_vma=False,
    )
```

```python
import jax
import jax.numpy as jnp
from jax import lax
from jax.experimental import pallas as pl
from jax.experimental.pallas import tpu as pltpu
from jax.sharding import PartitionSpec as P

LEFT = 64
RIGHT = 8
NADAPT = 8
RANK = 16
HEAD = 64
LANES = 128
eps = 1e-05
BF = jnp.bfloat16
F32 = jnp.float32

CORE = [(0, 1), (1, 0), (2, 3), (3, 2)]
PAIR = [(0, 2), (2, 0), (1, 3), (3, 1)]
SIDE = [(0, 1), (1, 0)]
ACROSS = [(s * 4 + t, (1 - s) * 4 + (t ^ 2)) for s in range(2) for t in range(4)]


def block_at(block, core):
    return (block // 2) * 4 + (block % 2) * 2 + core


NEXT = [(block_at(n, k), block_at(n + 1, k)) for n in range(3) for k in range(2)]
BEFORE = [(block_at(n + 1, k), block_at(n, k)) for n in range(3) for k in range(2)]


def by_core(value):
    return lax.ppermute(value, "tp", CORE)


def by_pair(value):
    return lax.ppermute(value, "tp", PAIR)


def by_side(value):
    return lax.ppermute(value, "ctx", SIDE)


def across(value):
    return lax.ppermute(value, ("ctx", "tp"), ACROSS)


def wide_table(table):
    place = jnp.arange(4*LANES, dtype=jnp.int32)
    index = jnp.where(place < 3*LANES, jnp.clip(place - LEFT, 0, LEFT+RIGHT), 0)
    pick = (index[:, None] == jnp.arange(table.shape[0], dtype=jnp.int32)[None, :]).astype(BF)
    rows = jnp.dot(pick, table, preferred_element_type=F32).astype(BF)
    return jnp.concatenate([rows, rows], axis=1)

def load_blocks(b_ref, sources, target, sems, parts):
    copies=[]
    for j, source in enumerate(sources):
        rows = source.shape[0]; cols = source.shape[1]//parts
        for part in range(parts):
            copies.append(pltpu.make_async_copy(
                source.at[:, part*cols:(part+1)*cols],
                target.at[part, pl.ds(pl.multiple_of((b_ref[0] ^ j)*rows, rows), rows), :],
                sems.at[j*parts+part]))
    for c in copies: c.start()
    for c in copies: c.wait()

def window(r0, length):
    lo=max(r0-LANES,0); hi=min(r0+2*LANES,length)
    return lo,hi

def biased(s, near, p, rows, length):
    parts=[]
    for sub in range(rows//LANES):
        r0=p*rows+sub*LANES
        e=near[sub*LANES:(sub+1)*LANES]
        band=pltpu.roll(e, 0, 1, stride=1, stride_axis=0)
        lo,hi=window(r0,length)
        pieces=[]
        if lo>0: pieces.append(jnp.broadcast_to(e[:,0:1],(LANES,lo)))
        pieces.append(band[:, lo-r0+LANES:hi-r0+LANES])
        if hi<length: pieces.append(jnp.broadcast_to(e[:,2*LANES-1:2*LANES],(LANES,length-hi)))
        parts.append(jnp.concatenate(pieces,axis=1))
    return s+jnp.concatenate(parts,axis=0)


def fwd_kernel(b_ref, s0,s1,s2,s3, text_ref, o_ref, lse_ref, qkv, sems):
    dc=pl.program_id(0); k=pl.program_id(1)
    @pl.when((dc==0)&(k==0))
    def _(): load_blocks(b_ref,(s0,s1,s2,s3),qkv,sems,2)
    rows=o_ref.shape[1]; length=qkv.shape[1]
    own=(lax.broadcasted_iota(jnp.int32,(rows,LANES),1)//64)==k
    key=qkv[dc,:,LANES:2*LANES]; val=qkv[dc,:,2*LANES:]
    for p in range(length//rows):
        q=qkv[dc,p*rows:(p+1)*rows,0:LANES].astype(F32)*0.125
        q=jnp.where(own,q,0.0).astype(BF)
        s=biased(nt(q,key),nt(q,text_ref[...]),p,rows,length)
        top=jnp.max(s,axis=-1,keepdims=True)
        e=jnp.exp(s-top)
        tot=jnp.sum(e,axis=-1,keepdims=True)
        o=jnp.dot(e.astype(BF),val,preferred_element_type=F32)/tot
        o=o.astype(BF)
        slot=p^b_ref[0]
        @pl.when(k==0)
        def _(): o_ref[slot]=o
        @pl.when(k==1)
        def _(): o_ref[slot]=jnp.where(own,o,o_ref[slot])
        lse_ref[0,p*rows:(p+1)*rows,:]=top+jnp.log(tot)

def attend(b, slots, text):
    rows=slots[0].shape[0]; n=len(slots); length=rows*n
    anys=[pl.BlockSpec(memory_space=pl.ANY)]*n
    return pl.pallas_call(
        fwd_kernel,
        grid_spec=pltpu.PrefetchScalarGridSpec(
            num_scalar_prefetch=1, grid=(2,2),
            in_specs=anys+[pl.BlockSpec(text.shape,lambda d,k,b:(0,0))],
            out_specs=(pl.BlockSpec((n,rows,LANES),lambda d,k,b:(0,0,d)),
                       pl.BlockSpec((1,length,1),lambda d,k,b:(2*d+k,0,0))),
            scratch_shapes=[pltpu.VMEM((2,length,3*LANES),BF),pltpu.SemaphoreType.DMA((2*n,))]),
        out_shape=(jax.ShapeDtypeStruct((n,rows,2*LANES),BF),jax.ShapeDtypeStruct((4,length,1),F32)),
        compiler_params=pltpu.CompilerParams(vmem_limit_bytes=48<<20),
        name="attend",
        cost_estimate=pl.CostEstimate(flops=4*4*length*length*64,bytes_accessed=length*8*LANES*2,transcendentals=4*length*length),
    )(b,*slots,text)

def bwd_kernel(b_ref, s0,s1,s2,s3, g0,g1,g2,g3, text_ref, lse_ref, out_ref, qkv, gout, dq_acc, dk_acc, dv_acc, sems, gsems):
    dc=pl.program_id(0); k=pl.program_id(1)
    @pl.when((dc==0)&(k==0))
    def _():
        load_blocks(b_ref,(s0,s1,s2,s3),qkv,sems,2)
        load_blocks(b_ref,(g0,g1,g2,g3),gout,gsems,2)
    rows=out_ref.shape[1]; length=qkv.shape[1]
    own=(lax.broadcasted_iota(jnp.int32,(rows,LANES),1)//64)==k
    key=qkv[dc,:,LANES:2*LANES]; val=qkv[dc,:,2*LANES:]
    text=text_ref[...]
    turn=((lax.broadcasted_iota(jnp.int32,(LANES,LANES),0)+lax.broadcasted_iota(jnp.int32,(LANES,LANES),1))==LANES-1).astype(BF)
    @pl.when(k==0)
    def _():
        dk_acc[...]=jnp.zeros_like(dk_acc); dv_acc[...]=jnp.zeros_like(dv_acc)
    for p in range(length//rows):
        span=slice(p*rows,(p+1)*rows)
        q=qkv[dc,span,0:LANES].astype(F32)*0.125
        q=jnp.where(own,q,0.0).astype(BF)
        g=jnp.where(own,gout[dc,span,:].astype(F32),0.0).astype(BF)
        s=biased(nt(q,key),nt(q,text),p,rows,length)
        pr=jnp.exp(s-lse_ref[0,span,:])
        dp=nt(g,val)
        w=pr*dp
        ds=(w-pr*jnp.sum(w,axis=-1,keepdims=True)).astype(BF)
        dv_acc[...]+=tn(g,pr.astype(BF))
        dk_acc[...]+=tn(q,ds)
        dq=jnp.dot(ds,key,preferred_element_type=F32)
        extra=[]
        t_lo=text[0:1,:].astype(F32); t_hi=text[2*LANES-1:2*LANES,:].astype(F32)
        for sub in range(rows//LANES):
            r0=p*rows+sub*LANES
            lo,hi=window(r0,length)
            d=ds[sub*LANES:(sub+1)*LANES].astype(F32)
            pieces=[]
            if lo-r0+LANES>0: pieces.append(jnp.zeros((LANES,lo-r0+LANES),F32))
            pieces.append(d[:,lo:hi])
            pieces.append(jnp.zeros((LANES,4*LANES-(hi-r0+LANES)),F32))
            w=jnp.concatenate(pieces,axis=1)
            w=jnp.dot(turn,w.astype(BF),preferred_element_type=F32)
            w=pltpu.roll(w,3*LANES+1,1,stride=1,stride_axis=0)
            w=jnp.dot(turn,w.astype(BF),preferred_element_type=F32)
            x=jnp.dot(w.astype(BF),text,preferred_element_type=F32)
            if lo>0: x+=jnp.sum(d[:,:lo],axis=-1,keepdims=True)*t_lo
            if hi<length: x+=jnp.sum(d[:,hi:],axis=-1,keepdims=True)*t_hi
            extra.append(x)
        dq=(dq+jnp.concatenate(extra,axis=0))*0.125
        dq_acc[span,:]=jnp.where(own,dq,dq_acc[span,:])
    @pl.when(k==1)
    def _():
        for p in range(length//rows):
            slot=p^b_ref[0]; span=slice(p*rows,(p+1)*rows)
            out_ref[slot,:,0:LANES]=dq_acc[span,:].astype(BF)
            out_ref[slot,:,LANES:2*LANES]=dk_acc[:,span].T.astype(BF)
            out_ref[slot,:,2*LANES:]=dv_acc[:,span].T.astype(BF)

def attend_back(b, slots, grads, text, lse):
    rows=slots[0].shape[0]; n=len(slots); length=rows*n
    anys=[pl.BlockSpec(memory_space=pl.ANY)]*(2*n)
    return pl.pallas_call(
        bwd_kernel,
        grid_spec=pltpu.PrefetchScalarGridSpec(
            num_scalar_prefetch=1, grid=(2,2),
            in_specs=anys+[pl.BlockSpec(text.shape,lambda d,k,b:(0,0)),pl.BlockSpec((1,length,1),lambda d,k,b:(2*d+k,0,0))],
            out_specs=pl.BlockSpec((n,rows,3*LANES),lambda d,k,b:(0,0,d)),
            scratch_shapes=[pltpu.VMEM((2,length,3*LANES),BF),pltpu.VMEM((2,length,LANES),BF),
              pltpu.VMEM((length,LANES),F32),pltpu.VMEM((LANES,length),F32),pltpu.VMEM((LANES,length),F32),
              pltpu.SemaphoreType.DMA((2*n,)),pltpu.SemaphoreType.DMA((2*n,))]),
        out_shape=jax.ShapeDtypeStruct((n,rows,6*LANES),BF),
        compiler_params=pltpu.CompilerParams(vmem_limit_bytes=30<<20),
        name="attend_back",
        cost_estimate=pl.CostEstimate(flops=10*4*length*length*64,bytes_accessed=length*14*LANES*2,transcendentals=4*length*length),
    )(b,*slots,*grads,text,lse)


def nn(first, second):
    return jnp.dot(first, second, preferred_element_type=F32)


def nt(first, second):
    return lax.dot_general(first, second, (((1,), (1,)), ((), ())), preferred_element_type=F32)


def tn(first, second):
    return lax.dot_general(first, second, (((0,), (0,)), ((), ())), preferred_element_type=F32)


def normalize(value):
    mean = jnp.mean(value, axis=-1, keepdims=True)
    square = jnp.mean(value * value, axis=-1, keepdims=True)
    scale = lax.rsqrt(square - mean * mean + eps)
    return ((value - mean) * scale, scale)


def normalize_back(grad, normed, scale):
    mean = jnp.mean(grad, axis=-1, keepdims=True)
    cross = jnp.mean(grad * normed, axis=-1, keepdims=True)
    return scale * (grad - mean - normed * cross)


def swish_slope(value, sigma):
    return sigma + value * sigma * (1.0 - sigma)


def mask_row(adapter):
    lanes = lax.broadcasted_iota(jnp.int32, (1, NADAPT * RANK), 1)
    return (lanes // RANK == adapter).astype(F32)


def chosen_rows(adapter):
    shape = (RANK, NADAPT * RANK)
    lanes = lax.broadcasted_iota(jnp.int32, shape, 1)
    rows = lax.broadcasted_iota(jnp.int32, shape, 0)
    return (lanes == rows + adapter * RANK).astype(BF)


def compact(pick, value):
    return nt(pick, value).astype(BF)


class Fetches:
    def __init__(self, sems):
        self.sems = sems
        self.used = 0

    def __call__(self, source, target):
        copy = pltpu.make_async_copy(source, target, self.sems.at[self.used])
        self.used += 1
        copy.start()
        return copy


def wait_all(copies):
    for copy in copies:
        copy.wait()


def block_of(where, number):
    side, pair, core = number // 4, (number // 2) % 2, number % 2
    return ((where[0] ^ pair) * 2 + (where[1] ^ core)) * 2 + (where[2] ^ side)


def fetch_columns(fetch, where, source, target):
    found = []
    for number in range(8):
        start = pl.multiple_of(block_of(where, number) * LANES, LANES)
        place = pl.ds(number * LANES, LANES)
        found.append(fetch(source.at[:, pl.ds(start, LANES)], target.at[:, place]))
    return found


def fetch_rows(fetch, where, source, target):
    found = []
    for number in range(8):
        start = pl.multiple_of(block_of(where, number) * LANES, LANES)
        place = pl.ds(number * LANES, LANES)
        found.append(fetch(source.at[pl.ds(start, LANES), :], target.at[place, :]))
    return found


def store_absolute(where, out, first, value):
    rows = value.shape[0]
    for number in range(8):
        pair, side, half = number // 4, (number // 2) % 2, number % 2
        out[side ^ where[2], pair ^ where[0], half, first : first + rows, :] = value[
            :, number * LANES : (number + 1) * LANES
        ]


def store_relative(where, out, first, value, number):
    side, pair, core = number // 4, (number // 2) % 2, number % 2
    out[(where[1] ^ core) ^ where[2], pair, where[2] ^ side, first : first + value.shape[0], :] = value


def store_edge(out, value, flip_side):
    rows = value.shape[0]
    width = value.shape[1] // 4
    for side in range(2):
        for pair in range(2):
            start = (2 * side + pair) * width
            out[side ^ flip_side, 1 - pair] = value[:, start : start + width]


def read_edge(edge):
    return jnp.concatenate([edge[s, p] for s in range(2) for p in range(2)], axis=1)


VMEM_SPEC = pl.BlockSpec(memory_space=pltpu.VMEM)
ANY_SPEC = pl.BlockSpec(memory_space=pltpu.HBM)
SMEM_SPEC = pl.BlockSpec(memory_space=pltpu.SMEM)


def run(body, name, places, outs, scratch, operands, flops=0, room=44, out_specs=None):
    specs = [SMEM_SPEC] + [VMEM_SPEC if p == "v" else ANY_SPEC for p in places]
    moved = sum(o.size * o.dtype.itemsize for o in list(operands[1:]) + list(outs))
    return pl.pallas_call(
        body,
        name=name,
        in_specs=specs,
        out_specs=out_specs or [VMEM_SPEC] * len(outs),
        out_shape=outs,
        scratch_shapes=scratch,
        compiler_params=pltpu.CompilerParams(vmem_limit_bytes=room << 20),
        cost_estimate=pl.CostEstimate(
            flops=flops, bytes_accessed=min(moved, 16 << 20), transcendentals=0
        ),
    )(*operands)


def shape(dims, dtype):
    return jax.ShapeDtypeStruct(dims, dtype)


def fetch_ffn_adapters(fetch, where, which, column, up_ff, down_ff, p_in, q_in, p_out):
    found = []
    for number in range(4):
        side, core = number // 2, number % 2
        start = (2 * where[0] + (where[1] ^ core)) * (2 * column) + (where[2] ^ side) * column
        start = pl.multiple_of(start, column)
        place = pl.ds(number * column, column)
        found.append(fetch(up_ff.at[which, :, pl.ds(start, column)], q_in.at[:, place]))
        found.append(fetch(down_ff.at[which, pl.ds(start, column), :], p_out.at[place, :]))
    return found


def ffn_body(which, down_at, up_at, column, where, own, following, *refs):
    ins, outs, ups = refs[:4], refs[4:8], refs[8:12]
    down, down_ff, up, up_ff = ups
    part, send, pre_out, t_in_out, t_out_out = refs[12:17]
    rows, w_in, w_out, p_in, q_in, p_out, q_out, pre, active, sems = refs[17:]
    fetch = Fetches(sems)
    count = own.shape[0]
    small = [fetch(down.at[down_at], p_in), fetch(up.at[up_at], q_out)]
    small += fetch_ffn_adapters(fetch, where, which, column, up_ff, down_ff, p_in, q_in, p_out)
    first = [
        fetch(r.at[:, pl.ds(0, column)], w_in.at[:, pl.ds(n * column, column)])
        for n, r in enumerate(ins)
    ]
    second = [
        fetch(r.at[:, pl.ds(r.shape[1] - column, column)], w_out.at[:, pl.ds(n * column, column)])
        for n, r in enumerate(outs)
    ]
    mask = mask_row(where[3])
    rows[:count] = own[...]
    rows[count:] = following[...]
    wait_all(small)
    t_in = (nn(rows[...], p_in[...]) * mask).astype(BF)
    t_in_out[...] = t_in
    t_out = jnp.zeros(t_in.shape, F32)
    saved = []
    for n in range(4):
        span = slice(n * column, (n + 1) * column)
        first[n].wait()
        value = nn(rows[...], w_in[:, span]) + nn(t_in, q_in[:, span])
        pre[n] = value
        saved.append(fetch(pre.at[n], pre_out.at[n]))
        act = (value * jax.nn.sigmoid(value)).astype(BF)
        active[:, span] = act
        t_out = t_out + nn(act, p_out[span, :])
    t_out = (t_out * mask).astype(BF)
    t_out_out[...] = t_out
    wait_all(second)
    width = w_out.shape[0] // 2
    for n in range(2):
        span = slice(n * width, (n + 1) * width)
        total = nt(active[...], w_out[span, :]) + nn(t_out, q_out[:, span])
        part[:, span] = total[:count]
        send[:, span] = total[count:].astype(BF)
    wait_all(saved)


def ffn(which, down_at, up_at, where, own, following, w_in, w_out, adapters):
    count, width = own.shape
    column = adapters[3].shape[2] // 8
    hidden = 4 * column
    ranks = NADAPT * RANK

    def body(*refs):
        ffn_body(which, down_at, up_at, column, *refs)

    return run(
        body,
        "hidden_forward",
        "vv" + "a" * 12,
        [
            shape((count, width), F32),
            shape((count, width), BF),
            shape((4, 2 * count, column), F32),
            shape((2 * count, ranks), BF),
            shape((2 * count, ranks), BF),
        ],
        [
            pltpu.VMEM((2 * count, width), BF),
            pltpu.VMEM((width, hidden), BF),
            pltpu.VMEM((width, hidden), BF),
            pltpu.VMEM((width, ranks), BF),
            pltpu.VMEM((ranks, hidden), BF),
            pltpu.VMEM((hidden, ranks), BF),
            pltpu.VMEM((ranks, width), BF),
            pltpu.VMEM((4, 2 * count, column), F32),
            pltpu.VMEM((2 * count, hidden), BF),
            pltpu.SemaphoreType.DMA((22,)),
        ],
        [where, own, following, *w_in, *w_out, *adapters],
        flops=8 * count * width * hidden,
        out_specs=[VMEM_SPEC, VMEM_SPEC, ANY_SPEC, VMEM_SPEC, VMEM_SPEC],
    )


def ffn_back_body(which, down_at, up_at, column, where, own, following, u_own, u_next, t_in, t_out, *refs):
    pre_in = refs[0]
    ins, outs, ups = refs[1:5], refs[5:9], refs[9:13]
    down, down_ff, up, up_ff = ups
    part, send, grads = refs[13:16]
    full, rows, w_in, w_out, p_in, q_in, p_out, q_out, pre, active, slope, sems = refs[16:]
    fetch = Fetches(sems)
    count = own.shape[0]
    small = [fetch(down.at[down_at], p_in), fetch(up.at[up_at], q_out)]
    small += fetch_ffn_adapters(fetch, where, which, column, up_ff, down_ff, p_in, q_in, p_out)
    second = []
    kept = []
    for n, r in enumerate(outs):
        source = r.at[:, pl.ds(r.shape[1] - column, column)]
        second.append(fetch(source, w_out.at[:, pl.ds(n * column, column)]))
        kept.append(fetch(pre_in.at[n], pre.at[n]))
    first = [
        fetch(r.at[:, pl.ds(0, column)], w_in.at[:, pl.ds(n * column, column)])
        for n, r in enumerate(ins)
    ]
    mask = mask_row(where[3])
    pick = chosen_rows(where[3])
    full[:count] = own[...]
    full[count:] = following[...]
    rows[:count] = u_own[...]
    rows[count:] = u_next[...]
    wait_all(small)
    r_out = (nt(full[...], q_out[...]) * mask).astype(BF)
    c_out = compact(pick, r_out)
    c_t_in = compact(pick, t_in[...])
    r_in = jnp.zeros(r_out.shape, F32)
    for n in range(4):
        span = slice(n * column, (n + 1) * column)
        second[n].wait()
        kept[n].wait()
        grad = nn(full[...], w_out[:, span]) + nt(r_out, p_out[span, :])
        value = pre[n]
        sigma = jax.nn.sigmoid(value)
        act = (value * sigma).astype(BF)
        grad = (grad * swish_slope(value, sigma)).astype(BF)
        slope[:, span] = grad
        r_in = r_in + nt(grad, q_in[:, span])
        side, core = n // 2, n % 2
        near = (where[1] ^ core) ^ where[2]
        far = where[2] ^ side
        both = jnp.concatenate([nn(c_out, act), nn(c_t_in, grad)], axis=0)
        for piece in range(column // LANES):
            grads[near, 4 + far * (column // LANES) + piece] = both[
                :, piece * LANES : (piece + 1) * LANES
            ]
    r_in = (r_in * mask).astype(BF)
    wait_all(first)
    width = w_in.shape[0] // 2
    for n in range(2):
        span = slice(n * width, (n + 1) * width)
        total = nt(slope[...], w_in[span, :]) + nt(r_in, p_in[span, :])
        part[:, span] = total[:count]
        send[:, span] = total[count:].astype(BF)
    narrow = jnp.concatenate(
        [nn(compact(pick, r_in), rows[...]), nn(compact(pick, t_out[...]), full[...])], axis=0
    )
    for number in range(8):
        pair, side, half = number // 4, (number // 2) % 2, number % 2
        grads[side ^ where[2], 2 * (pair ^ where[0]) + half] = narrow[
            :, number * LANES : (number + 1) * LANES
        ]


def ffn_back(which, down_at, up_at, where, own, following, u_own, u_next, kept, w_in, w_out, adapters):
    pre, t_in, t_out = kept
    count, width = own.shape
    column = adapters[3].shape[2] // 8
    hidden = 4 * column
    ranks = NADAPT * RANK

    def body(*refs):
        ffn_back_body(which, down_at, up_at, column, *refs)

    return run(
        body,
        "hidden_backward",
        "vvvvvv" + "a" * 13,
        [
            shape((count, width), F32),
            shape((count, width), BF),
            shape((2, 4 + 2 * column // LANES, 2 * RANK, LANES), F32),
        ],
        [
            pltpu.VMEM((2 * count, width), BF),
            pltpu.VMEM((2 * count, width), BF),
            pltpu.VMEM((width, hidden), BF),
            pltpu.VMEM((width, hidden), BF),
            pltpu.VMEM((width, ranks), BF),
            pltpu.VMEM((ranks, hidden), BF),
            pltpu.VMEM((hidden, ranks), BF),
            pltpu.VMEM((ranks, width), BF),
            pltpu.VMEM((4, 2 * count, column), F32),
            pltpu.VMEM((2 * count, hidden), BF),
            pltpu.VMEM((2 * count, hidden), BF),
            pltpu.SemaphoreType.DMA((22,)),
        ],
        [where, own, following, u_own, u_next, t_in, t_out, pre, *w_in, *w_out, *adapters],
        flops=8 * count * width * hidden,
    )


def fetch_heads(fetch, where, pieces, up, wide):
    width = pieces[0].shape[0]
    three = 3 * LANES
    found = []
    for number, piece in enumerate(pieces):
        slot, core = number // 2, number % 2
        found.append(
            fetch(
                piece.at[:, pl.ds(0, three)],
                wide.at[slot, pl.ds(0, width), pl.ds(core * three, three)],
            )
        )
        start = pl.multiple_of(block_of(where, number) * LANES, LANES)
        for kind in range(3):
            found.append(
                fetch(
                    up.at[kind, :, pl.ds(start, LANES)],
                    wide.at[
                        slot,
                        pl.ds(width + kind * LANES, LANES),
                        pl.ds(core * three + kind * LANES, LANES),
                    ],
                )
            )
    return found


def clear_heads(wide, width):
    for kind in range(3):
        span = slice(width + kind * LANES, width + (kind + 1) * LANES)
        for core in range(2):
            for other in range(3):
                if other != kind:
                    at = (core * 3 + other) * LANES
                    for slot in range(4):
                        wide[slot, span, at : at + LANES] = jnp.zeros((LANES, LANES), BF)


def heads_body(where, resid, part, other, *refs):
    pieces = refs[:8]
    down, up = refs[8:10]
    first = refs[10]
    slots = refs[11:15]
    t_out = refs[15]
    wide, thin, sems = refs[16:]
    width = resid.shape[1]
    fetch = Fetches(sems)
    small = [
        fetch(down.at[1 + kind], thin.at[:, pl.ds(kind * LANES, LANES)]) for kind in range(3)
    ]
    large = fetch_heads(fetch, where, pieces, up, wide)
    clear_heads(wide, width)
    value = resid[...] + 0.5 * (part[...] + other[...].astype(F32))
    first[...] = value
    rows = normalize(value)[0].astype(BF)
    mask = jnp.concatenate([mask_row(where[3])] * 3, axis=1)
    wait_all(small)
    reduced = (nn(rows, thin[...]) * mask).astype(BF)
    t_out[...] = reduced
    both = jnp.concatenate([rows, reduced], axis=1)
    for slot in range(4):
        wait_all(large[slot * 8 : slot * 8 + 8])
        slots[slot][...] = nn(both, wide[slot]).astype(BF)


def heads_forward(where, resid, part, other, pieces, down, up):
    count, width = resid.shape
    three = 3 * LANES
    found = run(
        heads_body,
        "heads_forward",
        "vvv" + "a" * 10,
        [shape((count, width), F32)]
        + [shape((count, 2 * three), BF)] * 4
        + [shape((count, three), BF)],
        [
            pltpu.VMEM((4, width + three, 2 * three), BF),
            pltpu.VMEM((width, three), BF),
            pltpu.SemaphoreType.DMA((35,)),
        ],
        [where, resid, part, other, *pieces, down, up],
        flops=2 * count * width * 3 * width,
    )
    return (found[0], found[1:5], found[5])


def heads_back_body(where, grad, first, t_in, g0, g1, g2, g3, partial, convs, *refs):
    pieces = refs[:8]
    down, up = refs[8:10]
    result, half, grads = refs[10:13]
    wide, thin, sems = refs[13:]
    width = grad.shape[1]
    three = 3 * LANES
    fetch = Fetches(sems)
    small = [
        fetch(down.at[1 + kind], thin.at[:, pl.ds(kind * LANES, LANES)]) for kind in range(3)
    ]
    large = fetch_heads(fetch, where, pieces, up, wide)
    clear_heads(wide, width)
    normed, scale = normalize(first[...])
    rows = normed.astype(BF)
    pick = chosen_rows(where[3])
    mask = jnp.concatenate([mask_row(where[3])] * 3, axis=1)
    ranks = [compact(pick, t_in[:, k * LANES : (k + 1) * LANES]) for k in range(3)]
    total = None
    for slot, g in enumerate((g0, g1, g2, g3)):
        wait_all(large[slot * 8 : slot * 8 + 8])
        term = nt(g[...], wide[slot])
        total = term if total is None else total + term
        for core in range(2):
            for kind in range(3):
                at = core * three + kind * LANES
                store_relative(
                    where, grads, (4 + kind) * RANK, nn(ranks[kind], g[:, at : at + LANES]),
                    2 * slot + core,
                )
    reduced = (total[:, width:] * mask).astype(BF)
    wait_all(small)
    total = total[:, :width] + nt(reduced, thin[...])
    value = grad[...] + normalize_back(total, normed, scale)
    result[...] = value
    half[...] = (0.5 * value).astype(BF)
    for kind in range(3):
        found = nn(compact(pick, reduced[:, kind * LANES : (kind + 1) * LANES]), rows)
        store_absolute(where, grads, kind * RANK, found)
    for side in range(2):
        for pair in range(2):
            for piece in range(2):
                grads[side, pair, piece, 3 * RANK : 4 * RANK, :] = partial[
                    side, pair, piece, :RANK, :
                ]
                grads[side, pair, piece, 7 * RANK : 8 * RANK, :] = partial[
                    side, pair, piece, RANK:, :
                ]
                grads[side, pair, piece, 8 * RANK :, :] = convs[side, pair, piece]


def heads_back(where, grad, first, t_in, slots, partial, convs, pieces, down, up):
    count, width = grad.shape
    three = 3 * LANES
    return run(
        heads_back_body,
        "heads_backward",
        "v" * 9 + "a" * 10,
        [
            shape((count, width), F32),
            shape((count, width), BF),
            shape((2, 2, 2, 13 * RANK, LANES), F32),
        ],
        [
            pltpu.VMEM((4, width + three, 2 * three), BF),
            pltpu.VMEM((width, three), BF),
            pltpu.SemaphoreType.DMA((35,)),
        ],
        [where, grad, first, t_in, *slots, partial, convs, *pieces, down, up],
        flops=2 * count * width * 3 * width,
    )


def fetch_piece_columns(fetch, pieces, at, target):
    found = []
    for number, piece in enumerate(pieces):
        found.append(
            fetch(piece.at[:, pl.ds(at, LANES)], target.at[:, pl.ds(number * LANES, LANES)])
        )
    return found


def pair_body(where, first, m0, m1, m2, m3, *refs):
    heads, convs = refs[:8], refs[8:16]
    down, up = refs[16:18]
    second, value_out, gate_out, edge, t_mix_out, t_pair_out = refs[18:24]
    w_mix, w_value, w_gate, p_mix, q_mix, p_pair, q_value, q_gate, sems = refs[24:]
    fetch = Fetches(sems)
    mixing = fetch_rows(fetch, where, down.at[6], p_mix) + [fetch(up.at[5], q_mix)]
    mixing += fetch_piece_columns(fetch, heads, 3 * LANES, w_mix)
    pairs = [fetch(down.at[4], p_pair)]
    pairs += fetch_columns(fetch, where, up.at[3], q_value)
    pairs += fetch_columns(fetch, where, up.at[4], q_gate)
    pairs += fetch_piece_columns(fetch, convs, 0, w_value)
    gates = fetch_piece_columns(fetch, convs, LANES, w_gate)
    mask = mask_row(where[3])
    mixed = jnp.concatenate([m0[...], m1[...], m2[...], m3[...]], axis=1)
    wait_all(mixing)
    t_mix = (nn(mixed, p_mix[...]) * mask).astype(BF)
    t_mix_out[...] = t_mix
    value = first[...] + nt(mixed, w_mix[...]) + nn(t_mix, q_mix[...])
    second[...] = value
    rows = normalize(value)[0].astype(BF)
    wait_all(pairs)
    t_pair = (nn(rows, p_pair[...]) * mask).astype(BF)
    t_pair_out[...] = t_pair
    value = nn(rows, w_value[...]) + nn(t_pair, q_value[...])
    value_out[...] = value
    wait_all(gates)
    gate = nn(rows, w_gate[...]) + nn(t_pair, q_gate[...])
    gate_out[...] = gate
    last = value.shape[0] - edge.shape[2]
    store_edge(edge, value[last:] * jax.nn.sigmoid(gate[last:]), where[0])


def pair_forward(where, first, mixed, heads, convs, down, up):
    count, width = first.shape
    ranks = NADAPT * RANK
    square = pltpu.VMEM((width, width), BF)
    return run(
        pair_body,
        "pair_forward",
        "v" * 5 + "a" * 18,
        [
            shape((count, width), F32),
            shape((count, width), F32),
            shape((count, width), F32),
            shape((2, 2, 32, width // 4), F32),
            shape((count, ranks), BF),
            shape((count, ranks), BF),
        ],
        [
            square,
            square,
            square,
            pltpu.VMEM((width, ranks), BF),
            pltpu.VMEM((ranks, width), BF),
            pltpu.VMEM((width, ranks), BF),
            pltpu.VMEM((ranks, width), BF),
            pltpu.VMEM((ranks, width), BF),
            pltpu.SemaphoreType.DMA((50,)),
        ],
        [where, first, *mixed, *heads, *convs, down, up],
        flops=6 * count * width * width,
    )


def tap_sums(padded, taps, kernel, count, starts):
    found = []
    for number in range(padded.shape[0]):
        span = slice(number * LANES, (number + 1) * LANES)
        total = None
        for tap in range(taps):
            term = kernel[tap : tap + 1, span] * padded[number, starts[tap] : starts[tap] + count, :]
            total = term if total is None else total + term
        found.append(total)
    return jnp.concatenate(found, axis=1)


def conv_body(taps, where, second, value, gate, edge, kernel, *refs):
    convs = refs[:8]
    down, up = refs[8:10]
    conv_out, third, rows_out, t_out = refs[10:14]
    w_out, p_out, q_out, padded, sems = refs[14:]
    fetch = Fetches(sems)
    small = fetch_rows(fetch, where, down.at[7], p_out) + [fetch(up.at[6], q_out)]
    small += fetch_piece_columns(fetch, convs, 2 * LANES, w_out)
    count = second.shape[0]
    early = edge.shape[2]
    before = read_edge(edge)
    gated = value[...] * jax.nn.sigmoid(gate[...])
    for number in range(padded.shape[0]):
        span = slice(number * LANES, (number + 1) * LANES)
        padded[number, :early, :] = before[:, span]
        padded[number, early:, :] = gated[:, span]
    conv = tap_sums(padded, taps, kernel, count, [early - taps + 1 + k for k in range(taps)])
    conv_out[...] = conv
    normed = normalize(conv)[0]
    active = (normed * jax.nn.sigmoid(normed)).astype(BF)
    mask = mask_row(where[3])
    wait_all(small)
    reduced = (nn(active, p_out[...]) * mask).astype(BF)
    t_out[...] = reduced
    result = second[...] + nt(active, w_out[...]) + nn(reduced, q_out[...])
    third[...] = result
    rows_out[...] = normalize(result)[0].astype(BF)


def conv_forward(taps, where, second, value, gate, edge, kernel, convs, down, up):
    count, width = second.shape
    ranks = NADAPT * RANK

    def body(*refs):
        conv_body(taps, *refs)

    return run(
        body,
        "conv_forward",
        "v" * 5 + "a" * 10,
        [
            shape((count, width), F32),
            shape((count, width), F32),
            shape((count, width), BF),
            shape((count, ranks), BF),
        ],
        [
            pltpu.VMEM((width, width), BF),
            pltpu.VMEM((width, ranks), BF),
            pltpu.VMEM((ranks, width), BF),
            pltpu.VMEM((width // LANES, count + 32, LANES), F32),
            pltpu.SemaphoreType.DMA((17,)),
        ],
        [where, second, value, gate, edge, kernel, *convs, down, up],
        flops=2 * count * width * width,
    )


def conv_back_body(taps, where, grad, part, other, third, conv, t_in, *refs):
    convs = refs[:8]
    down, up = refs[8:10]
    result, grad_conv, edge, grads = refs[10:14]
    w_out, p_out, q_out, sems = refs[14:]
    fetch = Fetches(sems)
    small = fetch_rows(fetch, where, down.at[7], p_out) + [fetch(up.at[6], q_out)]
    small += fetch_piece_columns(fetch, convs, 2 * LANES, w_out)
    normed, scale = normalize(third[...])
    value = grad[...] + normalize_back(part[...] + other[...].astype(F32), normed, scale)
    result[...] = value
    full = value.astype(BF)
    mask = mask_row(where[3])
    pick = chosen_rows(where[3])
    wait_all(small)
    reduced = (nt(full, q_out[...]) * mask).astype(BF)
    active_grad = nn(full, w_out[...]) + nt(reduced, p_out[...])
    normed, scale = normalize(conv[...])
    sigma = jax.nn.sigmoid(normed)
    active = (normed * sigma).astype(BF)
    inner = normalize_back(active_grad * swish_slope(normed, sigma), normed, scale)
    grad_conv[...] = inner
    store_edge(edge, inner[: edge.shape[2]], 1 - where[0])
    store_absolute(where, grads, 0, nn(compact(pick, t_in[...]), full))
    found = nn(compact(pick, reduced), active)
    for number in range(8):
        store_relative(where, grads, RANK, found[:, number * LANES : (number + 1) * LANES], number)


def conv_back(taps, where, grad, part, other, third, conv, t_in, convs, down, up):
    count, width = grad.shape
    ranks = NADAPT * RANK

    def body(*refs):
        conv_back_body(taps, *refs)

    return run(
        body,
        "conv_backward",
        "v" * 6 + "a" * 10,
        [
            shape((count, width), F32),
            shape((count, width), F32),
            shape((2, 2, 32, width // 4), F32),
            shape((2, 2, 2, 2 * RANK, LANES), F32),
        ],
        [
            pltpu.VMEM((width, width), BF),
            pltpu.VMEM((width, ranks), BF),
            pltpu.VMEM((ranks, width), BF),
            pltpu.SemaphoreType.DMA((17,)),
        ],
        [where, grad, part, other, third, conv, t_in, *convs, down, up],
        flops=2 * count * width * width,
    )


def pair_back_body(
    taps, where, grad, grad_conv, edge, value, gate, kernel, second, t_pair, t_mix,
    m0, m1, m2, m3, partial, *refs
):
    heads, convs = refs[:8], refs[8:16]
    down, up = refs[16:18]
    result = refs[18]
    slots = refs[19:23]
    grads, mix_grads = refs[23:25]
    w_mix, w_value, w_gate, p_mix, q_mix, p_pair, q_value, q_gate, padded, sems = refs[25:]
    fetch = Fetches(sems)
    pairs = [fetch(down.at[4], p_pair)]
    pairs += fetch_columns(fetch, where, up.at[3], q_value)
    pairs += fetch_columns(fetch, where, up.at[4], q_gate)
    pairs += fetch_piece_columns(fetch, convs, 0, w_value)
    pairs += fetch_piece_columns(fetch, convs, LANES, w_gate)
    mixing = fetch_rows(fetch, where, down.at[6], p_mix) + [fetch(up.at[5], q_mix)]
    mixing += fetch_piece_columns(fetch, heads, 3 * LANES, w_mix)
    count = grad.shape[0]
    after = read_edge(edge)
    inner = grad_conv[...]
    for number in range(padded.shape[0]):
        span = slice(number * LANES, (number + 1) * LANES)
        padded[number, :count, :] = inner[:, span]
        padded[number, count:, :] = after[:, span]
    gated = tap_sums(padded, taps, kernel, count, [taps - 1 - k for k in range(taps)])
    sigma = jax.nn.sigmoid(gate[...])
    half = gated * sigma
    g_value = half.astype(BF)
    g_gate = (half * value[...] * (1.0 - sigma)).astype(BF)
    mask = mask_row(where[3])
    pick = chosen_rows(where[3])
    normed, scale = normalize(second[...])
    rows = normed.astype(BF)
    wait_all(pairs)
    reduced = ((nt(g_value, q_value[...]) + nt(g_gate, q_gate[...])) * mask).astype(BF)
    total = nt(g_value, w_value[...]) + nt(g_gate, w_gate[...]) + nt(reduced, p_pair[...])
    value_now = grad[...] + normalize_back(total, normed, scale)
    result[...] = value_now
    store_absolute(where, grads, 0, nn(compact(pick, reduced), rows))
    rank = compact(pick, t_pair[...])
    up_value = nn(rank, g_value)
    up_gate = nn(rank, g_gate)
    for number in range(8):
        span = slice(number * LANES, (number + 1) * LANES)
        store_relative(where, grads, 3 * RANK, up_value[:, span], number)
        store_relative(where, grads, 4 * RANK, up_gate[:, span], number)
    for side in range(2):
        for pair in range(2):
            for piece in range(2):
                grads[side, pair, piece, RANK : 3 * RANK, :] = partial[side, pair, piece]
    full = value_now.astype(BF)
    wait_all(mixing)
    reduced = (nt(full, q_mix[...]) * mask).astype(BF)
    mixed_grad = (nn(full, w_mix[...]) + nt(reduced, p_mix[...])).astype(BF)
    width = mixed_grad.shape[1] // 4
    for slot in range(4):
        slots[slot][...] = mixed_grad[:, slot * width : (slot + 1) * width]
    store_absolute(where, mix_grads, 0, nn(compact(pick, t_mix[...]), full))
    mixed = jnp.concatenate([m0[...], m1[...], m2[...], m3[...]], axis=1)
    found = nn(compact(pick, reduced), mixed)
    for number in range(8):
        span = slice(number * LANES, (number + 1) * LANES)
        store_relative(where, mix_grads, RANK, found[:, span], number)


def pair_back(
    taps, where, grad, grad_conv, edge, value, gate, kernel, second, t_pair, t_mix, mixed,
    partial, heads, convs, down, up
):
    count, width = grad.shape
    ranks = NADAPT * RANK
    square = pltpu.VMEM((width, width), BF)

    def body(*refs):
        pair_back_body(taps, *refs)

    found = run(
        body,
        "pair_backward",
        "v" * 14 + "a" * 18,
        [shape((count, width), F32)]
        + [shape((count, width // 4), BF)] * 4
        + [
            shape((2, 2, 2, 5 * RANK, LANES), F32),
            shape((2, 2, 2, 2 * RANK, LANES), F32),
        ],
        [
            square,
            square,
            square,
            pltpu.VMEM((width, ranks), BF),
            pltpu.VMEM((ranks, width), BF),
            pltpu.VMEM((width, ranks), BF),
            pltpu.VMEM((ranks, width), BF),
            pltpu.VMEM((ranks, width), BF),
            pltpu.VMEM((width // LANES, count + 32, LANES), F32),
            pltpu.SemaphoreType.DMA((50,)),
        ],
        [
            where, grad, grad_conv, edge, value, gate, kernel, second, t_pair, t_mix, *mixed,
            partial, *heads, *convs, down, up,
        ],
        flops=6 * count * width * width,
        room=52,
    )
    return (found[0], found[1:5], found[5], found[6])


def start_body(where, own, following, own_out, next_out):
    own_out[...] = normalize(own[...].astype(F32))[0].astype(BF)
    next_out[...] = normalize(following[...].astype(F32))[0].astype(BF)


def start_rows(where, own, following):
    count, width = own.shape
    return run(
        start_body, "start_rows", "vv", [shape((count, width), BF)] * 2, [], [where, own, following]
    )


def turn_body(where, third, part, other, cotangent, output, grad, half):
    fourth = third[...] + 0.5 * (part[...] + other[...].astype(F32))
    normed, scale = normalize(fourth)
    output[...] = normed.astype(BF)
    value = normalize_back(cotangent[...].astype(F32), normed, scale)
    grad[...] = value
    half[...] = (0.5 * value).astype(BF)


def turn(where, third, part, other, cotangent):
    count, width = third.shape
    return run(
        turn_body,
        "turn",
        "vvvv",
        [shape((count, width), BF), shape((count, width), F32), shape((count, width), BF)],
        [],
        [where, third, part, other, cotangent],
    )


def finish_body(where, grad, part, other, own, result):
    normed, scale = normalize(own[...].astype(F32))
    total = part[...] + other[...].astype(F32)
    result[...] = (grad[...] + normalize_back(total, normed, scale)).astype(BF)


def finish(where, grad, part, other, own):
    count, width = grad.shape
    return run(
        finish_body, "finish", "vvvv", [shape((count, width), BF)], [], [where, grad, part, other, own]
    )[0]


def expand_body(plan, spread, turned, found, *refs):
    kinds = sorted({kind for kind, _, _ in plan})
    outs = refs[-len(kinds) - len(plan) - 1 : -len(plan) - 1]
    held = refs[-len(plan) - 1 : -1]
    sems = refs[-1]
    copies = []
    for item, (kind, slot, starts) in enumerate(plan):
        column = len(starts) * LANES
        for pair in range(2):
            for side in range(2):
                parts = [
                    found[:, side, pair, :, row : row + RANK, :].reshape(-1, LANES)
                    for row in starts
                ]
                value = jnp.concatenate(parts, axis=1)
                start = (2 * pair + side) * column
                if kind % 2 == 0:
                    held[item][start : start + column, :] = tn(value, spread[...])
                else:
                    held[item][:, start : start + column] = nn(turned[...], value)
        copy = pltpu.make_async_copy(held[item], outs[kinds.index(kind)].at[slot], sems.at[item])
        copy.start()
        copies.append(copy)
    wait_all(copies)


def expand_near_body(plan, near_count, where, spread, turned, *refs):
    pieces = refs[: 2 * near_count]
    kinds = len({kind for _, kind, _, _ in plan})
    outs = refs[-kinds - len(plan) - 1 : -len(plan) - 1]
    held = refs[-len(plan) - 1 : -1]
    sems = refs[-1]
    copies = []
    for item, (wide, kind, slot, group) in enumerate(plan):
        rows = slice(group * RANK, (group + 1) * RANK)
        order = [0, 1] if not wide else list(range(2, pieces[0].shape[1]))
        column = len(order) * LANES
        for near in range(near_count):
            parts = [
                jnp.concatenate(
                    [pieces[2 * near + core][:, n, rows, :].reshape(-1, LANES) for core in range(2)],
                    axis=0,
                )
                for n in order
            ]
            value = jnp.concatenate(parts, axis=1)
            pair, side = where[0] ^ (near % 2), where[2] ^ (near // 2)
            place = pl.ds(pl.multiple_of((2 * pair + side) * column, column), column)
            if kind % 2 == 0:
                held[item][place, :] = tn(value, spread[...])
            else:
                held[item][:, place] = nn(turned[...], value)
        at = sorted({k for _, k, _, _ in plan}).index(kind)
        copy = pltpu.make_async_copy(held[item], outs[at].at[slot], sems.at[item])
        copy.start()
        copies.append(copy)
    wait_all(copies)


def expand_near(plan, where, spread, turned, pieces, outs):
    kinds = sorted({kind for _, kind, _, _ in plan})
    held = [outs[kind].shape[1:] for _, kind, _, _ in plan]
    passed = [outs[k] for k in kinds]
    start = 3 + len(pieces)

    def body(*refs):
        expand_near_body(plan, len(pieces) // 2, *refs)

    result = pl.pallas_call(
        body,
        name="expand_near",
        in_specs=[SMEM_SPEC] + [VMEM_SPEC] * (2 + len(pieces)) + [ANY_SPEC] * len(passed),
        out_specs=[ANY_SPEC] * len(kinds),
        out_shape=[shape(outs[k].shape, F32) for k in kinds],
        scratch_shapes=[pltpu.VMEM(h, F32) for h in held]
        + [pltpu.SemaphoreType.DMA((len(plan),))],
        input_output_aliases={start + n: n for n in range(len(kinds))},
        compiler_params=pltpu.CompilerParams(vmem_limit_bytes=44 << 20),
        cost_estimate=pl.CostEstimate(flops=0, bytes_accessed=8 << 20, transcendentals=0),
    )(where, spread, turned, *pieces, *passed)
    outs = list(outs)
    for n, k in enumerate(kinds):
        outs[k] = result[n]
    return outs


def rows_of(base, blocks, rows, group, first=0):
    return [base + n * rows + group * RANK for n in range(first, blocks)]


def expand(plan, spread, turned, found, outs):
    kinds = sorted({kind for kind, _, _ in plan})
    fresh = [isinstance(outs[k], jax.ShapeDtypeStruct) for k in kinds]
    held = [shape(outs[kind].shape[1:], F32) for kind, _, _ in plan]
    passed = [outs[k] for k, f in zip(kinds, fresh) if not f]
    aliases = {}
    for n, k in enumerate(kinds):
        if not fresh[n]:
            aliases[3 + len(aliases)] = n

    def body(*refs):
        expand_body(plan, *refs)

    result = pl.pallas_call(
        body,
        name="expand",
        in_specs=[VMEM_SPEC] * 3 + [ANY_SPEC] * len(passed),
        out_specs=[ANY_SPEC] * len(kinds),
        out_shape=[shape(outs[k].shape, F32) for k in kinds],
        scratch_shapes=[pltpu.VMEM(h.shape, F32) for h in held]
        + [pltpu.SemaphoreType.DMA((len(plan),))],
        input_output_aliases=aliases,
        compiler_params=pltpu.CompilerParams(vmem_limit_bytes=44 << 20),
        cost_estimate=pl.CostEstimate(flops=0, bytes_accessed=8 << 20, transcendentals=0),
    )(spread, turned, found, *passed)
    outs = list(outs)
    for n, k in enumerate(kinds):
        outs[k] = result[n]
    return outs


def join(own, other, bit, axis):
    return jnp.where(
        bit == 0,
        jnp.concatenate([own, other], axis=axis),
        jnp.concatenate([other, own], axis=axis),
    )


def part_of(value, index, count, axis):
    size = value.shape[axis] // count
    return lax.dynamic_slice_in_dim(value, index * size, size, axis)


class Place:
    def __init__(self):
        self.side = lax.axis_index("ctx")
        index = lax.axis_index("tp")
        self.pair = index // 2
        self.core = index % 2
        self.block = 2 * self.side + self.pair


def sequence_rows(value, place):
    own = lax.dynamic_index_in_dim(value, place.core, 0, keepdims=False)
    other = lax.dynamic_index_in_dim(value, 1 - place.core, 0, keepdims=False)
    return join(own, by_core(other), place.core, 1)


def own_rows(value, place):
    half = sequence_rows(value, place)
    mine = part_of(half, place.pair, 2, 0)
    theirs = part_of(half, 1 - place.pair, 2, 0)
    return join(mine, by_pair(theirs), place.pair, 1)


def all_rows(value, place):
    half = sequence_rows(value, place)
    full = join(half, by_pair(half), place.pair, 1)
    return part_of(full, place.pair, 2, 0), part_of(full, 1 - place.pair, 2, 0)


def feature_parts(value, place):
    mine = part_of(value, place.pair, 2, 1)
    theirs = part_of(value, 1 - place.pair, 2, 1)
    half = join(mine, by_pair(theirs), place.pair, 0)
    kept = part_of(half, place.core, 2, 1)[None]
    given = part_of(half, 1 - place.core, 2, 1)[None]
    return join(kept, by_core(given), place.core, 0)


def side_half(weight, place):
    return part_of(weight, place.side, 2, weight.ndim - 1)


def gathered(weight):
    return lax.all_gather(weight, "shard", axis=0, tiled=True)


def hidden_pieces(base):
    over = by_side(base)
    return [base, by_core(base), over, by_core(over)]


def whole_pieces(base):
    over = by_side(base)
    found = []
    for near in (base, over):
        far = by_pair(near)
        found += [near, by_core(near), far, by_core(far)]
    return found


def after(value, other):
    return lax.optimization_barrier((value, other))[0]


def line_order():
    count = lax.axis_size("shard")
    index = jnp.arange(count)
    return index if count > 8 else jnp.mod(lax.axis_index("shard") - index, count)


def around_shard(value):
    count = lax.axis_size("shard")
    if count > 8:
        return lax.all_gather(value, "shard", axis=0, tiled=False)
    found = [value]
    for shift in range(1, count):
        route = [(n, (n + shift) % count) for n in range(count)]
        found.append(lax.ppermute(value, "shard", route))
    return jnp.stack(found, axis=0)


def everywhere(value):
    flat = value.astype(BF).reshape(-1, LANES)
    found = lax.all_gather(flat, ("shard", "ctx", "tp"), axis=0, tiled=True)
    return found.reshape((-1, 2, 2, 2) + flat.shape)


def exchanged(slots):
    return [slots[0], by_pair(slots[1]), by_side(slots[2]), across(slots[3])]


def on_device(
    inputs,
    adapter_id,
    cotangent,
    ffn1_in,
    ffn1_out,
    query_w,
    key_w,
    value_w,
    out_w,
    conv_in_w,
    conv_kernel,
    conv_out_w,
    ffn2_in,
    ffn2_out,
    distance_table,
    adapt_down,
    adapt_down_ff,
    adapt_up,
    adapt_up_ff,
):
    place = Place()
    mine = lax.dynamic_index_in_dim(adapter_id, place.core, 0, keepdims=False)
    where = jnp.stack([place.pair, place.core, place.side, mine]).astype(jnp.int32)
    block = place.block.astype(jnp.int32)[None]
    adapters = (adapt_down, adapt_down_ff, adapt_up, adapt_up_ff)

    taps = conv_kernel.shape[0]
    core_kernel = jnp.concatenate([conv_kernel, by_core(conv_kernel)], axis=1)
    kernel = jnp.stack([core_kernel, by_pair(core_kernel)], axis=1).reshape(taps, 4, 2, -1)
    kernel = join(kernel[:, :, :1], kernel[:, :, 1:], place.side, 2)
    kernel = kernel.transpose(0, 2, 1, 3).reshape(taps, -1).astype(F32)

    ids = lax.all_gather(adapter_id, "shard", axis=0, tiled=True)
    eye = jnp.eye(RANK, dtype=BF)

    def spread_of(order):
        chosen = (order[:, None] == jnp.arange(NADAPT, dtype=jnp.int32)[None, :]).astype(BF)
        return (chosen[:, None, :, None] * eye[None, :, None, :]).reshape(-1, NADAPT * RANK)

    index = line_order()
    picked = index[:, None] == jnp.arange(index.shape[0])[None, :]
    near_ids = jnp.sum(jnp.where(picked[:, :, None], ids.reshape(1, -1, 2), 0), axis=1)
    near_ids = join(near_ids[:, :1], near_ids[:, 1:], place.core, 1).T.reshape(-1)
    spread, spread_near = spread_of(ids), spread_of(near_ids)
    turned, turned_near = spread.T, spread_near.T
    text = wide_table(distance_table)

    turning = own_rows(cotangent, place)
    settled = (kernel, text, spread, spread_near, turned, turned_near, turning)
    (kernel, text, spread, spread_near, turned, turned_near, turning) = lax.optimization_barrier(
        settled
    )

    base_in = gathered(side_half(ffn1_in, place))
    own, following = all_rows(inputs, place)
    rows_own, rows_next = start_rows(where, own, following)
    base_out = gathered(after(side_half(ffn1_out, place), (base_in, rows_own, rows_next)))
    in_side, in_core = by_side(base_in), by_core(base_in)
    local = jnp.concatenate(
        [side_half(w, place) for w in (query_w, key_w, value_w, out_w)], axis=1
    )
    base_heads = gathered(after(local, (base_out, in_side, in_core, turning, spread, kernel)))
    out_side, out_core = by_side(base_out), by_core(base_out)
    w1_in = [base_in, in_core, in_side, by_core(in_side)]
    pair_local = side_half(conv_in_w, place)
    local = jnp.concatenate(
        [pair_local[:, 0], pair_local[:, 1], side_half(conv_out_w, place)], axis=1
    )
    step = local.shape[1]
    local = jnp.concatenate([local, jnp.zeros_like(local[:, : step // 3])], axis=1)
    base_convs = gathered(after(local, (base_heads, out_side, out_core, w1_in[3])))
    w1_out = [base_out, out_core, out_side, by_core(out_side)]
    heads_side, heads_pair = by_side(base_heads), by_pair(base_heads)
    heads_core = by_core(base_heads)
    local = jnp.concatenate([side_half(w, place) for w in (ffn2_in, ffn2_out)], axis=1)
    part, send, pre, t_in, t_out = ffn(
        0, 0, 7, where, rows_own, rows_next, w1_in, w1_out, adapters
    )
    kept_one = (rows_own, rows_next, (pre, t_in, t_out))
    base_two = gathered(after(local, (base_convs, heads_side, heads_pair, heads_core, send)))
    heads_far = by_side(heads_pair)
    heads = [base_heads, heads_core, heads_pair, by_core(heads_pair)]
    heads += [heads_side, by_core(heads_side), heads_far, by_core(heads_far)]
    base_convs = base_convs[:, :step]
    convs_pair = by_pair(after(base_convs, heads_pair))
    convs_side = by_side(after(base_convs, heads_far))

    first, slots, t_heads = heads_forward(
        where, own.astype(F32), part, by_pair(send), heads, adapt_down, adapt_up
    )
    slots = exchanged(slots)
    convs_far = by_pair(after(convs_side, tuple(slots)))
    two_side = by_side(after(base_two, tuple(slots)))
    mixed, logs = attend(block, slots, text)
    convs = [base_convs, convs_pair, convs_side, convs_far]
    convs = [v for piece in convs for v in (piece, by_core(after(piece, mixed)))]
    mixed = exchanged([mixed[n] for n in range(4)])
    second, value, gate, edge, t_mix, t_pair = pair_forward(
        where, first, mixed, heads, convs, adapt_down, adapt_up
    )
    w2 = [base_two, by_core(after(base_two, mixed[0])), two_side, by_core(after(two_side, edge))]
    edge = lax.ppermute(edge, ("ctx", "tp"), NEXT)
    conv, third, rows_own, t_conv = conv_forward(
        taps, where, second, value, gate, edge, kernel, convs, adapt_down, adapt_up
    )
    rows_next = by_pair(rows_own)
    part, send, pre, t_in, t_out = ffn(1, 5, 8, where, rows_own, rows_next, w2, w2, adapters)
    kept_two = (rows_own, rows_next, (pre, t_in, t_out))

    output, grad, half = turn(where, third, part, by_pair(send), turning)
    part, send, sums_two = ffn_back(
        1, 5, 8, where, half, by_pair(half), *kept_two, w2, w2, adapters
    )
    grad, grad_conv, edge, partial = conv_back(
        taps, where, grad, part, by_pair(send), third, conv, t_conv, convs, adapt_down, adapt_up
    )
    came = after(by_side(after(sums_two[1], send)), grad_conv)
    sums_two = sums_two[0] + came
    edge = lax.ppermute(edge, ("ctx", "tp"), BEFORE)
    grad, grad_slots, conv_sums, partial = pair_back(
        taps, where, grad, grad_conv, edge, value, gate, kernel, second, t_pair, t_mix, mixed,
        partial, heads, convs, adapt_down, adapt_up,
    )
    came = after(by_pair(sums_two[2:4]), grad)
    sums_two = jnp.concatenate([sums_two[:2] + came, sums_two[4:]], axis=0)
    found_two = everywhere(sums_two)
    grad_slots = exchanged(grad_slots)
    back = attend_back(block, slots, grad_slots, text, logs)
    output = feature_parts(output, place)
    back = exchanged([back[n] for n in range(4)])
    grad, half, head_sums = heads_back(
        after(where, output), grad, first, t_heads, back, partial, conv_sums, heads,
        adapt_down, adapt_up,
    )
    other_half = by_pair(half)
    head_sums = head_sums[0] + by_side(head_sums[1].astype(BF)).astype(F32)
    head_sums = head_sums[0] + by_pair(head_sums[1].astype(BF)).astype(F32)
    found_heads = everywhere(after(head_sums, other_half))
    part, send, sums_one = ffn_back(
        0, 0, 7, where, half, other_half, *kept_one, w1_in, w1_out, adapters
    )
    sums_one = sums_one[0] + by_side(sums_one[1].astype(BF)).astype(F32)
    sums_one = jnp.concatenate([sums_one[:2] + by_pair(sums_one[2:4]), sums_one[4:]], axis=0)
    line = around_shard(sums_one.astype(BF))
    pieces = [line, by_pair(line), by_side(line)]
    pieces.append(by_pair(pieces[2]))
    pieces = [v for piece in pieces for v in (piece, by_core(piece))]
    input_grad = finish(where, grad, part, by_pair(send), own)
    input_grad = feature_parts(input_grad, place).astype(F32)

    outs = [shape(v.shape, F32) for v in (adapt_down, adapt_up, adapt_down_ff, adapt_up_ff)]
    ffn_blocks, ffn_rows = sums_two.shape[:2]
    plan = [(kind, slot, rows_of(0, 2, ffn_rows, g)) for kind, slot, g in ((0, 5, 0), (1, 8, 1))]
    plan += [
        (kind, 1, rows_of(0, ffn_blocks, ffn_rows, g, 2)) for kind, g in ((2, 0), (3, 1))
    ]
    outs = expand(plan, spread, turned, after(found_two, send), outs)
    head_blocks, head_rows = head_sums.shape[:2]
    places = ((0, 1), (0, 2), (0, 3), (1, 5), (1, 0), (1, 1), (1, 2), (0, 6))
    places += ((0, 4), (1, 6), (0, 7), (1, 3), (1, 4))
    plan = [
        (kind, slot, rows_of(0, head_blocks, head_rows, g))
        for g, (kind, slot) in enumerate(places)
    ]
    outs = expand(plan, spread, turned, found_heads, outs)
    outs = expand_near(
        [(False, 0, 0, 0), (False, 1, 7, 1), (True, 2, 0, 0), (True, 3, 0, 1)],
        where, spread_near, turned_near, pieces, outs,
    )
    return (output, input_grad, outs[0], outs[2], outs[1], outs[3])


def solution(mesh):
    placed = (
        P("shard", "ctx", "tp"),
        P("shard"),
        P("shard", "ctx", "tp"),
        P("shard", "tp"),
        P("shard", "tp"),
        P("shard", "tp"),
        P("shard", "tp"),
        P("shard", "tp"),
        P("shard", "tp"),
        P("shard", None, "tp"),
        P(None, "tp"),
        P("shard", "tp"),
        P("shard", "tp"),
        P("shard", "tp"),
        P(),
        P(),
        P(),
        P(),
        P(),
    )
    return jax.shard_map(
        on_device,
        mesh=mesh,
        in_specs=placed,
        out_specs=(P("shard", "ctx", "tp"), P("shard", "ctx", "tp"), P(), P(), P(), P()),
        check_vma=False,
    )
```

```python
import jax
import jax.numpy as jnp
from jax import lax
from jax.experimental import pallas as pl
from jax.experimental.pallas import tpu as pltpu
from jax.sharding import PartitionSpec as P

LEFT = 64
RIGHT = 8
NADAPT = 8
RANK = 16
HEAD = 64
LANES = 128
eps = 1e-05
BF = jnp.bfloat16
F32 = jnp.float32

CORE = [(0, 1), (1, 0), (2, 3), (3, 2)]
PAIR = [(0, 2), (2, 0), (1, 3), (3, 1)]
SIDE = [(0, 1), (1, 0)]
ACROSS = [(s * 4 + t, (1 - s) * 4 + (t ^ 2)) for s in range(2) for t in range(4)]


def block_at(block, core):
    return (block // 2) * 4 + (block % 2) * 2 + core


NEXT = [(block_at(n, k), block_at(n + 1, k)) for n in range(3) for k in range(2)]
BEFORE = [(block_at(n + 1, k), block_at(n, k)) for n in range(3) for k in range(2)]


def by_core(value):
    return lax.ppermute(value, "tp", CORE)


def by_pair(value):
    return lax.ppermute(value, "tp", PAIR)


def by_side(value):
    return lax.ppermute(value, "ctx", SIDE)


def across(value):
    return lax.ppermute(value, ("ctx", "tp"), ACROSS)


def wide_table(table):
    place = jnp.arange(4*LANES, dtype=jnp.int32)
    index = jnp.where(place < 3*LANES, jnp.clip(place - LEFT, 0, LEFT+RIGHT), 0)
    pick = (index[:, None] == jnp.arange(table.shape[0], dtype=jnp.int32)[None, :]).astype(BF)
    rows = jnp.dot(pick, table, preferred_element_type=F32).astype(BF)
    return jnp.concatenate([rows, rows], axis=1)

def load_blocks(b_ref, sources, target, sems, parts):
    copies=[]
    for j, source in enumerate(sources):
        rows = source.shape[0]; cols = source.shape[1]//parts
        for part in range(parts):
            copies.append(pltpu.make_async_copy(
                source.at[:, part*cols:(part+1)*cols],
                target.at[part, pl.ds(pl.multiple_of((b_ref[0] ^ j)*rows, rows), rows), :],
                sems.at[j*parts+part]))
    for c in copies: c.start()
    for c in copies: c.wait()

def window(r0, length):
    lo=max(r0-LANES,0); hi=min(r0+2*LANES,length)
    return lo,hi

def biased(s, near, p, rows, length):
    parts=[]
    for sub in range(rows//LANES):
        r0=p*rows+sub*LANES
        e=near[sub*LANES:(sub+1)*LANES]
        band=pltpu.roll(e, 0, 1, stride=1, stride_axis=0)
        lo,hi=window(r0,length)
        pieces=[]
        if lo>0: pieces.append(jnp.broadcast_to(e[:,0:1],(LANES,lo)))
        pieces.append(band[:, lo-r0+LANES:hi-r0+LANES])
        if hi<length: pieces.append(jnp.broadcast_to(e[:,2*LANES-1:2*LANES],(LANES,length-hi)))
        parts.append(jnp.concatenate(pieces,axis=1))
    return s+jnp.concatenate(parts,axis=0)


def fwd_kernel(b_ref, s0,s1,s2,s3, text_ref, o_ref, lse_ref, qkv, sems):
    dc=pl.program_id(0); k=pl.program_id(1)
    @pl.when((dc==0)&(k==0))
    def _(): load_blocks(b_ref,(s0,s1,s2,s3),qkv,sems,2)
    rows=o_ref.shape[1]; length=qkv.shape[1]
    own=(lax.broadcasted_iota(jnp.int32,(rows,LANES),1)//64)==k
    key=qkv[dc,:,LANES:2*LANES]; val=qkv[dc,:,2*LANES:]
    for p in range(length//rows):
        q=qkv[dc,p*rows:(p+1)*rows,0:LANES].astype(F32)*0.125
        q=jnp.where(own,q,0.0).astype(BF)
        s=biased(nt(q,key),nt(q,text_ref[...]),p,rows,length)
        top=jnp.max(s,axis=-1,keepdims=True)
        e=jnp.exp(s-top)
        tot=jnp.sum(e,axis=-1,keepdims=True)
        o=jnp.dot(e.astype(BF),val,preferred_element_type=F32)/tot
        o=o.astype(BF)
        slot=p^b_ref[0]
        @pl.when(k==0)
        def _(): o_ref[slot]=o
        @pl.when(k==1)
        def _(): o_ref[slot]=jnp.where(own,o,o_ref[slot])
        lse_ref[0,p*rows:(p+1)*rows,:]=top+jnp.log(tot)

def attend(b, slots, text):
    rows=slots[0].shape[0]; n=len(slots); length=rows*n
    anys=[pl.BlockSpec(memory_space=pl.ANY)]*n
    return pl.pallas_call(
        fwd_kernel,
        grid_spec=pltpu.PrefetchScalarGridSpec(
            num_scalar_prefetch=1, grid=(2,2),
            in_specs=anys+[pl.BlockSpec(text.shape,lambda d,k,b:(0,0))],
            out_specs=(pl.BlockSpec((n,rows,LANES),lambda d,k,b:(0,0,d)),
                       pl.BlockSpec((1,length,1),lambda d,k,b:(2*d+k,0,0))),
            scratch_shapes=[pltpu.VMEM((2,length,3*LANES),BF),pltpu.SemaphoreType.DMA((2*n,))]),
        out_shape=(jax.ShapeDtypeStruct((n,rows,2*LANES),BF),jax.ShapeDtypeStruct((4,length,1),F32)),
        compiler_params=pltpu.CompilerParams(vmem_limit_bytes=48<<20),
        name="attend",
        cost_estimate=pl.CostEstimate(flops=4*4*length*length*64,bytes_accessed=length*8*LANES*2,transcendentals=4*length*length),
    )(b,*slots,text)

def bwd_kernel(b_ref, s0,s1,s2,s3, g0,g1,g2,g3, text_ref, lse_ref, out_ref, qkv, gout, dq_acc, dk_acc, dv_acc, sems, gsems):
    dc=pl.program_id(0); k=pl.program_id(1)
    @pl.when((dc==0)&(k==0))
    def _():
        load_blocks(b_ref,(s0,s1,s2,s3),qkv,sems,2)
        load_blocks(b_ref,(g0,g1,g2,g3),gout,gsems,2)
    rows=out_ref.shape[1]; length=qkv.shape[1]
    own=(lax.broadcasted_iota(jnp.int32,(rows,LANES),1)//64)==k
    key=qkv[dc,:,LANES:2*LANES]; val=qkv[dc,:,2*LANES:]
    text=text_ref[...]
    turn=((lax.broadcasted_iota(jnp.int32,(LANES,LANES),0)+lax.broadcasted_iota(jnp.int32,(LANES,LANES),1))==LANES-1).astype(BF)
    @pl.when(k==0)
    def _():
        dk_acc[...]=jnp.zeros_like(dk_acc); dv_acc[...]=jnp.zeros_like(dv_acc)
    for p in range(length//rows):
        span=slice(p*rows,(p+1)*rows)
        q=qkv[dc,span,0:LANES].astype(F32)*0.125
        q=jnp.where(own,q,0.0).astype(BF)
        g=jnp.where(own,gout[dc,span,:].astype(F32),0.0).astype(BF)
        s=biased(nt(q,key),nt(q,text),p,rows,length)
        pr=jnp.exp(s-lse_ref[0,span,:])
        dp=nt(g,val)
        w=pr*dp
        ds=(w-pr*jnp.sum(w,axis=-1,keepdims=True)).astype(BF)
        dv_acc[...]+=tn(g,pr.astype(BF))
        dk_acc[...]+=tn(q,ds)
        dq=jnp.dot(ds,key,preferred_element_type=F32)
        extra=[]
        t_lo=text[0:1,:].astype(F32); t_hi=text[2*LANES-1:2*LANES,:].astype(F32)
        for sub in range(rows//LANES):
            r0=p*rows+sub*LANES
            lo,hi=window(r0,length)
            d=ds[sub*LANES:(sub+1)*LANES].astype(F32)
            pieces=[]
            if lo-r0+LANES>0: pieces.append(jnp.zeros((LANES,lo-r0+LANES),F32))
            pieces.append(d[:,lo:hi])
            pieces.append(jnp.zeros((LANES,4*LANES-(hi-r0+LANES)),F32))
            w=jnp.concatenate(pieces,axis=1)
            w=jnp.dot(turn,w.astype(BF),preferred_element_type=F32)
            w=pltpu.roll(w,3*LANES+1,1,stride=1,stride_axis=0)
            w=jnp.dot(turn,w.astype(BF),preferred_element_type=F32)
            x=jnp.dot(w.astype(BF),text,preferred_element_type=F32)
            if lo>0: x+=jnp.sum(d[:,:lo],axis=-1,keepdims=True)*t_lo
            if hi<length: x+=jnp.sum(d[:,hi:],axis=-1,keepdims=True)*t_hi
            extra.append(x)
        dq=(dq+jnp.concatenate(extra,axis=0))*0.125
        dq_acc[span,:]=jnp.where(own,dq,dq_acc[span,:])
    @pl.when(k==1)
    def _():
        for p in range(length//rows):
            slot=p^b_ref[0]; span=slice(p*rows,(p+1)*rows)
            out_ref[slot,:,0:LANES]=dq_acc[span,:].astype(BF)
            out_ref[slot,:,LANES:2*LANES]=dk_acc[:,span].T.astype(BF)
            out_ref[slot,:,2*LANES:]=dv_acc[:,span].T.astype(BF)

def attend_back(b, slots, grads, text, lse):
    rows=slots[0].shape[0]; n=len(slots); length=rows*n
    anys=[pl.BlockSpec(memory_space=pl.ANY)]*(2*n)
    return pl.pallas_call(
        bwd_kernel,
        grid_spec=pltpu.PrefetchScalarGridSpec(
            num_scalar_prefetch=1, grid=(2,2),
            in_specs=anys+[pl.BlockSpec(text.shape,lambda d,k,b:(0,0)),pl.BlockSpec((1,length,1),lambda d,k,b:(2*d+k,0,0))],
            out_specs=pl.BlockSpec((n,rows,3*LANES),lambda d,k,b:(0,0,d)),
            scratch_shapes=[pltpu.VMEM((2,length,3*LANES),BF),pltpu.VMEM((2,length,LANES),BF),
              pltpu.VMEM((length,LANES),F32),pltpu.VMEM((LANES,length),F32),pltpu.VMEM((LANES,length),F32),
              pltpu.SemaphoreType.DMA((2*n,)),pltpu.SemaphoreType.DMA((2*n,))]),
        out_shape=jax.ShapeDtypeStruct((n,rows,6*LANES),BF),
        compiler_params=pltpu.CompilerParams(vmem_limit_bytes=30<<20),
        name="attend_back",
        cost_estimate=pl.CostEstimate(flops=10*4*length*length*64,bytes_accessed=length*14*LANES*2,transcendentals=4*length*length),
    )(b,*slots,*grads,text,lse)


def nn(first, second):
    return jnp.dot(first, second, preferred_element_type=F32)


def nt(first, second):
    return lax.dot_general(first, second, (((1,), (1,)), ((), ())), preferred_element_type=F32)


def tn(first, second):
    return lax.dot_general(first, second, (((0,), (0,)), ((), ())), preferred_element_type=F32)


def normalize(value):
    mean = jnp.mean(value, axis=-1, keepdims=True)
    square = jnp.mean(value * value, axis=-1, keepdims=True)
    scale = lax.rsqrt(square - mean * mean + eps)
    return ((value - mean) * scale, scale)


def normalize_back(grad, normed, scale):
    mean = jnp.mean(grad, axis=-1, keepdims=True)
    cross = jnp.mean(grad * normed, axis=-1, keepdims=True)
    return scale * (grad - mean - normed * cross)


def swish_slope(value, sigma):
    return sigma + value * sigma * (1.0 - sigma)


def mask_row(adapter):
    lanes = lax.broadcasted_iota(jnp.int32, (1, NADAPT * RANK), 1)
    return (lanes // RANK == adapter).astype(F32)


def chosen_rows(adapter):
    shape = (RANK, NADAPT * RANK)
    lanes = lax.broadcasted_iota(jnp.int32, shape, 1)
    rows = lax.broadcasted_iota(jnp.int32, shape, 0)
    return (lanes == rows + adapter * RANK).astype(BF)


def compact(pick, value):
    return nt(pick, value).astype(BF)


class Fetches:
    def __init__(self, sems):
        self.sems = sems
        self.used = 0

    def __call__(self, source, target):
        copy = pltpu.make_async_copy(source, target, self.sems.at[self.used])
        self.used += 1
        copy.start()
        return copy


def wait_all(copies):
    for copy in copies:
        copy.wait()


def block_of(where, number):
    side, pair, core = number // 4, (number // 2) % 2, number % 2
    return ((where[0] ^ pair) * 2 + (where[1] ^ core)) * 2 + (where[2] ^ side)


def fetch_columns(fetch, where, source, target):
    found = []
    for number in range(8):
        start = pl.multiple_of(block_of(where, number) * LANES, LANES)
        place = pl.ds(number * LANES, LANES)
        found.append(fetch(source.at[:, pl.ds(start, LANES)], target.at[:, place]))
    return found


def fetch_rows(fetch, where, source, target):
    found = []
    for number in range(8):
        start = pl.multiple_of(block_of(where, number) * LANES, LANES)
        place = pl.ds(number * LANES, LANES)
        found.append(fetch(source.at[pl.ds(start, LANES), :], target.at[place, :]))
    return found


def store_absolute(where, out, first, value):
    rows = value.shape[0]
    for number in range(8):
        pair, side, half = number // 4, (number // 2) % 2, number % 2
        out[side ^ where[2], pair ^ where[0], half, first : first + rows, :] = value[
            :, number * LANES : (number + 1) * LANES
        ]


def store_relative(where, out, first, value, number):
    side, pair, core = number // 4, (number // 2) % 2, number % 2
    out[(where[1] ^ core) ^ where[2], pair, where[2] ^ side, first : first + value.shape[0], :] = value


def store_edge(out, value, flip_side):
    rows = value.shape[0]
    width = value.shape[1] // 4
    for side in range(2):
        for pair in range(2):
            start = (2 * side + pair) * width
            out[side ^ flip_side, 1 - pair] = value[:, start : start + width]


def read_edge(edge):
    return jnp.concatenate([edge[s, p] for s in range(2) for p in range(2)], axis=1)


VMEM_SPEC = pl.BlockSpec(memory_space=pltpu.VMEM)
ANY_SPEC = pl.BlockSpec(memory_space=pltpu.HBM)
SMEM_SPEC = pl.BlockSpec(memory_space=pltpu.SMEM)


def run(body, name, places, outs, scratch, operands, flops=0, room=44, out_specs=None):
    specs = [SMEM_SPEC] + [VMEM_SPEC if p == "v" else ANY_SPEC for p in places]
    moved = sum(o.size * o.dtype.itemsize for o in list(operands[1:]) + list(outs))
    return pl.pallas_call(
        body,
        name=name,
        in_specs=specs,
        out_specs=out_specs or [VMEM_SPEC] * len(outs),
        out_shape=outs,
        scratch_shapes=scratch,
        compiler_params=pltpu.CompilerParams(vmem_limit_bytes=room << 20),
        cost_estimate=pl.CostEstimate(
            flops=flops, bytes_accessed=min(moved, 16 << 20), transcendentals=0
        ),
    )(*operands)


def shape(dims, dtype):
    return jax.ShapeDtypeStruct(dims, dtype)


def fetch_ffn_adapters(fetch, where, which, column, up_ff, down_ff, p_in, q_in, p_out):
    found = []
    for number in range(4):
        side, core = number // 2, number % 2
        start = (2 * where[0] + (where[1] ^ core)) * (2 * column) + (where[2] ^ side) * column
        start = pl.multiple_of(start, column)
        place = pl.ds(number * column, column)
        found.append(fetch(up_ff.at[which, :, pl.ds(start, column)], q_in.at[:, place]))
        found.append(fetch(down_ff.at[which, pl.ds(start, column), :], p_out.at[place, :]))
    return found


def ffn_body(which, down_at, up_at, column, where, own, following, *refs):
    ins, outs, ups = refs[:4], refs[4:8], refs[8:12]
    down, down_ff, up, up_ff = ups
    part, send, pre_out, t_in_out, t_out_out = refs[12:17]
    rows, w_in, w_out, p_in, q_in, p_out, q_out, pre, active, sems = refs[17:]
    fetch = Fetches(sems)
    count = own.shape[0]
    small = [fetch(down.at[down_at], p_in), fetch(up.at[up_at], q_out)]
    small += fetch_ffn_adapters(fetch, where, which, column, up_ff, down_ff, p_in, q_in, p_out)
    first = [
        fetch(r.at[:, pl.ds(0, column)], w_in.at[:, pl.ds(n * column, column)])
        for n, r in enumerate(ins)
    ]
    second = [
        fetch(r.at[:, pl.ds(r.shape[1] - column, column)], w_out.at[:, pl.ds(n * column, column)])
        for n, r in enumerate(outs)
    ]
    mask = mask_row(where[3])
    rows[:count] = own[...]
    rows[count:] = following[...]
    wait_all(small)
    t_in = (nn(rows[...], p_in[...]) * mask).astype(BF)
    t_in_out[...] = t_in
    t_out = jnp.zeros(t_in.shape, F32)
    saved = []
    for n in range(4):
        span = slice(n * column, (n + 1) * column)
        first[n].wait()
        value = nn(rows[...], w_in[:, span]) + nn(t_in, q_in[:, span])
        pre[n] = value
        saved.append(fetch(pre.at[n], pre_out.at[n]))
        act = (value * jax.nn.sigmoid(value)).astype(BF)
        active[:, span] = act
        t_out = t_out + nn(act, p_out[span, :])
    t_out = (t_out * mask).astype(BF)
    t_out_out[...] = t_out
    wait_all(second)
    width = w_out.shape[0] // 2
    for n in range(2):
        span = slice(n * width, (n + 1) * width)
        total = nt(active[...], w_out[span, :]) + nn(t_out, q_out[:, span])
        part[:, span] = total[:count]
        send[:, span] = total[count:].astype(BF)
    wait_all(saved)


def ffn(which, down_at, up_at, where, own, following, w_in, w_out, adapters):
    count, width = own.shape
    column = adapters[3].shape[2] // 8
    hidden = 4 * column
    ranks = NADAPT * RANK

    def body(*refs):
        ffn_body(which, down_at, up_at, column, *refs)

    return run(
        body,
        "hidden_forward",
        "vv" + "a" * 12,
        [
            shape((count, width), F32),
            shape((count, width), BF),
            shape((4, 2 * count, column), F32),
            shape((2 * count, ranks), BF),
            shape((2 * count, ranks), BF),
        ],
        [
            pltpu.VMEM((2 * count, width), BF),
            pltpu.VMEM((width, hidden), BF),
            pltpu.VMEM((width, hidden), BF),
            pltpu.VMEM((width, ranks), BF),
            pltpu.VMEM((ranks, hidden), BF),
            pltpu.VMEM((hidden, ranks), BF),
            pltpu.VMEM((ranks, width), BF),
            pltpu.VMEM((4, 2 * count, column), F32),
            pltpu.VMEM((2 * count, hidden), BF),
            pltpu.SemaphoreType.DMA((22,)),
        ],
        [where, own, following, *w_in, *w_out, *adapters],
        flops=8 * count * width * hidden,
        out_specs=[VMEM_SPEC, VMEM_SPEC, ANY_SPEC, VMEM_SPEC, VMEM_SPEC],
    )


def ffn_back_body(which, down_at, up_at, column, where, own, following, u_own, u_next, t_in, t_out, *refs):
    pre_in = refs[0]
    ins, outs, ups = refs[1:5], refs[5:9], refs[9:13]
    down, down_ff, up, up_ff = ups
    part, send, grads = refs[13:16]
    full, rows, w_in, w_out, p_in, q_in, p_out, q_out, pre, active, slope, sems = refs[16:]
    fetch = Fetches(sems)
    count = own.shape[0]
    small = [fetch(down.at[down_at], p_in), fetch(up.at[up_at], q_out)]
    small += fetch_ffn_adapters(fetch, where, which, column, up_ff, down_ff, p_in, q_in, p_out)
    second = []
    kept = []
    for n, r in enumerate(outs):
        source = r.at[:, pl.ds(r.shape[1] - column, column)]
        second.append(fetch(source, w_out.at[:, pl.ds(n * column, column)]))
        kept.append(fetch(pre_in.at[n], pre.at[n]))
    first = [
        fetch(r.at[:, pl.ds(0, column)], w_in.at[:, pl.ds(n * column, column)])
        for n, r in enumerate(ins)
    ]
    mask = mask_row(where[3])
    pick = chosen_rows(where[3])
    full[:count] = own[...]
    full[count:] = following[...]
    rows[:count] = u_own[...]
    rows[count:] = u_next[...]
    wait_all(small)
    r_out = (nt(full[...], q_out[...]) * mask).astype(BF)
    c_out = compact(pick, r_out)
    c_t_in = compact(pick, t_in[...])
    r_in = jnp.zeros(r_out.shape, F32)
    for n in range(4):
        span = slice(n * column, (n + 1) * column)
        second[n].wait()
        kept[n].wait()
        grad = nn(full[...], w_out[:, span]) + nt(r_out, p_out[span, :])
        value = pre[n]
        sigma = jax.nn.sigmoid(value)
        act = (value * sigma).astype(BF)
        grad = (grad * swish_slope(value, sigma)).astype(BF)
        slope[:, span] = grad
        r_in = r_in + nt(grad, q_in[:, span])
        side, core = n // 2, n % 2
        near = (where[1] ^ core) ^ where[2]
        far = where[2] ^ side
        both = jnp.concatenate([nn(c_out, act), nn(c_t_in, grad)], axis=0)
        for piece in range(column // LANES):
            grads[near, 4 + far * (column // LANES) + piece] = both[
                :, piece * LANES : (piece + 1) * LANES
            ]
    r_in = (r_in * mask).astype(BF)
    wait_all(first)
    width = w_in.shape[0] // 2
    for n in range(2):
        span = slice(n * width, (n + 1) * width)
        total = nt(slope[...], w_in[span, :]) + nt(r_in, p_in[span, :])
        part[:, span] = total[:count]
        send[:, span] = total[count:].astype(BF)
    narrow = jnp.concatenate(
        [nn(compact(pick, r_in), rows[...]), nn(compact(pick, t_out[...]), full[...])], axis=0
    )
    for number in range(8):
        pair, side, half = number // 4, (number // 2) % 2, number % 2
        grads[side ^ where[2], 2 * (pair ^ where[0]) + half] = narrow[
            :, number * LANES : (number + 1) * LANES
        ]


def ffn_back(which, down_at, up_at, where, own, following, u_own, u_next, kept, w_in, w_out, adapters):
    pre, t_in, t_out = kept
    count, width = own.shape
    column = adapters[3].shape[2] // 8
    hidden = 4 * column
    ranks = NADAPT * RANK

    def body(*refs):
        ffn_back_body(which, down_at, up_at, column, *refs)

    return run(
        body,
        "hidden_backward",
        "vvvvvv" + "a" * 13,
        [
            shape((count, width), F32),
            shape((count, width), BF),
            shape((2, 4 + 2 * column // LANES, 2 * RANK, LANES), F32),
        ],
        [
            pltpu.VMEM((2 * count, width), BF),
            pltpu.VMEM((2 * count, width), BF),
            pltpu.VMEM((width, hidden), BF),
            pltpu.VMEM((width, hidden), BF),
            pltpu.VMEM((width, ranks), BF),
            pltpu.VMEM((ranks, hidden), BF),
            pltpu.VMEM((hidden, ranks), BF),
            pltpu.VMEM((ranks, width), BF),
            pltpu.VMEM((4, 2 * count, column), F32),
            pltpu.VMEM((2 * count, hidden), BF),
            pltpu.VMEM((2 * count, hidden), BF),
            pltpu.SemaphoreType.DMA((22,)),
        ],
        [where, own, following, u_own, u_next, t_in, t_out, pre, *w_in, *w_out, *adapters],
        flops=8 * count * width * hidden,
    )


def fetch_heads(fetch, where, pieces, up, wide):
    width = pieces[0].shape[0]
    three = 3 * LANES
    found = []
    for number, piece in enumerate(pieces):
        slot, core = number // 2, number % 2
        found.append(
            fetch(
                piece.at[:, pl.ds(0, three)],
                wide.at[slot, pl.ds(0, width), pl.ds(core * three, three)],
            )
        )
        start = pl.multiple_of(block_of(where, number) * LANES, LANES)
        for kind in range(3):
            found.append(
                fetch(
                    up.at[kind, :, pl.ds(start, LANES)],
                    wide.at[
                        slot,
                        pl.ds(width + kind * LANES, LANES),
                        pl.ds(core * three + kind * LANES, LANES),
                    ],
                )
            )
    return found


def clear_heads(wide, width):
    for kind in range(3):
        span = slice(width + kind * LANES, width + (kind + 1) * LANES)
        for core in range(2):
            for other in range(3):
                if other != kind:
                    at = (core * 3 + other) * LANES
                    for slot in range(4):
                        wide[slot, span, at : at + LANES] = jnp.zeros((LANES, LANES), BF)


def heads_body(where, resid, part, other, *refs):
    pieces = refs[:8]
    down, up = refs[8:10]
    first = refs[10]
    slots = refs[11:15]
    t_out = refs[15]
    wide, thin, sems = refs[16:]
    width = resid.shape[1]
    fetch = Fetches(sems)
    small = [
        fetch(down.at[1 + kind], thin.at[:, pl.ds(kind * LANES, LANES)]) for kind in range(3)
    ]
    large = fetch_heads(fetch, where, pieces, up, wide)
    clear_heads(wide, width)
    value = resid[...] + 0.5 * (part[...] + other[...].astype(F32))
    first[...] = value
    rows = normalize(value)[0].astype(BF)
    mask = jnp.concatenate([mask_row(where[3])] * 3, axis=1)
    wait_all(small)
    reduced = (nn(rows, thin[...]) * mask).astype(BF)
    t_out[...] = reduced
    both = jnp.concatenate([rows, reduced], axis=1)
    for slot in range(4):
        wait_all(large[slot * 8 : slot * 8 + 8])
        slots[slot][...] = nn(both, wide[slot]).astype(BF)


def heads_forward(where, resid, part, other, pieces, down, up):
    count, width = resid.shape
    three = 3 * LANES
    found = run(
        heads_body,
        "heads_forward",
        "vvv" + "a" * 10,
        [shape((count, width), F32)]
        + [shape((count, 2 * three), BF)] * 4
        + [shape((count, three), BF)],
        [
            pltpu.VMEM((4, width + three, 2 * three), BF),
            pltpu.VMEM((width, three), BF),
            pltpu.SemaphoreType.DMA((35,)),
        ],
        [where, resid, part, other, *pieces, down, up],
        flops=2 * count * width * 3 * width,
    )
    return (found[0], found[1:5], found[5])


def heads_back_body(where, grad, first, t_in, g0, g1, g2, g3, partial, convs, *refs):
    pieces = refs[:8]
    down, up = refs[8:10]
    result, half, grads = refs[10:13]
    wide, thin, sems = refs[13:]
    width = grad.shape[1]
    three = 3 * LANES
    fetch = Fetches(sems)
    small = [
        fetch(down.at[1 + kind], thin.at[:, pl.ds(kind * LANES, LANES)]) for kind in range(3)
    ]
    large = fetch_heads(fetch, where, pieces, up, wide)
    clear_heads(wide, width)
    normed, scale = normalize(first[...])
    rows = normed.astype(BF)
    pick = chosen_rows(where[3])
    mask = jnp.concatenate([mask_row(where[3])] * 3, axis=1)
    ranks = [compact(pick, t_in[:, k * LANES : (k + 1) * LANES]) for k in range(3)]
    total = None
    for slot, g in enumerate((g0, g1, g2, g3)):
        wait_all(large[slot * 8 : slot * 8 + 8])
        term = nt(g[...], wide[slot])
        total = term if total is None else total + term
        for core in range(2):
            for kind in range(3):
                at = core * three + kind * LANES
                store_relative(
                    where, grads, (4 + kind) * RANK, nn(ranks[kind], g[:, at : at + LANES]),
                    2 * slot + core,
                )
    reduced = (total[:, width:] * mask).astype(BF)
    wait_all(small)
    total = total[:, :width] + nt(reduced, thin[...])
    value = grad[...] + normalize_back(total, normed, scale)
    result[...] = value
    half[...] = (0.5 * value).astype(BF)
    for kind in range(3):
        found = nn(compact(pick, reduced[:, kind * LANES : (kind + 1) * LANES]), rows)
        store_absolute(where, grads, kind * RANK, found)
    for side in range(2):
        for pair in range(2):
            for piece in range(2):
                grads[side, pair, piece, 3 * RANK : 4 * RANK, :] = partial[
                    side, pair, piece, :RANK, :
                ]
                grads[side, pair, piece, 7 * RANK : 8 * RANK, :] = partial[
                    side, pair, piece, RANK:, :
                ]
                grads[side, pair, piece, 8 * RANK :, :] = convs[side, pair, piece]


def heads_back(where, grad, first, t_in, slots, partial, convs, pieces, down, up):
    count, width = grad.shape
    three = 3 * LANES
    return run(
        heads_back_body,
        "heads_backward",
        "v" * 9 + "a" * 10,
        [
            shape((count, width), F32),
            shape((count, width), BF),
            shape((2, 2, 2, 13 * RANK, LANES), F32),
        ],
        [
            pltpu.VMEM((4, width + three, 2 * three), BF),
            pltpu.VMEM((width, three), BF),
            pltpu.SemaphoreType.DMA((35,)),
        ],
        [where, grad, first, t_in, *slots, partial, convs, *pieces, down, up],
        flops=2 * count * width * 3 * width,
    )


def fetch_piece_columns(fetch, pieces, at, target):
    found = []
    for number, piece in enumerate(pieces):
        found.append(
            fetch(piece.at[:, pl.ds(at, LANES)], target.at[:, pl.ds(number * LANES, LANES)])
        )
    return found


def pair_body(where, first, m0, m1, m2, m3, *refs):
    heads, convs = refs[:8], refs[8:16]
    down, up = refs[16:18]
    second, value_out, gate_out, edge, t_mix_out, t_pair_out = refs[18:24]
    w_mix, w_value, w_gate, p_mix, q_mix, p_pair, q_value, q_gate, sems = refs[24:]
    fetch = Fetches(sems)
    mixing = fetch_rows(fetch, where, down.at[6], p_mix) + [fetch(up.at[5], q_mix)]
    mixing += fetch_piece_columns(fetch, heads, 3 * LANES, w_mix)
    pairs = [fetch(down.at[4], p_pair)]
    pairs += fetch_columns(fetch, where, up.at[3], q_value)
    pairs += fetch_columns(fetch, where, up.at[4], q_gate)
    pairs += fetch_piece_columns(fetch, convs, 0, w_value)
    gates = fetch_piece_columns(fetch, convs, LANES, w_gate)
    mask = mask_row(where[3])
    mixed = jnp.concatenate([m0[...], m1[...], m2[...], m3[...]], axis=1)
    wait_all(mixing)
    t_mix = (nn(mixed, p_mix[...]) * mask).astype(BF)
    t_mix_out[...] = t_mix
    value = first[...] + nt(mixed, w_mix[...]) + nn(t_mix, q_mix[...])
    second[...] = value
    rows = normalize(value)[0].astype(BF)
    wait_all(pairs)
    t_pair = (nn(rows, p_pair[...]) * mask).astype(BF)
    t_pair_out[...] = t_pair
    value = nn(rows, w_value[...]) + nn(t_pair, q_value[...])
    value_out[...] = value
    wait_all(gates)
    gate = nn(rows, w_gate[...]) + nn(t_pair, q_gate[...])
    gate_out[...] = gate
    last = value.shape[0] - edge.shape[2]
    store_edge(edge, value[last:] * jax.nn.sigmoid(gate[last:]), where[0])


def pair_forward(where, first, mixed, heads, convs, down, up):
    count, width = first.shape
    ranks = NADAPT * RANK
    square = pltpu.VMEM((width, width), BF)
    return run(
        pair_body,
        "pair_forward",
        "v" * 5 + "a" * 18,
        [
            shape((count, width), F32),
            shape((count, width), F32),
            shape((count, width), F32),
            shape((2, 2, 32, width // 4), F32),
            shape((count, ranks), BF),
            shape((count, ranks), BF),
        ],
        [
            square,
            square,
            square,
            pltpu.VMEM((width, ranks), BF),
            pltpu.VMEM((ranks, width), BF),
            pltpu.VMEM((width, ranks), BF),
            pltpu.VMEM((ranks, width), BF),
            pltpu.VMEM((ranks, width), BF),
            pltpu.SemaphoreType.DMA((50,)),
        ],
        [where, first, *mixed, *heads, *convs, down, up],
        flops=6 * count * width * width,
    )


def tap_sums(padded, taps, kernel, count, starts):
    found = []
    for number in range(padded.shape[0]):
        span = slice(number * LANES, (number + 1) * LANES)
        total = None
        for tap in range(taps):
            term = kernel[tap : tap + 1, span] * padded[number, starts[tap] : starts[tap] + count, :]
            total = term if total is None else total + term
        found.append(total)
    return jnp.concatenate(found, axis=1)


def conv_body(taps, where, second, value, gate, edge, kernel, *refs):
    convs = refs[:8]
    down, up = refs[8:10]
    conv_out, third, rows_out, t_out = refs[10:14]
    w_out, p_out, q_out, padded, sems = refs[14:]
    fetch = Fetches(sems)
    small = fetch_rows(fetch, where, down.at[7], p_out) + [fetch(up.at[6], q_out)]
    small += fetch_piece_columns(fetch, convs, 2 * LANES, w_out)
    count = second.shape[0]
    early = edge.shape[2]
    before = read_edge(edge)
    gated = value[...] * jax.nn.sigmoid(gate[...])
    for number in range(padded.shape[0]):
        span = slice(number * LANES, (number + 1) * LANES)
        padded[number, :early, :] = before[:, span]
        padded[number, early:, :] = gated[:, span]
    conv = tap_sums(padded, taps, kernel, count, [early - taps + 1 + k for k in range(taps)])
    conv_out[...] = conv
    normed = normalize(conv)[0]
    active = (normed * jax.nn.sigmoid(normed)).astype(BF)
    mask = mask_row(where[3])
    wait_all(small)
    reduced = (nn(active, p_out[...]) * mask).astype(BF)
    t_out[...] = reduced
    result = second[...] + nt(active, w_out[...]) + nn(reduced, q_out[...])
    third[...] = result
    rows_out[...] = normalize(result)[0].astype(BF)


def conv_forward(taps, where, second, value, gate, edge, kernel, convs, down, up):
    count, width = second.shape
    ranks = NADAPT * RANK

    def body(*refs):
        conv_body(taps, *refs)

    return run(
        body,
        "conv_forward",
        "v" * 5 + "a" * 10,
        [
            shape((count, width), F32),
            shape((count, width), F32),
            shape((count, width), BF),
            shape((count, ranks), BF),
        ],
        [
            pltpu.VMEM((width, width), BF),
            pltpu.VMEM((width, ranks), BF),
            pltpu.VMEM((ranks, width), BF),
            pltpu.VMEM((width // LANES, count + 32, LANES), F32),
            pltpu.SemaphoreType.DMA((17,)),
        ],
        [where, second, value, gate, edge, kernel, *convs, down, up],
        flops=2 * count * width * width,
    )


def conv_back_body(taps, where, grad, part, other, third, conv, t_in, *refs):
    convs = refs[:8]
    down, up = refs[8:10]
    result, grad_conv, edge, grads = refs[10:14]
    w_out, p_out, q_out, sems = refs[14:]
    fetch = Fetches(sems)
    small = fetch_rows(fetch, where, down.at[7], p_out) + [fetch(up.at[6], q_out)]
    small += fetch_piece_columns(fetch, convs, 2 * LANES, w_out)
    normed, scale = normalize(third[...])
    value = grad[...] + normalize_back(part[...] + other[...].astype(F32), normed, scale)
    result[...] = value
    full = value.astype(BF)
    mask = mask_row(where[3])
    pick = chosen_rows(where[3])
    wait_all(small)
    reduced = (nt(full, q_out[...]) * mask).astype(BF)
    active_grad = nn(full, w_out[...]) + nt(reduced, p_out[...])
    normed, scale = normalize(conv[...])
    sigma = jax.nn.sigmoid(normed)
    active = (normed * sigma).astype(BF)
    inner = normalize_back(active_grad * swish_slope(normed, sigma), normed, scale)
    grad_conv[...] = inner
    store_edge(edge, inner[: edge.shape[2]], 1 - where[0])
    store_absolute(where, grads, 0, nn(compact(pick, t_in[...]), full))
    found = nn(compact(pick, reduced), active)
    for number in range(8):
        store_relative(where, grads, RANK, found[:, number * LANES : (number + 1) * LANES], number)


def conv_back(taps, where, grad, part, other, third, conv, t_in, convs, down, up):
    count, width = grad.shape
    ranks = NADAPT * RANK

    def body(*refs):
        conv_back_body(taps, *refs)

    return run(
        body,
        "conv_backward",
        "v" * 6 + "a" * 10,
        [
            shape((count, width), F32),
            shape((count, width), F32),
            shape((2, 2, 32, width // 4), F32),
            shape((2, 2, 2, 2 * RANK, LANES), F32),
        ],
        [
            pltpu.VMEM((width, width), BF),
            pltpu.VMEM((width, ranks), BF),
            pltpu.VMEM((ranks, width), BF),
            pltpu.SemaphoreType.DMA((17,)),
        ],
        [where, grad, part, other, third, conv, t_in, *convs, down, up],
        flops=2 * count * width * width,
    )


def pair_back_body(
    taps, where, grad, grad_conv, edge, value, gate, kernel, second, t_pair, t_mix,
    m0, m1, m2, m3, partial, *refs
):
    heads, convs = refs[:8], refs[8:16]
    down, up = refs[16:18]
    result = refs[18]
    slots = refs[19:23]
    grads, mix_grads = refs[23:25]
    w_mix, w_value, w_gate, p_mix, q_mix, p_pair, q_value, q_gate, padded, sems = refs[25:]
    fetch = Fetches(sems)
    pairs = [fetch(down.at[4], p_pair)]
    pairs += fetch_columns(fetch, where, up.at[3], q_value)
    pairs += fetch_columns(fetch, where, up.at[4], q_gate)
    pairs += fetch_piece_columns(fetch, convs, 0, w_value)
    pairs += fetch_piece_columns(fetch, convs, LANES, w_gate)
    mixing = fetch_rows(fetch, where, down.at[6], p_mix) + [fetch(up.at[5], q_mix)]
    mixing += fetch_piece_columns(fetch, heads, 3 * LANES, w_mix)
    count = grad.shape[0]
    after = read_edge(edge)
    inner = grad_conv[...]
    for number in range(padded.shape[0]):
        span = slice(number * LANES, (number + 1) * LANES)
        padded[number, :count, :] = inner[:, span]
        padded[number, count:, :] = after[:, span]
    gated = tap_sums(padded, taps, kernel, count, [taps - 1 - k for k in range(taps)])
    sigma = jax.nn.sigmoid(gate[...])
    half = gated * sigma
    g_value = half.astype(BF)
    g_gate = (half * value[...] * (1.0 - sigma)).astype(BF)
    mask = mask_row(where[3])
    pick = chosen_rows(where[3])
    normed, scale = normalize(second[...])
    rows = normed.astype(BF)
    wait_all(pairs)
    reduced = ((nt(g_value, q_value[...]) + nt(g_gate, q_gate[...])) * mask).astype(BF)
    total = nt(g_value, w_value[...]) + nt(g_gate, w_gate[...]) + nt(reduced, p_pair[...])
    value_now = grad[...] + normalize_back(total, normed, scale)
    result[...] = value_now
    store_absolute(where, grads, 0, nn(compact(pick, reduced), rows))
    rank = compact(pick, t_pair[...])
    up_value = nn(rank, g_value)
    up_gate = nn(rank, g_gate)
    for number in range(8):
        span = slice(number * LANES, (number + 1) * LANES)
        store_relative(where, grads, 3 * RANK, up_value[:, span], number)
        store_relative(where, grads, 4 * RANK, up_gate[:, span], number)
    for side in range(2):
        for pair in range(2):
            for piece in range(2):
                grads[side, pair, piece, RANK : 3 * RANK, :] = partial[side, pair, piece]
    full = value_now.astype(BF)
    wait_all(mixing)
    reduced = (nt(full, q_mix[...]) * mask).astype(BF)
    mixed_grad = (nn(full, w_mix[...]) + nt(reduced, p_mix[...])).astype(BF)
    width = mixed_grad.shape[1] // 4
    for slot in range(4):
        slots[slot][...] = mixed_grad[:, slot * width : (slot + 1) * width]
    store_absolute(where, mix_grads, 0, nn(compact(pick, t_mix[...]), full))
    mixed = jnp.concatenate([m0[...], m1[...], m2[...], m3[...]], axis=1)
    found = nn(compact(pick, reduced), mixed)
    for number in range(8):
        span = slice(number * LANES, (number + 1) * LANES)
        store_relative(where, mix_grads, RANK, found[:, span], number)


def pair_back(
    taps, where, grad, grad_conv, edge, value, gate, kernel, second, t_pair, t_mix, mixed,
    partial, heads, convs, down, up
):
    count, width = grad.shape
    ranks = NADAPT * RANK
    square = pltpu.VMEM((width, width), BF)

    def body(*refs):
        pair_back_body(taps, *refs)

    found = run(
        body,
        "pair_backward",
        "v" * 14 + "a" * 18,
        [shape((count, width), F32)]
        + [shape((count, width // 4), BF)] * 4
        + [
            shape((2, 2, 2, 5 * RANK, LANES), F32),
            shape((2, 2, 2, 2 * RANK, LANES), F32),
        ],
        [
            square,
            square,
            square,
            pltpu.VMEM((width, ranks), BF),
            pltpu.VMEM((ranks, width), BF),
            pltpu.VMEM((width, ranks), BF),
            pltpu.VMEM((ranks, width), BF),
            pltpu.VMEM((ranks, width), BF),
            pltpu.VMEM((width // LANES, count + 32, LANES), F32),
            pltpu.SemaphoreType.DMA((50,)),
        ],
        [
            where, grad, grad_conv, edge, value, gate, kernel, second, t_pair, t_mix, *mixed,
            partial, *heads, *convs, down, up,
        ],
        flops=6 * count * width * width,
        room=52,
    )
    return (found[0], found[1:5], found[5], found[6])


def start_body(where, own, following, own_out, next_out):
    own_out[...] = normalize(own[...].astype(F32))[0].astype(BF)
    next_out[...] = normalize(following[...].astype(F32))[0].astype(BF)


def start_rows(where, own, following):
    count, width = own.shape
    return run(
        start_body, "start_rows", "vv", [shape((count, width), BF)] * 2, [], [where, own, following]
    )


def turn_body(where, third, part, other, cotangent, output, grad, half):
    fourth = third[...] + 0.5 * (part[...] + other[...].astype(F32))
    normed, scale = normalize(fourth)
    output[...] = normed.astype(BF)
    value = normalize_back(cotangent[...].astype(F32), normed, scale)
    grad[...] = value
    half[...] = (0.5 * value).astype(BF)


def turn(where, third, part, other, cotangent):
    count, width = third.shape
    return run(
        turn_body,
        "turn",
        "vvvv",
        [shape((count, width), BF), shape((count, width), F32), shape((count, width), BF)],
        [],
        [where, third, part, other, cotangent],
    )


def finish_body(where, grad, part, other, own, result):
    normed, scale = normalize(own[...].astype(F32))
    total = part[...] + other[...].astype(F32)
    result[...] = (grad[...] + normalize_back(total, normed, scale)).astype(BF)


def finish(where, grad, part, other, own):
    count, width = grad.shape
    return run(
        finish_body, "finish", "vvvv", [shape((count, width), BF)], [], [where, grad, part, other, own]
    )[0]


def expand_body(plan, spread, turned, found, *refs):
    kinds = sorted({kind for kind, _, _ in plan})
    outs = refs[-len(kinds) - len(plan) - 1 : -len(plan) - 1]
    held = refs[-len(plan) - 1 : -1]
    sems = refs[-1]
    copies = []
    for item, (kind, slot, starts) in enumerate(plan):
        column = len(starts) * LANES
        for pair in range(2):
            for side in range(2):
                parts = [
                    found[:, side, pair, :, row : row + RANK, :].reshape(-1, LANES)
                    for row in starts
                ]
                value = jnp.concatenate(parts, axis=1)
                start = (2 * pair + side) * column
                if kind % 2 == 0:
                    held[item][start : start + column, :] = tn(value, spread[...])
                else:
                    held[item][:, start : start + column] = nn(turned[...], value)
        copy = pltpu.make_async_copy(held[item], outs[kinds.index(kind)].at[slot], sems.at[item])
        copy.start()
        copies.append(copy)
    wait_all(copies)


def expand_near_body(plan, near_count, where, spread, turned, *refs):
    pieces = refs[: 2 * near_count]
    kinds = len({kind for _, kind, _, _ in plan})
    outs = refs[-kinds - len(plan) - 1 : -len(plan) - 1]
    held = refs[-len(plan) - 1 : -1]
    sems = refs[-1]
    copies = []
    for item, (wide, kind, slot, group) in enumerate(plan):
        rows = slice(group * RANK, (group + 1) * RANK)
        order = [0, 1] if not wide else list(range(2, pieces[0].shape[1]))
        column = len(order) * LANES
        for near in range(near_count):
            parts = [
                jnp.concatenate(
                    [pieces[2 * near + core][:, n, rows, :].reshape(-1, LANES) for core in range(2)],
                    axis=0,
                )
                for n in order
            ]
            value = jnp.concatenate(parts, axis=1)
            pair, side = where[0] ^ (near % 2), where[2] ^ (near // 2)
            place = pl.ds(pl.multiple_of((2 * pair + side) * column, column), column)
            if kind % 2 == 0:
                held[item][place, :] = tn(value, spread[...])
            else:
                held[item][:, place] = nn(turned[...], value)
        at = sorted({k for _, k, _, _ in plan}).index(kind)
        copy = pltpu.make_async_copy(held[item], outs[at].at[slot], sems.at[item])
        copy.start()
        copies.append(copy)
    wait_all(copies)


def expand_near(plan, where, spread, turned, pieces, outs):
    kinds = sorted({kind for _, kind, _, _ in plan})
    held = [outs[kind].shape[1:] for _, kind, _, _ in plan]
    passed = [outs[k] for k in kinds]
    start = 3 + len(pieces)

    def body(*refs):
        expand_near_body(plan, len(pieces) // 2, *refs)

    result = pl.pallas_call(
        body,
        name="expand_near",
        in_specs=[SMEM_SPEC] + [VMEM_SPEC] * (2 + len(pieces)) + [ANY_SPEC] * len(passed),
        out_specs=[ANY_SPEC] * len(kinds),
        out_shape=[shape(outs[k].shape, F32) for k in kinds],
        scratch_shapes=[pltpu.VMEM(h, F32) for h in held]
        + [pltpu.SemaphoreType.DMA((len(plan),))],
        input_output_aliases={start + n: n for n in range(len(kinds))},
        compiler_params=pltpu.CompilerParams(vmem_limit_bytes=44 << 20),
        cost_estimate=pl.CostEstimate(flops=0, bytes_accessed=8 << 20, transcendentals=0),
    )(where, spread, turned, *pieces, *passed)
    outs = list(outs)
    for n, k in enumerate(kinds):
        outs[k] = result[n]
    return outs


def rows_of(base, blocks, rows, group, first=0):
    return [base + n * rows + group * RANK for n in range(first, blocks)]


def expand(plan, spread, turned, found, outs):
    kinds = sorted({kind for kind, _, _ in plan})
    fresh = [isinstance(outs[k], jax.ShapeDtypeStruct) for k in kinds]
    held = [shape(outs[kind].shape[1:], F32) for kind, _, _ in plan]
    passed = [outs[k] for k, f in zip(kinds, fresh) if not f]
    aliases = {}
    for n, k in enumerate(kinds):
        if not fresh[n]:
            aliases[3 + len(aliases)] = n

    def body(*refs):
        expand_body(plan, *refs)

    result = pl.pallas_call(
        body,
        name="expand",
        in_specs=[VMEM_SPEC] * 3 + [ANY_SPEC] * len(passed),
        out_specs=[ANY_SPEC] * len(kinds),
        out_shape=[shape(outs[k].shape, F32) for k in kinds],
        scratch_shapes=[pltpu.VMEM(h.shape, F32) for h in held]
        + [pltpu.SemaphoreType.DMA((len(plan),))],
        input_output_aliases=aliases,
        compiler_params=pltpu.CompilerParams(vmem_limit_bytes=44 << 20),
        cost_estimate=pl.CostEstimate(flops=0, bytes_accessed=8 << 20, transcendentals=0),
    )(spread, turned, found, *passed)
    outs = list(outs)
    for n, k in enumerate(kinds):
        outs[k] = result[n]
    return outs


def join(own, other, bit, axis):
    return jnp.where(
        bit == 0,
        jnp.concatenate([own, other], axis=axis),
        jnp.concatenate([other, own], axis=axis),
    )


def part_of(value, index, count, axis):
    size = value.shape[axis] // count
    return lax.dynamic_slice_in_dim(value, index * size, size, axis)


class Place:
    def __init__(self):
        self.side = lax.axis_index("ctx")
        index = lax.axis_index("tp")
        self.pair = index // 2
        self.core = index % 2
        self.block = 2 * self.side + self.pair


def sequence_rows(value, place):
    own = lax.dynamic_index_in_dim(value, place.core, 0, keepdims=False)
    other = lax.dynamic_index_in_dim(value, 1 - place.core, 0, keepdims=False)
    return join(own, by_core(other), place.core, 1)


def own_rows(value, place):
    half = sequence_rows(value, place)
    mine = part_of(half, place.pair, 2, 0)
    theirs = part_of(half, 1 - place.pair, 2, 0)
    return join(mine, by_pair(theirs), place.pair, 1)


def all_rows(value, place):
    half = sequence_rows(value, place)
    full = join(half, by_pair(half), place.pair, 1)
    return part_of(full, place.pair, 2, 0), part_of(full, 1 - place.pair, 2, 0)


def feature_parts(value, place):
    mine = part_of(value, place.pair, 2, 1)
    theirs = part_of(value, 1 - place.pair, 2, 1)
    half = join(mine, by_pair(theirs), place.pair, 0)
    kept = part_of(half, place.core, 2, 1)[None]
    given = part_of(half, 1 - place.core, 2, 1)[None]
    return join(kept, by_core(given), place.core, 0)


def side_half(weight, place):
    return part_of(weight, place.side, 2, weight.ndim - 1)


def gathered(weight):
    return lax.all_gather(weight, "shard", axis=0, tiled=True)


def hidden_pieces(base):
    over = by_side(base)
    return [base, by_core(base), over, by_core(over)]


def whole_pieces(base):
    over = by_side(base)
    found = []
    for near in (base, over):
        far = by_pair(near)
        found += [near, by_core(near), far, by_core(far)]
    return found


def after(value, other):
    return lax.optimization_barrier((value, other))[0]


def line_order():
    count = lax.axis_size("shard")
    index = jnp.arange(count)
    return index if count > 8 else jnp.mod(lax.axis_index("shard") - index, count)


def around_shard(value):
    count = lax.axis_size("shard")
    if count > 8:
        return lax.all_gather(value, "shard", axis=0, tiled=False)
    found = [value]
    for shift in range(1, count):
        route = [(n, (n + shift) % count) for n in range(count)]
        found.append(lax.ppermute(value, "shard", route))
    return jnp.stack(found, axis=0)


def everywhere(value):
    flat = value.astype(BF).reshape(-1, LANES)
    found = lax.all_gather(flat, ("shard", "ctx", "tp"), axis=0, tiled=True)
    return found.reshape((-1, 2, 2, 2) + flat.shape)


def exchanged(slots):
    return [slots[0], by_pair(slots[1]), by_side(slots[2]), across(slots[3])]


def on_device(
    inputs,
    adapter_id,
    cotangent,
    ffn1_in,
    ffn1_out,
    query_w,
    key_w,
    value_w,
    out_w,
    conv_in_w,
    conv_kernel,
    conv_out_w,
    ffn2_in,
    ffn2_out,
    distance_table,
    adapt_down,
    adapt_down_ff,
    adapt_up,
    adapt_up_ff,
):
    place = Place()
    mine = lax.dynamic_index_in_dim(adapter_id, place.core, 0, keepdims=False)
    where = jnp.stack([place.pair, place.core, place.side, mine]).astype(jnp.int32)
    block = place.block.astype(jnp.int32)[None]
    adapters = (adapt_down, adapt_down_ff, adapt_up, adapt_up_ff)

    taps = conv_kernel.shape[0]
    core_kernel = jnp.concatenate([conv_kernel, by_core(conv_kernel)], axis=1)
    kernel = jnp.stack([core_kernel, by_pair(core_kernel)], axis=1).reshape(taps, 4, 2, -1)
    kernel = join(kernel[:, :, :1], kernel[:, :, 1:], place.side, 2)
    kernel = kernel.transpose(0, 2, 1, 3).reshape(taps, -1).astype(F32)

    ids = lax.all_gather(adapter_id, "shard", axis=0, tiled=True)
    eye = jnp.eye(RANK, dtype=BF)

    def spread_of(order):
        chosen = (order[:, None] == jnp.arange(NADAPT, dtype=jnp.int32)[None, :]).astype(BF)
        return (chosen[:, None, :, None] * eye[None, :, None, :]).reshape(-1, NADAPT * RANK)

    index = line_order()
    picked = index[:, None] == jnp.arange(index.shape[0])[None, :]
    near_ids = jnp.sum(jnp.where(picked[:, :, None], ids.reshape(1, -1, 2), 0), axis=1)
    near_ids = join(near_ids[:, :1], near_ids[:, 1:], place.core, 1).T.reshape(-1)
    spread, spread_near = spread_of(ids), spread_of(near_ids)
    turned, turned_near = spread.T, spread_near.T
    text = wide_table(distance_table)

    turning = own_rows(cotangent, place)
    settled = (kernel, text, spread, spread_near, turned, turned_near, turning)
    (kernel, text, spread, spread_near, turned, turned_near, turning) = lax.optimization_barrier(
        settled
    )

    base_in = gathered(side_half(ffn1_in, place))
    own, following = all_rows(inputs, place)
    rows_own, rows_next = start_rows(where, own, following)
    base_out = gathered(after(side_half(ffn1_out, place), (base_in, rows_own, rows_next)))
    in_side, in_core = by_side(base_in), by_core(base_in)
    local = jnp.concatenate(
        [side_half(w, place) for w in (query_w, key_w, value_w, out_w)], axis=1
    )
    base_heads = gathered(after(local, (base_out, in_side, in_core, turning, spread, kernel)))
    out_side, out_core = by_side(base_out), by_core(base_out)
    w1_in = [base_in, in_core, in_side, by_core(in_side)]
    pair_local = side_half(conv_in_w, place)
    local = jnp.concatenate(
        [pair_local[:, 0], pair_local[:, 1], side_half(conv_out_w, place)], axis=1
    )
    step = local.shape[1]
    local = jnp.concatenate([local, jnp.zeros_like(local[:, : step // 3])], axis=1)
    base_convs = gathered(after(local, (base_heads, out_side, out_core, w1_in[3])))
    w1_out = [base_out, out_core, out_side, by_core(out_side)]
    heads_side, heads_pair = by_side(base_heads), by_pair(base_heads)
    heads_core = by_core(base_heads)
    local = jnp.concatenate([side_half(w, place) for w in (ffn2_in, ffn2_out)], axis=1)
    part, send, pre, t_in, t_out = ffn(
        0, 0, 7, where, rows_own, rows_next, w1_in, w1_out, adapters
    )
    kept_one = (rows_own, rows_next, (pre, t_in, t_out))
    base_two = gathered(after(local, (base_convs, heads_side, heads_pair, heads_core, send)))
    other = by_pair(send)
    heads_far = by_side(heads_pair)
    heads = [base_heads, heads_core, heads_pair, by_core(heads_pair)]
    heads += [heads_side, by_core(heads_side), heads_far, by_core(after(heads_far, other))]
    base_convs = base_convs[:, :step]
    convs_pair = by_pair(after(base_convs, heads_pair))
    convs_side = by_side(after(base_convs, heads_far))

    first, slots, t_heads = heads_forward(
        where, own.astype(F32), part, other, heads, adapt_down, adapt_up
    )
    slots = exchanged(slots)
    convs_far = by_pair(after(convs_side, tuple(slots)))
    two_side = by_side(after(base_two, tuple(slots)))
    mixed, logs = attend(block, slots, text)
    convs = [base_convs, convs_pair, convs_side, convs_far]
    convs = [v for piece in convs for v in (piece, by_core(after(piece, mixed)))]
    mixed = exchanged([mixed[n] for n in range(4)])
    second, value, gate, edge, t_mix, t_pair = pair_forward(
        where, first, mixed, heads, convs, adapt_down, adapt_up
    )
    w2 = [base_two, by_core(after(base_two, mixed[0])), two_side, by_core(after(two_side, edge))]
    edge = lax.ppermute(edge, ("ctx", "tp"), NEXT)
    conv, third, rows_own, t_conv = conv_forward(
        taps, where, second, value, gate, edge, kernel, convs, adapt_down, adapt_up
    )
    rows_next = by_pair(rows_own)
    part, send, pre, t_in, t_out = ffn(1, 5, 8, where, rows_own, rows_next, w2, w2, adapters)
    kept_two = (rows_own, rows_next, (pre, t_in, t_out))

    output, grad, half = turn(where, third, part, by_pair(send), turning)
    part, send, sums_two = ffn_back(
        1, 5, 8, where, half, by_pair(half), *kept_two, w2, w2, adapters
    )
    grad, grad_conv, edge, partial = conv_back(
        taps, where, grad, part, by_pair(send), third, conv, t_conv, convs, adapt_down, adapt_up
    )
    came = after(by_side(after(sums_two[1], send)), grad_conv)
    sums_two = sums_two[0] + came
    edge = lax.ppermute(edge, ("ctx", "tp"), BEFORE)
    grad, grad_slots, conv_sums, partial = pair_back(
        taps, where, grad, grad_conv, edge, value, gate, kernel, second, t_pair, t_mix, mixed,
        partial, heads, convs, adapt_down, adapt_up,
    )
    came = after(by_pair(sums_two[2:4]), grad)
    sums_two = jnp.concatenate([sums_two[:2] + came, sums_two[4:]], axis=0)
    found_two = everywhere(sums_two)
    grad_slots = exchanged(grad_slots)
    back = attend_back(block, slots, grad_slots, text, logs)
    output = feature_parts(output, place)
    back = exchanged([back[n] for n in range(4)])
    grad, half, head_sums = heads_back(
        after(where, output), grad, first, t_heads, back, partial, conv_sums, heads,
        adapt_down, adapt_up,
    )
    other_half = by_pair(half)
    head_sums = head_sums[0] + by_side(head_sums[1].astype(BF)).astype(F32)
    head_sums = head_sums[0] + by_pair(head_sums[1].astype(BF)).astype(F32)
    found_heads = everywhere(after(head_sums, other_half))
    part, send, sums_one = ffn_back(
        0, 0, 7, where, half, other_half, *kept_one, w1_in, w1_out, adapters
    )
    sums_one = sums_one[0] + by_side(sums_one[1].astype(BF)).astype(F32)
    sums_one = jnp.concatenate([sums_one[:2] + by_pair(sums_one[2:4]), sums_one[4:]], axis=0)
    line = around_shard(sums_one.astype(BF))
    pieces = [line, by_pair(line), by_side(line)]
    pieces.append(by_pair(pieces[2]))
    pieces = [v for piece in pieces for v in (piece, by_core(piece))]
    input_grad = finish(where, grad, part, by_pair(send), own)
    input_grad = feature_parts(input_grad, place).astype(F32)

    outs = [shape(v.shape, F32) for v in (adapt_down, adapt_up, adapt_down_ff, adapt_up_ff)]
    ffn_blocks, ffn_rows = sums_two.shape[:2]
    plan = [(kind, slot, rows_of(0, 2, ffn_rows, g)) for kind, slot, g in ((0, 5, 0), (1, 8, 1))]
    plan += [
        (kind, 1, rows_of(0, ffn_blocks, ffn_rows, g, 2)) for kind, g in ((2, 0), (3, 1))
    ]
    outs = expand(plan, spread, turned, after(found_two, send), outs)
    head_blocks, head_rows = head_sums.shape[:2]
    places = ((0, 1), (0, 2), (0, 3), (1, 5), (1, 0), (1, 1), (1, 2), (0, 6))
    places += ((0, 4), (1, 6), (0, 7), (1, 3), (1, 4))
    plan = [
        (kind, slot, rows_of(0, head_blocks, head_rows, g))
        for g, (kind, slot) in enumerate(places)
    ]
    outs = expand(plan, spread, turned, found_heads, outs)
    outs = expand_near(
        [(False, 0, 0, 0), (False, 1, 7, 1), (True, 2, 0, 0), (True, 3, 0, 1)],
        where, spread_near, turned_near, pieces, outs,
    )
    return (output, input_grad, outs[0], outs[2], outs[1], outs[3])


def solution(mesh):
    placed = (
        P("shard", "ctx", "tp"),
        P("shard"),
        P("shard", "ctx", "tp"),
        P("shard", "tp"),
        P("shard", "tp"),
        P("shard", "tp"),
        P("shard", "tp"),
        P("shard", "tp"),
        P("shard", "tp"),
        P("shard", None, "tp"),
        P(None, "tp"),
        P("shard", "tp"),
        P("shard", "tp"),
        P("shard", "tp"),
        P(),
        P(),
        P(),
        P(),
        P(),
    )
    return jax.shard_map(
        on_device,
        mesh=mesh,
        in_specs=placed,
        out_specs=(P("shard", "ctx", "tp"), P("shard", "ctx", "tp"), P(), P(), P(), P()),
        check_vma=False,
    )
```

```python
import jax
import jax.numpy as jnp
from jax import lax
from jax.experimental import pallas as pl
from jax.experimental.pallas import tpu as pltpu
from jax.sharding import PartitionSpec as P

LEFT = 64
RIGHT = 8
NADAPT = 8
RANK = 16
HEAD = 64
LANES = 128
eps = 1e-05
BF = jnp.bfloat16
F32 = jnp.float32

CORE = [(0, 1), (1, 0), (2, 3), (3, 2)]
PAIR = [(0, 2), (2, 0), (1, 3), (3, 1)]
SIDE = [(0, 1), (1, 0)]
ACROSS = [(s * 4 + t, (1 - s) * 4 + (t ^ 2)) for s in range(2) for t in range(4)]


def block_at(block, core):
    return (block // 2) * 4 + (block % 2) * 2 + core


NEXT = [(block_at(n, k), block_at(n + 1, k)) for n in range(3) for k in range(2)]
BEFORE = [(block_at(n + 1, k), block_at(n, k)) for n in range(3) for k in range(2)]


def by_core(value):
    return lax.ppermute(value, "tp", CORE)


def by_pair(value):
    return lax.ppermute(value, "tp", PAIR)


def by_side(value):
    return lax.ppermute(value, "ctx", SIDE)


def across(value):
    return lax.ppermute(value, ("ctx", "tp"), ACROSS)


def wide_table(table):
    place = jnp.arange(4*LANES, dtype=jnp.int32)
    index = jnp.where(place < 3*LANES, jnp.clip(place - LEFT, 0, LEFT+RIGHT), 0)
    pick = (index[:, None] == jnp.arange(table.shape[0], dtype=jnp.int32)[None, :]).astype(BF)
    rows = jnp.dot(pick, table, preferred_element_type=F32).astype(BF)
    return jnp.concatenate([rows, rows], axis=1)

def load_blocks(b_ref, sources, target, sems, parts):
    copies=[]
    for j, source in enumerate(sources):
        rows = source.shape[0]; cols = source.shape[1]//parts
        for part in range(parts):
            copies.append(pltpu.make_async_copy(
                source.at[:, part*cols:(part+1)*cols],
                target.at[part, pl.ds(pl.multiple_of((b_ref[0] ^ j)*rows, rows), rows), :],
                sems.at[j*parts+part]))
    for c in copies: c.start()
    for c in copies: c.wait()

def window(r0, length):
    lo=max(r0-LANES,0); hi=min(r0+2*LANES,length)
    return lo,hi

def biased(s, near, p, rows, length):
    parts=[]
    for sub in range(rows//LANES):
        r0=p*rows+sub*LANES
        e=near[sub*LANES:(sub+1)*LANES]
        band=pltpu.roll(e, 0, 1, stride=1, stride_axis=0)
        lo,hi=window(r0,length)
        pieces=[]
        if lo>0: pieces.append(jnp.broadcast_to(e[:,0:1],(LANES,lo)))
        pieces.append(band[:, lo-r0+LANES:hi-r0+LANES])
        if hi<length: pieces.append(jnp.broadcast_to(e[:,2*LANES-1:2*LANES],(LANES,length-hi)))
        parts.append(jnp.concatenate(pieces,axis=1))
    return s+jnp.concatenate(parts,axis=0)


def fwd_kernel(b_ref, s0,s1,s2,s3, text_ref, o_ref, lse_ref, qkv, sems):
    dc=pl.program_id(0); k=pl.program_id(1)
    @pl.when((dc==0)&(k==0))
    def _(): load_blocks(b_ref,(s0,s1,s2,s3),qkv,sems,2)
    rows=o_ref.shape[1]; length=qkv.shape[1]
    own=(lax.broadcasted_iota(jnp.int32,(rows,LANES),1)//64)==k
    key=qkv[dc,:,LANES:2*LANES]; val=qkv[dc,:,2*LANES:]
    for p in range(length//rows):
        q=qkv[dc,p*rows:(p+1)*rows,0:LANES].astype(F32)*0.125
        q=jnp.where(own,q,0.0).astype(BF)
        s=biased(nt(q,key),nt(q,text_ref[...]),p,rows,length)
        top=jnp.max(s,axis=-1,keepdims=True)
        e=jnp.exp(s-top)
        tot=jnp.sum(e,axis=-1,keepdims=True)
        o=jnp.dot(e.astype(BF),val,preferred_element_type=F32)/tot
        o=o.astype(BF)
        slot=p^b_ref[0]
        @pl.when(k==0)
        def _(): o_ref[slot]=o
        @pl.when(k==1)
        def _(): o_ref[slot]=jnp.where(own,o,o_ref[slot])
        lse_ref[0,p*rows:(p+1)*rows,:]=top+jnp.log(tot)

def attend(b, slots, text):
    rows=slots[0].shape[0]; n=len(slots); length=rows*n
    anys=[pl.BlockSpec(memory_space=pl.ANY)]*n
    return pl.pallas_call(
        fwd_kernel,
        grid_spec=pltpu.PrefetchScalarGridSpec(
            num_scalar_prefetch=1, grid=(2,2),
            in_specs=anys+[pl.BlockSpec(text.shape,lambda d,k,b:(0,0))],
            out_specs=(pl.BlockSpec((n,rows,LANES),lambda d,k,b:(0,0,d)),
                       pl.BlockSpec((1,length,1),lambda d,k,b:(2*d+k,0,0))),
            scratch_shapes=[pltpu.VMEM((2,length,3*LANES),BF),pltpu.SemaphoreType.DMA((2*n,))]),
        out_shape=(jax.ShapeDtypeStruct((n,rows,2*LANES),BF),jax.ShapeDtypeStruct((4,length,1),F32)),
        compiler_params=pltpu.CompilerParams(vmem_limit_bytes=48<<20),
        name="attend",
        cost_estimate=pl.CostEstimate(flops=4*4*length*length*64,bytes_accessed=length*8*LANES*2,transcendentals=4*length*length),
    )(b,*slots,text)

def bwd_kernel(b_ref, s0,s1,s2,s3, g0,g1,g2,g3, text_ref, lse_ref, out_ref, qkv, gout, dq_acc, dk_acc, dv_acc, sems, gsems):
    dc=pl.program_id(0); k=pl.program_id(1)
    @pl.when((dc==0)&(k==0))
    def _():
        load_blocks(b_ref,(s0,s1,s2,s3),qkv,sems,2)
        load_blocks(b_ref,(g0,g1,g2,g3),gout,gsems,2)
    rows=out_ref.shape[1]; length=qkv.shape[1]
    own=(lax.broadcasted_iota(jnp.int32,(rows,LANES),1)//64)==k
    key=qkv[dc,:,LANES:2*LANES]; val=qkv[dc,:,2*LANES:]
    text=text_ref[...]
    turn=((lax.broadcasted_iota(jnp.int32,(LANES,LANES),0)+lax.broadcasted_iota(jnp.int32,(LANES,LANES),1))==LANES-1).astype(BF)
    @pl.when(k==0)
    def _():
        dk_acc[...]=jnp.zeros_like(dk_acc); dv_acc[...]=jnp.zeros_like(dv_acc)
    for p in range(length//rows):
        span=slice(p*rows,(p+1)*rows)
        q=qkv[dc,span,0:LANES].astype(F32)*0.125
        q=jnp.where(own,q,0.0).astype(BF)
        g=jnp.where(own,gout[dc,span,:].astype(F32),0.0).astype(BF)
        s=biased(nt(q,key),nt(q,text),p,rows,length)
        pr=jnp.exp(s-lse_ref[0,span,:])
        dp=nt(g,val)
        w=pr*dp
        ds=(w-pr*jnp.sum(w,axis=-1,keepdims=True)).astype(BF)
        dv_acc[...]+=tn(g,pr.astype(BF))
        dk_acc[...]+=tn(q,ds)
        dq=jnp.dot(ds,key,preferred_element_type=F32)
        extra=[]
        t_lo=text[0:1,:].astype(F32); t_hi=text[2*LANES-1:2*LANES,:].astype(F32)
        for sub in range(rows//LANES):
            r0=p*rows+sub*LANES
            lo,hi=window(r0,length)
            d=ds[sub*LANES:(sub+1)*LANES].astype(F32)
            pieces=[]
            if lo-r0+LANES>0: pieces.append(jnp.zeros((LANES,lo-r0+LANES),F32))
            pieces.append(d[:,lo:hi])
            pieces.append(jnp.zeros((LANES,4*LANES-(hi-r0+LANES)),F32))
            w=jnp.concatenate(pieces,axis=1)
            w=jnp.dot(turn,w.astype(BF),preferred_element_type=F32)
            w=pltpu.roll(w,3*LANES+1,1,stride=1,stride_axis=0)
            w=jnp.dot(turn,w.astype(BF),preferred_element_type=F32)
            x=jnp.dot(w.astype(BF),text,preferred_element_type=F32)
            if lo>0: x+=jnp.sum(d[:,:lo],axis=-1,keepdims=True)*t_lo
            if hi<length: x+=jnp.sum(d[:,hi:],axis=-1,keepdims=True)*t_hi
            extra.append(x)
        dq=(dq+jnp.concatenate(extra,axis=0))*0.125
        dq_acc[span,:]=jnp.where(own,dq,dq_acc[span,:])
    @pl.when(k==1)
    def _():
        for p in range(length//rows):
            slot=p^b_ref[0]; span=slice(p*rows,(p+1)*rows)
            out_ref[slot,:,0:LANES]=dq_acc[span,:].astype(BF)
            out_ref[slot,:,LANES:2*LANES]=dk_acc[:,span].T.astype(BF)
            out_ref[slot,:,2*LANES:]=dv_acc[:,span].T.astype(BF)

def attend_back(b, slots, grads, text, lse):
    rows=slots[0].shape[0]; n=len(slots); length=rows*n
    anys=[pl.BlockSpec(memory_space=pl.ANY)]*(2*n)
    return pl.pallas_call(
        bwd_kernel,
        grid_spec=pltpu.PrefetchScalarGridSpec(
            num_scalar_prefetch=1, grid=(2,2),
            in_specs=anys+[pl.BlockSpec(text.shape,lambda d,k,b:(0,0)),pl.BlockSpec((1,length,1),lambda d,k,b:(2*d+k,0,0))],
            out_specs=pl.BlockSpec((n,rows,3*LANES),lambda d,k,b:(0,0,d)),
            scratch_shapes=[pltpu.VMEM((2,length,3*LANES),BF),pltpu.VMEM((2,length,LANES),BF),
              pltpu.VMEM((length,LANES),F32),pltpu.VMEM((LANES,length),F32),pltpu.VMEM((LANES,length),F32),
              pltpu.SemaphoreType.DMA((2*n,)),pltpu.SemaphoreType.DMA((2*n,))]),
        out_shape=jax.ShapeDtypeStruct((n,rows,6*LANES),BF),
        compiler_params=pltpu.CompilerParams(vmem_limit_bytes=30<<20),
        name="attend_back",
        cost_estimate=pl.CostEstimate(flops=10*4*length*length*64,bytes_accessed=length*14*LANES*2,transcendentals=4*length*length),
    )(b,*slots,*grads,text,lse)


def nn(first, second):
    return jnp.dot(first, second, preferred_element_type=F32)


def nt(first, second):
    return lax.dot_general(first, second, (((1,), (1,)), ((), ())), preferred_element_type=F32)


def tn(first, second):
    return lax.dot_general(first, second, (((0,), (0,)), ((), ())), preferred_element_type=F32)


def normalize(value):
    mean = jnp.mean(value, axis=-1, keepdims=True)
    square = jnp.mean(value * value, axis=-1, keepdims=True)
    scale = lax.rsqrt(square - mean * mean + eps)
    return ((value - mean) * scale, scale)


def normalize_back(grad, normed, scale):
    mean = jnp.mean(grad, axis=-1, keepdims=True)
    cross = jnp.mean(grad * normed, axis=-1, keepdims=True)
    return scale * (grad - mean - normed * cross)


def swish_slope(value, sigma):
    return sigma + value * sigma * (1.0 - sigma)


def mask_row(adapter):
    lanes = lax.broadcasted_iota(jnp.int32, (1, NADAPT * RANK), 1)
    return (lanes // RANK == adapter).astype(F32)


def chosen_rows(adapter):
    shape = (RANK, NADAPT * RANK)
    lanes = lax.broadcasted_iota(jnp.int32, shape, 1)
    rows = lax.broadcasted_iota(jnp.int32, shape, 0)
    return (lanes == rows + adapter * RANK).astype(BF)


def compact(pick, value):
    return nt(pick, value).astype(BF)


class Fetches:
    def __init__(self, sems):
        self.sems = sems
        self.used = 0

    def __call__(self, source, target):
        copy = pltpu.make_async_copy(source, target, self.sems.at[self.used])
        self.used += 1
        copy.start()
        return copy


def wait_all(copies):
    for copy in copies:
        copy.wait()


def block_of(where, number):
    side, pair, core = number // 4, (number // 2) % 2, number % 2
    return ((where[0] ^ pair) * 2 + (where[1] ^ core)) * 2 + (where[2] ^ side)


def fetch_columns(fetch, where, source, target):
    found = []
    for number in range(8):
        start = pl.multiple_of(block_of(where, number) * LANES, LANES)
        place = pl.ds(number * LANES, LANES)
        found.append(fetch(source.at[:, pl.ds(start, LANES)], target.at[:, place]))
    return found


def fetch_rows(fetch, where, source, target):
    found = []
    for number in range(8):
        start = pl.multiple_of(block_of(where, number) * LANES, LANES)
        place = pl.ds(number * LANES, LANES)
        found.append(fetch(source.at[pl.ds(start, LANES), :], target.at[place, :]))
    return found


def store_absolute(where, out, first, value):
    rows = value.shape[0]
    for number in range(8):
        pair, side, half = number // 4, (number // 2) % 2, number % 2
        out[side ^ where[2], pair ^ where[0], half, first : first + rows, :] = value[
            :, number * LANES : (number + 1) * LANES
        ]


def store_relative(where, out, first, value, number):
    side, pair, core = number // 4, (number // 2) % 2, number % 2
    out[(where[1] ^ core) ^ where[2], pair, where[2] ^ side, first : first + value.shape[0], :] = value


def store_edge(out, value, flip_side):
    rows = value.shape[0]
    width = value.shape[1] // 4
    for side in range(2):
        for pair in range(2):
            start = (2 * side + pair) * width
            out[side ^ flip_side, 1 - pair] = value[:, start : start + width]


def read_edge(edge):
    return jnp.concatenate([edge[s, p] for s in range(2) for p in range(2)], axis=1)


VMEM_SPEC = pl.BlockSpec(memory_space=pltpu.VMEM)
ANY_SPEC = pl.BlockSpec(memory_space=pltpu.HBM)
SMEM_SPEC = pl.BlockSpec(memory_space=pltpu.SMEM)


def run(body, name, places, outs, scratch, operands, flops=0, room=44, out_specs=None):
    specs = [SMEM_SPEC] + [VMEM_SPEC if p == "v" else ANY_SPEC for p in places]
    moved = sum(o.size * o.dtype.itemsize for o in list(operands[1:]) + list(outs))
    return pl.pallas_call(
        body,
        name=name,
        in_specs=specs,
        out_specs=out_specs or [VMEM_SPEC] * len(outs),
        out_shape=outs,
        scratch_shapes=scratch,
        compiler_params=pltpu.CompilerParams(vmem_limit_bytes=room << 20),
        cost_estimate=pl.CostEstimate(
            flops=flops, bytes_accessed=min(moved, 16 << 20), transcendentals=0
        ),
    )(*operands)


def shape(dims, dtype):
    return jax.ShapeDtypeStruct(dims, dtype)


def fetch_ffn_adapters(fetch, where, which, column, up_ff, down_ff, p_in, q_in, p_out):
    found = []
    for number in range(4):
        side, core = number // 2, number % 2
        start = (2 * where[0] + (where[1] ^ core)) * (2 * column) + (where[2] ^ side) * column
        start = pl.multiple_of(start, column)
        place = pl.ds(number * column, column)
        found.append(fetch(up_ff.at[which, :, pl.ds(start, column)], q_in.at[:, place]))
        found.append(fetch(down_ff.at[which, pl.ds(start, column), :], p_out.at[place, :]))
    return found


def ffn_body(which, down_at, up_at, column, where, own, following, *refs):
    ins, outs, ups = refs[:4], refs[4:8], refs[8:12]
    down, down_ff, up, up_ff = ups
    part, send, pre_out, t_in_out, t_out_out = refs[12:17]
    rows, w_in, w_out, p_in, q_in, p_out, q_out, pre, active, sems = refs[17:]
    fetch = Fetches(sems)
    count = own.shape[0]
    small = [fetch(down.at[down_at], p_in), fetch(up.at[up_at], q_out)]
    small += fetch_ffn_adapters(fetch, where, which, column, up_ff, down_ff, p_in, q_in, p_out)
    first = [
        fetch(r.at[:, pl.ds(0, column)], w_in.at[:, pl.ds(n * column, column)])
        for n, r in enumerate(ins)
    ]
    second = [
        fetch(r.at[:, pl.ds(r.shape[1] - column, column)], w_out.at[:, pl.ds(n * column, column)])
        for n, r in enumerate(outs)
    ]
    mask = mask_row(where[3])
    rows[:count] = own[...]
    rows[count:] = following[...]
    wait_all(small)
    t_in = (nn(rows[...], p_in[...]) * mask).astype(BF)
    t_in_out[...] = t_in
    t_out = jnp.zeros(t_in.shape, F32)
    saved = []
    for n in range(4):
        span = slice(n * column, (n + 1) * column)
        first[n].wait()
        value = nn(rows[...], w_in[:, span]) + nn(t_in, q_in[:, span])
        pre[n] = value
        saved.append(fetch(pre.at[n], pre_out.at[n]))
        act = (value * jax.nn.sigmoid(value)).astype(BF)
        active[:, span] = act
        t_out = t_out + nn(act, p_out[span, :])
    t_out = (t_out * mask).astype(BF)
    t_out_out[...] = t_out
    wait_all(second)
    width = w_out.shape[0] // 2
    for n in range(2):
        span = slice(n * width, (n + 1) * width)
        total = nt(active[...], w_out[span, :]) + nn(t_out, q_out[:, span])
        part[:, span] = total[:count]
        send[:, span] = total[count:].astype(BF)
    wait_all(saved)


def ffn(which, down_at, up_at, where, own, following, w_in, w_out, adapters):
    count, width = own.shape
    column = adapters[3].shape[2] // 8
    hidden = 4 * column
    ranks = NADAPT * RANK

    def body(*refs):
        ffn_body(which, down_at, up_at, column, *refs)

    return run(
        body,
        "hidden_forward",
        "vv" + "a" * 12,
        [
            shape((count, width), F32),
            shape((count, width), BF),
            shape((4, 2 * count, column), F32),
            shape((2 * count, ranks), BF),
            shape((2 * count, ranks), BF),
        ],
        [
            pltpu.VMEM((2 * count, width), BF),
            pltpu.VMEM((width, hidden), BF),
            pltpu.VMEM((width, hidden), BF),
            pltpu.VMEM((width, ranks), BF),
            pltpu.VMEM((ranks, hidden), BF),
            pltpu.VMEM((hidden, ranks), BF),
            pltpu.VMEM((ranks, width), BF),
            pltpu.VMEM((4, 2 * count, column), F32),
            pltpu.VMEM((2 * count, hidden), BF),
            pltpu.SemaphoreType.DMA((22,)),
        ],
        [where, own, following, *w_in, *w_out, *adapters],
        flops=8 * count * width * hidden,
        out_specs=[VMEM_SPEC, VMEM_SPEC, ANY_SPEC, VMEM_SPEC, VMEM_SPEC],
    )


def ffn_back_body(which, down_at, up_at, column, where, own, following, u_own, u_next, t_in, t_out, *refs):
    pre_in = refs[0]
    ins, outs, ups = refs[1:5], refs[5:9], refs[9:13]
    down, down_ff, up, up_ff = ups
    part, send, grads = refs[13:16]
    full, rows, w_in, w_out, p_in, q_in, p_out, q_out, pre, active, slope, sems = refs[16:]
    fetch = Fetches(sems)
    count = own.shape[0]
    small = [fetch(down.at[down_at], p_in), fetch(up.at[up_at], q_out)]
    small += fetch_ffn_adapters(fetch, where, which, column, up_ff, down_ff, p_in, q_in, p_out)
    second = []
    kept = []
    for n, r in enumerate(outs):
        source = r.at[:, pl.ds(r.shape[1] - column, column)]
        second.append(fetch(source, w_out.at[:, pl.ds(n * column, column)]))
        kept.append(fetch(pre_in.at[n], pre.at[n]))
    first = [
        fetch(r.at[:, pl.ds(0, column)], w_in.at[:, pl.ds(n * column, column)])
        for n, r in enumerate(ins)
    ]
    mask = mask_row(where[3])
    pick = chosen_rows(where[3])
    full[:count] = own[...]
    full[count:] = following[...]
    rows[:count] = u_own[...]
    rows[count:] = u_next[...]
    wait_all(small)
    r_out = (nt(full[...], q_out[...]) * mask).astype(BF)
    c_out = compact(pick, r_out)
    c_t_in = compact(pick, t_in[...])
    r_in = jnp.zeros(r_out.shape, F32)
    for n in range(4):
        span = slice(n * column, (n + 1) * column)
        second[n].wait()
        kept[n].wait()
        grad = nn(full[...], w_out[:, span]) + nt(r_out, p_out[span, :])
        value = pre[n]
        sigma = jax.nn.sigmoid(value)
        act = (value * sigma).astype(BF)
        grad = (grad * swish_slope(value, sigma)).astype(BF)
        slope[:, span] = grad
        r_in = r_in + nt(grad, q_in[:, span])
        side, core = n // 2, n % 2
        near = (where[1] ^ core) ^ where[2]
        far = where[2] ^ side
        both = jnp.concatenate([nn(c_out, act), nn(c_t_in, grad)], axis=0)
        for piece in range(column // LANES):
            grads[near, 4 + far * (column // LANES) + piece] = both[
                :, piece * LANES : (piece + 1) * LANES
            ]
    r_in = (r_in * mask).astype(BF)
    wait_all(first)
    width = w_in.shape[0] // 2
    for n in range(2):
        span = slice(n * width, (n + 1) * width)
        total = nt(slope[...], w_in[span, :]) + nt(r_in, p_in[span, :])
        part[:, span] = total[:count]
        send[:, span] = total[count:].astype(BF)
    narrow = jnp.concatenate(
        [nn(compact(pick, r_in), rows[...]), nn(compact(pick, t_out[...]), full[...])], axis=0
    )
    for number in range(8):
        pair, side, half = number // 4, (number // 2) % 2, number % 2
        grads[side ^ where[2], 2 * (pair ^ where[0]) + half] = narrow[
            :, number * LANES : (number + 1) * LANES
        ]


def ffn_back(which, down_at, up_at, where, own, following, u_own, u_next, kept, w_in, w_out, adapters):
    pre, t_in, t_out = kept
    count, width = own.shape
    column = adapters[3].shape[2] // 8
    hidden = 4 * column
    ranks = NADAPT * RANK

    def body(*refs):
        ffn_back_body(which, down_at, up_at, column, *refs)

    return run(
        body,
        "hidden_backward",
        "vvvvvv" + "a" * 13,
        [
            shape((count, width), F32),
            shape((count, width), BF),
            shape((2, 4 + 2 * column // LANES, 2 * RANK, LANES), F32),
        ],
        [
            pltpu.VMEM((2 * count, width), BF),
            pltpu.VMEM((2 * count, width), BF),
            pltpu.VMEM((width, hidden), BF),
            pltpu.VMEM((width, hidden), BF),
            pltpu.VMEM((width, ranks), BF),
            pltpu.VMEM((ranks, hidden), BF),
            pltpu.VMEM((hidden, ranks), BF),
            pltpu.VMEM((ranks, width), BF),
            pltpu.VMEM((4, 2 * count, column), F32),
            pltpu.VMEM((2 * count, hidden), BF),
            pltpu.VMEM((2 * count, hidden), BF),
            pltpu.SemaphoreType.DMA((22,)),
        ],
        [where, own, following, u_own, u_next, t_in, t_out, pre, *w_in, *w_out, *adapters],
        flops=8 * count * width * hidden,
    )


def fetch_heads(fetch, where, pieces, up, wide):
    width = pieces[0].shape[0]
    three = 3 * LANES
    found = []
    for number, piece in enumerate(pieces):
        slot, core = number // 2, number % 2
        found.append(
            fetch(
                piece.at[:, pl.ds(0, three)],
                wide.at[slot, pl.ds(0, width), pl.ds(core * three, three)],
            )
        )
        start = pl.multiple_of(block_of(where, number) * LANES, LANES)
        for kind in range(3):
            found.append(
                fetch(
                    up.at[kind, :, pl.ds(start, LANES)],
                    wide.at[
                        slot,
                        pl.ds(width + kind * LANES, LANES),
                        pl.ds(core * three + kind * LANES, LANES),
                    ],
                )
            )
    return found


def clear_heads(wide, width):
    for kind in range(3):
        span = slice(width + kind * LANES, width + (kind + 1) * LANES)
        for core in range(2):
            for other in range(3):
                if other != kind:
                    at = (core * 3 + other) * LANES
                    for slot in range(4):
                        wide[slot, span, at : at + LANES] = jnp.zeros((LANES, LANES), BF)


def heads_body(where, resid, part, other, *refs):
    pieces = refs[:8]
    down, up = refs[8:10]
    first = refs[10]
    slots = refs[11:15]
    t_out = refs[15]
    wide, thin, sems = refs[16:]
    width = resid.shape[1]
    fetch = Fetches(sems)
    small = [
        fetch(down.at[1 + kind], thin.at[:, pl.ds(kind * LANES, LANES)]) for kind in range(3)
    ]
    large = fetch_heads(fetch, where, pieces, up, wide)
    clear_heads(wide, width)
    value = resid[...] + 0.5 * (part[...] + other[...].astype(F32))
    first[...] = value
    rows = normalize(value)[0].astype(BF)
    mask = jnp.concatenate([mask_row(where[3])] * 3, axis=1)
    wait_all(small)
    reduced = (nn(rows, thin[...]) * mask).astype(BF)
    t_out[...] = reduced
    both = jnp.concatenate([rows, reduced], axis=1)
    for slot in range(4):
        wait_all(large[slot * 8 : slot * 8 + 8])
        slots[slot][...] = nn(both, wide[slot]).astype(BF)


def heads_forward(where, resid, part, other, pieces, down, up):
    count, width = resid.shape
    three = 3 * LANES
    found = run(
        heads_body,
        "heads_forward",
        "vvv" + "a" * 10,
        [shape((count, width), F32)]
        + [shape((count, 2 * three), BF)] * 4
        + [shape((count, three), BF)],
        [
            pltpu.VMEM((4, width + three, 2 * three), BF),
            pltpu.VMEM((width, three), BF),
            pltpu.SemaphoreType.DMA((35,)),
        ],
        [where, resid, part, other, *pieces, down, up],
        flops=2 * count * width * 3 * width,
    )
    return (found[0], found[1:5], found[5])


def heads_back_body(where, grad, first, t_in, g0, g1, g2, g3, partial, convs, *refs):
    pieces = refs[:8]
    down, up = refs[8:10]
    result, half, grads = refs[10:13]
    wide, thin, sems = refs[13:]
    width = grad.shape[1]
    three = 3 * LANES
    fetch = Fetches(sems)
    small = [
        fetch(down.at[1 + kind], thin.at[:, pl.ds(kind * LANES, LANES)]) for kind in range(3)
    ]
    large = fetch_heads(fetch, where, pieces, up, wide)
    clear_heads(wide, width)
    normed, scale = normalize(first[...])
    rows = normed.astype(BF)
    pick = chosen_rows(where[3])
    mask = jnp.concatenate([mask_row(where[3])] * 3, axis=1)
    ranks = [compact(pick, t_in[:, k * LANES : (k + 1) * LANES]) for k in range(3)]
    total = None
    for slot, g in enumerate((g0, g1, g2, g3)):
        wait_all(large[slot * 8 : slot * 8 + 8])
        term = nt(g[...], wide[slot])
        total = term if total is None else total + term
        for core in range(2):
            for kind in range(3):
                at = core * three + kind * LANES
                store_relative(
                    where, grads, (4 + kind) * RANK, nn(ranks[kind], g[:, at : at + LANES]),
                    2 * slot + core,
                )
    reduced = (total[:, width:] * mask).astype(BF)
    wait_all(small)
    total = total[:, :width] + nt(reduced, thin[...])
    value = grad[...] + normalize_back(total, normed, scale)
    result[...] = value
    half[...] = (0.5 * value).astype(BF)
    for kind in range(3):
        found = nn(compact(pick, reduced[:, kind * LANES : (kind + 1) * LANES]), rows)
        store_absolute(where, grads, kind * RANK, found)
    for side in range(2):
        for pair in range(2):
            for piece in range(2):
                grads[side, pair, piece, 3 * RANK : 4 * RANK, :] = partial[
                    side, pair, piece, :RANK, :
                ]
                grads[side, pair, piece, 7 * RANK : 8 * RANK, :] = partial[
                    side, pair, piece, RANK:, :
                ]
                grads[side, pair, piece, 8 * RANK :, :] = convs[side, pair, piece]


def heads_back(where, grad, first, t_in, slots, partial, convs, pieces, down, up):
    count, width = grad.shape
    three = 3 * LANES
    return run(
        heads_back_body,
        "heads_backward",
        "v" * 9 + "a" * 10,
        [
            shape((count, width), F32),
            shape((count, width), BF),
            shape((2, 2, 2, 13 * RANK, LANES), F32),
        ],
        [
            pltpu.VMEM((4, width + three, 2 * three), BF),
            pltpu.VMEM((width, three), BF),
            pltpu.SemaphoreType.DMA((35,)),
        ],
        [where, grad, first, t_in, *slots, partial, convs, *pieces, down, up],
        flops=2 * count * width * 3 * width,
    )


def fetch_piece_columns(fetch, pieces, at, target):
    found = []
    for number, piece in enumerate(pieces):
        found.append(
            fetch(piece.at[:, pl.ds(at, LANES)], target.at[:, pl.ds(number * LANES, LANES)])
        )
    return found


def pair_body(where, first, m0, m1, m2, m3, *refs):
    heads, convs = refs[:8], refs[8:16]
    down, up = refs[16:18]
    second, value_out, gate_out, edge, t_mix_out, t_pair_out = refs[18:24]
    w_mix, w_value, w_gate, p_mix, q_mix, p_pair, q_value, q_gate, sems = refs[24:]
    fetch = Fetches(sems)
    mixing = fetch_rows(fetch, where, down.at[6], p_mix) + [fetch(up.at[5], q_mix)]
    mixing += fetch_piece_columns(fetch, heads, 3 * LANES, w_mix)
    pairs = [fetch(down.at[4], p_pair)]
    pairs += fetch_columns(fetch, where, up.at[3], q_value)
    pairs += fetch_columns(fetch, where, up.at[4], q_gate)
    pairs += fetch_piece_columns(fetch, convs, 0, w_value)
    gates = fetch_piece_columns(fetch, convs, LANES, w_gate)
    mask = mask_row(where[3])
    mixed = jnp.concatenate([m0[...], m1[...], m2[...], m3[...]], axis=1)
    wait_all(mixing)
    t_mix = (nn(mixed, p_mix[...]) * mask).astype(BF)
    t_mix_out[...] = t_mix
    value = first[...] + nt(mixed, w_mix[...]) + nn(t_mix, q_mix[...])
    second[...] = value
    rows = normalize(value)[0].astype(BF)
    wait_all(pairs)
    t_pair = (nn(rows, p_pair[...]) * mask).astype(BF)
    t_pair_out[...] = t_pair
    value = nn(rows, w_value[...]) + nn(t_pair, q_value[...])
    value_out[...] = value
    wait_all(gates)
    gate = nn(rows, w_gate[...]) + nn(t_pair, q_gate[...])
    gate_out[...] = gate
    last = value.shape[0] - edge.shape[2]
    store_edge(edge, value[last:] * jax.nn.sigmoid(gate[last:]), where[0])


def pair_forward(where, first, mixed, heads, convs, down, up):
    count, width = first.shape
    ranks = NADAPT * RANK
    square = pltpu.VMEM((width, width), BF)
    return run(
        pair_body,
        "pair_forward",
        "v" * 5 + "a" * 18,
        [
            shape((count, width), F32),
            shape((count, width), F32),
            shape((count, width), F32),
            shape((2, 2, 32, width // 4), F32),
            shape((count, ranks), BF),
            shape((count, ranks), BF),
        ],
        [
            square,
            square,
            square,
            pltpu.VMEM((width, ranks), BF),
            pltpu.VMEM((ranks, width), BF),
            pltpu.VMEM((width, ranks), BF),
            pltpu.VMEM((ranks, width), BF),
            pltpu.VMEM((ranks, width), BF),
            pltpu.SemaphoreType.DMA((50,)),
        ],
        [where, first, *mixed, *heads, *convs, down, up],
        flops=6 * count * width * width,
    )


def tap_sums(padded, taps, kernel, count, starts):
    found = []
    for number in range(padded.shape[0]):
        span = slice(number * LANES, (number + 1) * LANES)
        total = None
        for tap in range(taps):
            term = kernel[tap : tap + 1, span] * padded[number, starts[tap] : starts[tap] + count, :]
            total = term if total is None else total + term
        found.append(total)
    return jnp.concatenate(found, axis=1)


def conv_body(taps, where, second, value, gate, edge, kernel, *refs):
    convs = refs[:8]
    down, up = refs[8:10]
    conv_out, third, rows_out, t_out = refs[10:14]
    w_out, p_out, q_out, padded, sems = refs[14:]
    fetch = Fetches(sems)
    small = fetch_rows(fetch, where, down.at[7], p_out) + [fetch(up.at[6], q_out)]
    small += fetch_piece_columns(fetch, convs, 2 * LANES, w_out)
    count = second.shape[0]
    early = edge.shape[2]
    before = read_edge(edge)
    gated = value[...] * jax.nn.sigmoid(gate[...])
    for number in range(padded.shape[0]):
        span = slice(number * LANES, (number + 1) * LANES)
        padded[number, :early, :] = before[:, span]
        padded[number, early:, :] = gated[:, span]
    conv = tap_sums(padded, taps, kernel, count, [early - taps + 1 + k for k in range(taps)])
    conv_out[...] = conv
    normed = normalize(conv)[0]
    active = (normed * jax.nn.sigmoid(normed)).astype(BF)
    mask = mask_row(where[3])
    wait_all(small)
    reduced = (nn(active, p_out[...]) * mask).astype(BF)
    t_out[...] = reduced
    result = second[...] + nt(active, w_out[...]) + nn(reduced, q_out[...])
    third[...] = result
    rows_out[...] = normalize(result)[0].astype(BF)


def conv_forward(taps, where, second, value, gate, edge, kernel, convs, down, up):
    count, width = second.shape
    ranks = NADAPT * RANK

    def body(*refs):
        conv_body(taps, *refs)

    return run(
        body,
        "conv_forward",
        "v" * 5 + "a" * 10,
        [
            shape((count, width), F32),
            shape((count, width), F32),
            shape((count, width), BF),
            shape((count, ranks), BF),
        ],
        [
            pltpu.VMEM((width, width), BF),
            pltpu.VMEM((width, ranks), BF),
            pltpu.VMEM((ranks, width), BF),
            pltpu.VMEM((width // LANES, count + 32, LANES), F32),
            pltpu.SemaphoreType.DMA((17,)),
        ],
        [where, second, value, gate, edge, kernel, *convs, down, up],
        flops=2 * count * width * width,
    )


def conv_back_body(taps, where, grad, part, other, third, conv, t_in, *refs):
    convs = refs[:8]
    down, up = refs[8:10]
    result, grad_conv, edge, grads = refs[10:14]
    w_out, p_out, q_out, sems = refs[14:]
    fetch = Fetches(sems)
    small = fetch_rows(fetch, where, down.at[7], p_out) + [fetch(up.at[6], q_out)]
    small += fetch_piece_columns(fetch, convs, 2 * LANES, w_out)
    normed, scale = normalize(third[...])
    value = grad[...] + normalize_back(part[...] + other[...].astype(F32), normed, scale)
    result[...] = value
    full = value.astype(BF)
    mask = mask_row(where[3])
    pick = chosen_rows(where[3])
    wait_all(small)
    reduced = (nt(full, q_out[...]) * mask).astype(BF)
    active_grad = nn(full, w_out[...]) + nt(reduced, p_out[...])
    normed, scale = normalize(conv[...])
    sigma = jax.nn.sigmoid(normed)
    active = (normed * sigma).astype(BF)
    inner = normalize_back(active_grad * swish_slope(normed, sigma), normed, scale)
    grad_conv[...] = inner
    store_edge(edge, inner[: edge.shape[2]], 1 - where[0])
    store_absolute(where, grads, 0, nn(compact(pick, t_in[...]), full))
    found = nn(compact(pick, reduced), active)
    for number in range(8):
        store_relative(where, grads, RANK, found[:, number * LANES : (number + 1) * LANES], number)


def conv_back(taps, where, grad, part, other, third, conv, t_in, convs, down, up):
    count, width = grad.shape
    ranks = NADAPT * RANK

    def body(*refs):
        conv_back_body(taps, *refs)

    return run(
        body,
        "conv_backward",
        "v" * 6 + "a" * 10,
        [
            shape((count, width), F32),
            shape((count, width), F32),
            shape((2, 2, 32, width // 4), F32),
            shape((2, 2, 2, 2 * RANK, LANES), F32),
        ],
        [
            pltpu.VMEM((width, width), BF),
            pltpu.VMEM((width, ranks), BF),
            pltpu.VMEM((ranks, width), BF),
            pltpu.SemaphoreType.DMA((17,)),
        ],
        [where, grad, part, other, third, conv, t_in, *convs, down, up],
        flops=2 * count * width * width,
    )


def pair_back_body(
    taps, where, grad, grad_conv, edge, value, gate, kernel, second, t_pair, t_mix,
    m0, m1, m2, m3, partial, *refs
):
    heads, convs = refs[:8], refs[8:16]
    down, up = refs[16:18]
    result = refs[18]
    slots = refs[19:23]
    grads, mix_grads = refs[23:25]
    w_mix, w_value, w_gate, p_mix, q_mix, p_pair, q_value, q_gate, padded, sems = refs[25:]
    fetch = Fetches(sems)
    pairs = [fetch(down.at[4], p_pair)]
    pairs += fetch_columns(fetch, where, up.at[3], q_value)
    pairs += fetch_columns(fetch, where, up.at[4], q_gate)
    pairs += fetch_piece_columns(fetch, convs, 0, w_value)
    pairs += fetch_piece_columns(fetch, convs, LANES, w_gate)
    mixing = fetch_rows(fetch, where, down.at[6], p_mix) + [fetch(up.at[5], q_mix)]
    mixing += fetch_piece_columns(fetch, heads, 3 * LANES, w_mix)
    count = grad.shape[0]
    after = read_edge(edge)
    inner = grad_conv[...]
    for number in range(padded.shape[0]):
        span = slice(number * LANES, (number + 1) * LANES)
        padded[number, :count, :] = inner[:, span]
        padded[number, count:, :] = after[:, span]
    gated = tap_sums(padded, taps, kernel, count, [taps - 1 - k for k in range(taps)])
    sigma = jax.nn.sigmoid(gate[...])
    half = gated * sigma
    g_value = half.astype(BF)
    g_gate = (half * value[...] * (1.0 - sigma)).astype(BF)
    mask = mask_row(where[3])
    pick = chosen_rows(where[3])
    normed, scale = normalize(second[...])
    rows = normed.astype(BF)
    wait_all(pairs)
    reduced = ((nt(g_value, q_value[...]) + nt(g_gate, q_gate[...])) * mask).astype(BF)
    total = nt(g_value, w_value[...]) + nt(g_gate, w_gate[...]) + nt(reduced, p_pair[...])
    value_now = grad[...] + normalize_back(total, normed, scale)
    result[...] = value_now
    store_absolute(where, grads, 0, nn(compact(pick, reduced), rows))
    rank = compact(pick, t_pair[...])
    up_value = nn(rank, g_value)
    up_gate = nn(rank, g_gate)
    for number in range(8):
        span = slice(number * LANES, (number + 1) * LANES)
        store_relative(where, grads, 3 * RANK, up_value[:, span], number)
        store_relative(where, grads, 4 * RANK, up_gate[:, span], number)
    for side in range(2):
        for pair in range(2):
            for piece in range(2):
                grads[side, pair, piece, RANK : 3 * RANK, :] = partial[side, pair, piece]
    full = value_now.astype(BF)
    wait_all(mixing)
    reduced = (nt(full, q_mix[...]) * mask).astype(BF)
    mixed_grad = (nn(full, w_mix[...]) + nt(reduced, p_mix[...])).astype(BF)
    width = mixed_grad.shape[1] // 4
    for slot in range(4):
        slots[slot][...] = mixed_grad[:, slot * width : (slot + 1) * width]
    store_absolute(where, mix_grads, 0, nn(compact(pick, t_mix[...]), full))
    mixed = jnp.concatenate([m0[...], m1[...], m2[...], m3[...]], axis=1)
    found = nn(compact(pick, reduced), mixed)
    for number in range(8):
        span = slice(number * LANES, (number + 1) * LANES)
        store_relative(where, mix_grads, RANK, found[:, span], number)


def pair_back(
    taps, where, grad, grad_conv, edge, value, gate, kernel, second, t_pair, t_mix, mixed,
    partial, heads, convs, down, up
):
    count, width = grad.shape
    ranks = NADAPT * RANK
    square = pltpu.VMEM((width, width), BF)

    def body(*refs):
        pair_back_body(taps, *refs)

    found = run(
        body,
        "pair_backward",
        "v" * 14 + "a" * 18,
        [shape((count, width), F32)]
        + [shape((count, width // 4), BF)] * 4
        + [
            shape((2, 2, 2, 5 * RANK, LANES), F32),
            shape((2, 2, 2, 2 * RANK, LANES), F32),
        ],
        [
            square,
            square,
            square,
            pltpu.VMEM((width, ranks), BF),
            pltpu.VMEM((ranks, width), BF),
            pltpu.VMEM((width, ranks), BF),
            pltpu.VMEM((ranks, width), BF),
            pltpu.VMEM((ranks, width), BF),
            pltpu.VMEM((width // LANES, count + 32, LANES), F32),
            pltpu.SemaphoreType.DMA((50,)),
        ],
        [
            where, grad, grad_conv, edge, value, gate, kernel, second, t_pair, t_mix, *mixed,
            partial, *heads, *convs, down, up,
        ],
        flops=6 * count * width * width,
        room=52,
    )
    return (found[0], found[1:5], found[5], found[6])


def start_body(where, own, following, own_out, next_out):
    own_out[...] = normalize(own[...].astype(F32))[0].astype(BF)
    next_out[...] = normalize(following[...].astype(F32))[0].astype(BF)


def start_rows(where, own, following):
    count, width = own.shape
    return run(
        start_body, "start_rows", "vv", [shape((count, width), BF)] * 2, [], [where, own, following]
    )


def turn_body(where, third, part, other, cotangent, output, grad, half):
    fourth = third[...] + 0.5 * (part[...] + other[...].astype(F32))
    normed, scale = normalize(fourth)
    output[...] = normed.astype(BF)
    value = normalize_back(cotangent[...].astype(F32), normed, scale)
    grad[...] = value
    half[...] = (0.5 * value).astype(BF)


def turn(where, third, part, other, cotangent):
    count, width = third.shape
    return run(
        turn_body,
        "turn",
        "vvvv",
        [shape((count, width), BF), shape((count, width), F32), shape((count, width), BF)],
        [],
        [where, third, part, other, cotangent],
    )


def finish_body(where, grad, part, other, own, result):
    normed, scale = normalize(own[...].astype(F32))
    total = part[...] + other[...].astype(F32)
    result[...] = (grad[...] + normalize_back(total, normed, scale)).astype(BF)


def finish(where, grad, part, other, own):
    count, width = grad.shape
    return run(
        finish_body, "finish", "vvvv", [shape((count, width), BF)], [], [where, grad, part, other, own]
    )[0]


def expand_body(plan, spread, turned, found, *refs):
    kinds = sorted({kind for kind, _, _ in plan})
    outs = refs[-len(kinds) - len(plan) - 1 : -len(plan) - 1]
    held = refs[-len(plan) - 1 : -1]
    sems = refs[-1]
    copies = []
    for item, (kind, slot, starts) in enumerate(plan):
        column = len(starts) * LANES
        times = len(starts[0])
        for pair in range(2):
            for side in range(2):
                parts = []
                for rows in starts:
                    terms = [
                        found[:, side, pair ^ far, :, row : row + RANK, :].reshape(-1, LANES)
                        for far, row in enumerate(rows)
                    ]
                    parts.append(jnp.concatenate(terms, axis=0))
                value = jnp.concatenate(parts, axis=1)
                start = (2 * pair + side) * column
                if kind % 2 == 0:
                    whole = jnp.concatenate([spread[...]] * times, axis=0)
                    held[item][start : start + column, :] = tn(value, whole)
                else:
                    whole = jnp.concatenate([turned[...]] * times, axis=1)
                    held[item][:, start : start + column] = nn(whole, value)
        copy = pltpu.make_async_copy(held[item], outs[kinds.index(kind)].at[slot], sems.at[item])
        copy.start()
        copies.append(copy)
    wait_all(copies)


def expand_near_body(plan, near_count, where, spread, turned, *refs):
    pieces = refs[: 2 * near_count]
    kinds = len({kind for _, kind, _, _ in plan})
    outs = refs[-kinds - len(plan) - 1 : -len(plan) - 1]
    held = refs[-len(plan) - 1 : -1]
    sems = refs[-1]
    copies = []
    for item, (wide, kind, slot, group) in enumerate(plan):
        rows = slice(group * RANK, (group + 1) * RANK)
        order = [0, 1] if not wide else list(range(2, pieces[0].shape[1]))
        column = len(order) * LANES
        for near in range(near_count):
            parts = [
                jnp.concatenate(
                    [pieces[2 * near + core][:, n, rows, :].reshape(-1, LANES) for core in range(2)],
                    axis=0,
                )
                for n in order
            ]
            value = jnp.concatenate(parts, axis=1)
            pair, side = where[0] ^ (near % 2), where[2] ^ (near // 2)
            place = pl.ds(pl.multiple_of((2 * pair + side) * column, column), column)
            if kind % 2 == 0:
                held[item][place, :] = tn(value, spread[...])
            else:
                held[item][:, place] = nn(turned[...], value)
        at = sorted({k for _, k, _, _ in plan}).index(kind)
        copy = pltpu.make_async_copy(held[item], outs[at].at[slot], sems.at[item])
        copy.start()
        copies.append(copy)
    wait_all(copies)


def expand_near(plan, where, spread, turned, pieces, outs):
    kinds = sorted({kind for _, kind, _, _ in plan})
    held = [outs[kind].shape[1:] for _, kind, _, _ in plan]
    passed = [outs[k] for k in kinds]
    start = 3 + len(pieces)

    def body(*refs):
        expand_near_body(plan, len(pieces) // 2, *refs)

    result = pl.pallas_call(
        body,
        name="expand_near",
        in_specs=[SMEM_SPEC] + [VMEM_SPEC] * (2 + len(pieces)) + [ANY_SPEC] * len(passed),
        out_specs=[ANY_SPEC] * len(kinds),
        out_shape=[shape(outs[k].shape, F32) for k in kinds],
        scratch_shapes=[pltpu.VMEM(h, F32) for h in held]
        + [pltpu.SemaphoreType.DMA((len(plan),))],
        input_output_aliases={start + n: n for n in range(len(kinds))},
        compiler_params=pltpu.CompilerParams(vmem_limit_bytes=44 << 20),
        cost_estimate=pl.CostEstimate(flops=0, bytes_accessed=8 << 20, transcendentals=0),
    )(where, spread, turned, *pieces, *passed)
    outs = list(outs)
    for n, k in enumerate(kinds):
        outs[k] = result[n]
    return outs


def rows_of(base, blocks, rows, group, first=0):
    return [(base + n * rows + group * RANK,) for n in range(first, blocks)]


def expand(plan, spread, turned, found, outs):
    kinds = sorted({kind for kind, _, _ in plan})
    fresh = [isinstance(outs[k], jax.ShapeDtypeStruct) for k in kinds]
    held = [shape(outs[kind].shape[1:], F32) for kind, _, _ in plan]
    passed = [outs[k] for k, f in zip(kinds, fresh) if not f]
    aliases = {}
    for n, k in enumerate(kinds):
        if not fresh[n]:
            aliases[3 + len(aliases)] = n

    def body(*refs):
        expand_body(plan, *refs)

    result = pl.pallas_call(
        body,
        name="expand",
        in_specs=[VMEM_SPEC] * 3 + [ANY_SPEC] * len(passed),
        out_specs=[ANY_SPEC] * len(kinds),
        out_shape=[shape(outs[k].shape, F32) for k in kinds],
        scratch_shapes=[pltpu.VMEM(h.shape, F32) for h in held]
        + [pltpu.SemaphoreType.DMA((len(plan),))],
        input_output_aliases=aliases,
        compiler_params=pltpu.CompilerParams(vmem_limit_bytes=44 << 20),
        cost_estimate=pl.CostEstimate(flops=0, bytes_accessed=8 << 20, transcendentals=0),
    )(spread, turned, found, *passed)
    outs = list(outs)
    for n, k in enumerate(kinds):
        outs[k] = result[n]
    return outs


def join(own, other, bit, axis):
    return jnp.where(
        bit == 0,
        jnp.concatenate([own, other], axis=axis),
        jnp.concatenate([other, own], axis=axis),
    )


def part_of(value, index, count, axis):
    size = value.shape[axis] // count
    return lax.dynamic_slice_in_dim(value, index * size, size, axis)


class Place:
    def __init__(self):
        self.side = lax.axis_index("ctx")
        index = lax.axis_index("tp")
        self.pair = index // 2
        self.core = index % 2
        self.block = 2 * self.side + self.pair


def sequence_rows(value, place):
    own = lax.dynamic_index_in_dim(value, place.core, 0, keepdims=False)
    other = lax.dynamic_index_in_dim(value, 1 - place.core, 0, keepdims=False)
    return join(own, by_core(other), place.core, 1)


def own_rows(value, place):
    half = sequence_rows(value, place)
    mine = part_of(half, place.pair, 2, 0)
    theirs = part_of(half, 1 - place.pair, 2, 0)
    return join(mine, by_pair(theirs), place.pair, 1)


def all_rows(value, place):
    half = sequence_rows(value, place)
    full = join(half, by_pair(half), place.pair, 1)
    return part_of(full, place.pair, 2, 0), part_of(full, 1 - place.pair, 2, 0)


def feature_parts(value, place):
    mine = part_of(value, place.pair, 2, 1)
    theirs = part_of(value, 1 - place.pair, 2, 1)
    half = join(mine, by_pair(theirs), place.pair, 0)
    kept = part_of(half, place.core, 2, 1)[None]
    given = part_of(half, 1 - place.core, 2, 1)[None]
    return join(kept, by_core(given), place.core, 0)


def side_half(weight, place):
    return part_of(weight, place.side, 2, weight.ndim - 1)


def gathered(weight):
    return lax.all_gather(weight, "shard", axis=0, tiled=True)


def hidden_pieces(base):
    over = by_side(base)
    return [base, by_core(base), over, by_core(over)]


def whole_pieces(base):
    over = by_side(base)
    found = []
    for near in (base, over):
        far = by_pair(near)
        found += [near, by_core(near), far, by_core(far)]
    return found


def after(value, other):
    return lax.optimization_barrier((value, other))[0]


def line_order():
    count = lax.axis_size("shard")
    index = jnp.arange(count)
    return index if count > 8 else jnp.mod(lax.axis_index("shard") - index, count)


def around_shard(value):
    count = lax.axis_size("shard")
    if count > 8:
        return lax.all_gather(value, "shard", axis=0, tiled=False)
    found = [value]
    for shift in range(1, count):
        route = [(n, (n + shift) % count) for n in range(count)]
        found.append(lax.ppermute(value, "shard", route))
    return jnp.stack(found, axis=0)


def everywhere(value):
    flat = value.astype(BF).reshape(-1, LANES)
    found = lax.all_gather(flat, ("shard", "ctx", "tp"), axis=0, tiled=True)
    return found.reshape((-1, 2, 2, 2) + flat.shape)


def exchanged(slots):
    return [slots[0], by_pair(slots[1]), by_side(slots[2]), across(slots[3])]


def on_device(
    inputs,
    adapter_id,
    cotangent,
    ffn1_in,
    ffn1_out,
    query_w,
    key_w,
    value_w,
    out_w,
    conv_in_w,
    conv_kernel,
    conv_out_w,
    ffn2_in,
    ffn2_out,
    distance_table,
    adapt_down,
    adapt_down_ff,
    adapt_up,
    adapt_up_ff,
):
    place = Place()
    mine = lax.dynamic_index_in_dim(adapter_id, place.core, 0, keepdims=False)
    where = jnp.stack([place.pair, place.core, place.side, mine]).astype(jnp.int32)
    block = place.block.astype(jnp.int32)[None]
    adapters = (adapt_down, adapt_down_ff, adapt_up, adapt_up_ff)

    taps = conv_kernel.shape[0]
    core_kernel = jnp.concatenate([conv_kernel, by_core(conv_kernel)], axis=1)
    kernel = jnp.stack([core_kernel, by_pair(core_kernel)], axis=1).reshape(taps, 4, 2, -1)
    kernel = join(kernel[:, :, :1], kernel[:, :, 1:], place.side, 2)
    kernel = kernel.transpose(0, 2, 1, 3).reshape(taps, -1).astype(F32)

    ids = lax.all_gather(adapter_id, "shard", axis=0, tiled=True)
    eye = jnp.eye(RANK, dtype=BF)

    def spread_of(order):
        chosen = (order[:, None] == jnp.arange(NADAPT, dtype=jnp.int32)[None, :]).astype(BF)
        return (chosen[:, None, :, None] * eye[None, :, None, :]).reshape(-1, NADAPT * RANK)

    index = line_order()
    picked = index[:, None] == jnp.arange(index.shape[0])[None, :]
    near_ids = jnp.sum(jnp.where(picked[:, :, None], ids.reshape(1, -1, 2), 0), axis=1)
    near_ids = join(near_ids[:, :1], near_ids[:, 1:], place.core, 1).T.reshape(-1)
    spread, spread_near = spread_of(ids), spread_of(near_ids)
    turned, turned_near = spread.T, spread_near.T
    text = wide_table(distance_table)

    turning = own_rows(cotangent, place)
    settled = (kernel, text, spread, spread_near, turned, turned_near, turning)
    (kernel, text, spread, spread_near, turned, turned_near, turning) = lax.optimization_barrier(
        settled
    )

    base_in = gathered(side_half(ffn1_in, place))
    own, following = all_rows(inputs, place)
    rows_own, rows_next = start_rows(where, own, following)
    base_out = gathered(after(side_half(ffn1_out, place), (base_in, rows_own, rows_next)))
    in_side, in_core = by_side(base_in), by_core(base_in)
    local = jnp.concatenate(
        [side_half(w, place) for w in (query_w, key_w, value_w, out_w)], axis=1
    )
    base_heads = gathered(after(local, (base_out, in_side, in_core, turning, spread, kernel)))
    out_side, out_core = by_side(base_out), by_core(base_out)
    w1_in = [base_in, in_core, in_side, by_core(in_side)]
    pair_local = side_half(conv_in_w, place)
    local = jnp.concatenate(
        [pair_local[:, 0], pair_local[:, 1], side_half(conv_out_w, place)], axis=1
    )
    step = local.shape[1]
    local = jnp.concatenate([local, jnp.zeros_like(local[:, : step // 3])], axis=1)
    base_convs = gathered(after(local, (base_heads, out_side, out_core, w1_in[3])))
    w1_out = [base_out, out_core, out_side, by_core(out_side)]
    heads_side, heads_pair = by_side(base_heads), by_pair(base_heads)
    heads_core = by_core(base_heads)
    local = jnp.concatenate([side_half(w, place) for w in (ffn2_in, ffn2_out)], axis=1)
    part, send, pre, t_in, t_out = ffn(
        0, 0, 7, where, rows_own, rows_next, w1_in, w1_out, adapters
    )
    kept_one = (rows_own, rows_next, (pre, t_in, t_out))
    base_two = gathered(after(local, (base_convs, heads_side, heads_pair, heads_core, send)))
    other = by_pair(send)
    heads_far = by_side(heads_pair)
    heads = [base_heads, heads_core, heads_pair, by_core(heads_pair)]
    heads += [heads_side, by_core(heads_side), heads_far, by_core(after(heads_far, other))]
    base_convs = base_convs[:, :step]
    convs_pair = by_pair(after(base_convs, heads_pair))
    convs_side = by_side(after(base_convs, heads_far))

    first, slots, t_heads = heads_forward(
        where, own.astype(F32), part, other, heads, adapt_down, adapt_up
    )
    slots = exchanged(slots)
    convs_far = by_pair(after(convs_side, tuple(slots)))
    two_side = by_side(after(base_two, tuple(slots)))
    mixed, logs = attend(block, slots, text)
    convs = [base_convs, convs_pair, convs_side, convs_far]
    convs = [v for piece in convs for v in (piece, by_core(after(piece, mixed)))]
    mixed = exchanged([mixed[n] for n in range(4)])
    second, value, gate, edge, t_mix, t_pair = pair_forward(
        where, first, mixed, heads, convs, adapt_down, adapt_up
    )
    w2 = [base_two, by_core(after(base_two, mixed[0])), two_side, by_core(after(two_side, edge))]
    edge = lax.ppermute(edge, ("ctx", "tp"), NEXT)
    conv, third, rows_own, t_conv = conv_forward(
        taps, where, second, value, gate, edge, kernel, convs, adapt_down, adapt_up
    )
    rows_next = by_pair(rows_own)
    part, send, pre, t_in, t_out = ffn(1, 5, 8, where, rows_own, rows_next, w2, w2, adapters)
    kept_two = (rows_own, rows_next, (pre, t_in, t_out))

    output, grad, half = turn(where, third, part, by_pair(send), turning)
    part, send, sums_two = ffn_back(
        1, 5, 8, where, half, by_pair(half), *kept_two, w2, w2, adapters
    )
    grad, grad_conv, edge, partial = conv_back(
        taps, where, grad, part, by_pair(send), third, conv, t_conv, convs, adapt_down, adapt_up
    )
    came = after(by_side(after(sums_two[1], send)), grad_conv)
    sums_two = sums_two[0] + came
    edge = lax.ppermute(edge, ("ctx", "tp"), BEFORE)
    grad, grad_slots, conv_sums, partial = pair_back(
        taps, where, grad, grad_conv, edge, value, gate, kernel, second, t_pair, t_mix, mixed,
        partial, heads, convs, adapt_down, adapt_up,
    )
    found_two = everywhere(sums_two)
    grad_slots = exchanged(grad_slots)
    back = attend_back(block, slots, grad_slots, text, logs)
    output = feature_parts(output, place)
    back = exchanged([back[n] for n in range(4)])
    grad, half, head_sums = heads_back(
        after(where, output), grad, first, t_heads, back, partial, conv_sums, heads,
        adapt_down, adapt_up,
    )
    other_half = by_pair(half)
    head_sums = head_sums[0] + by_side(head_sums[1].astype(BF)).astype(F32)
    head_sums = head_sums[0] + by_pair(head_sums[1].astype(BF)).astype(F32)
    found_heads = everywhere(after(head_sums, other_half))
    outs = [shape(v.shape, F32) for v in (adapt_down, adapt_up, adapt_down_ff, adapt_up_ff)]
    ffn_blocks, ffn_rows = sums_two.shape[:2]
    plan = [
        (kind, slot, [(n * ffn_rows + g * RANK, (n + 2) * ffn_rows + g * RANK) for n in range(2)])
        for kind, slot, g in ((0, 5, 0), (1, 8, 1))
    ]
    plan += [
        (kind, 1, rows_of(0, ffn_blocks, ffn_rows, g, 4)) for kind, g in ((2, 0), (3, 1))
    ]
    outs = expand(plan, spread, turned, after(found_two, half), outs)
    part, send, sums_one = ffn_back(
        0, 0, 7, after(where, outs[0]), half, other_half, *kept_one, w1_in, w1_out, adapters
    )
    sums_one = sums_one[0] + by_side(sums_one[1].astype(BF)).astype(F32)
    sums_one = jnp.concatenate([sums_one[:2] + by_pair(sums_one[2:4]), sums_one[4:]], axis=0)
    line = around_shard(sums_one.astype(BF))
    pieces = [line, by_pair(line), by_side(line)]
    pieces.append(by_pair(pieces[2]))
    pieces = [v for piece in pieces for v in (piece, by_core(piece))]
    input_grad = finish(where, grad, part, by_pair(send), own)
    input_grad = feature_parts(input_grad, place).astype(F32)

    head_blocks, head_rows = head_sums.shape[:2]
    places = ((0, 1), (0, 2), (0, 3), (1, 5), (1, 0), (1, 1), (1, 2), (0, 6))
    places += ((0, 4), (1, 6), (0, 7), (1, 3), (1, 4))
    plan = [
        (kind, slot, rows_of(0, head_blocks, head_rows, g))
        for g, (kind, slot) in enumerate(places)
    ]
    outs = expand(plan, spread, turned, found_heads, outs)
    outs = expand_near(
        [(False, 0, 0, 0), (False, 1, 7, 1), (True, 2, 0, 0), (True, 3, 0, 1)],
        where, spread_near, turned_near, pieces, outs,
    )
    return (output, input_grad, outs[0], outs[2], outs[1], outs[3])


def solution(mesh):
    placed = (
        P("shard", "ctx", "tp"),
        P("shard"),
        P("shard", "ctx", "tp"),
        P("shard", "tp"),
        P("shard", "tp"),
        P("shard", "tp"),
        P("shard", "tp"),
        P("shard", "tp"),
        P("shard", "tp"),
        P("shard", None, "tp"),
        P(None, "tp"),
        P("shard", "tp"),
        P("shard", "tp"),
        P("shard", "tp"),
        P(),
        P(),
        P(),
        P(),
        P(),
    )
    return jax.shard_map(
        on_device,
        mesh=mesh,
        in_specs=placed,
        out_specs=(P("shard", "ctx", "tp"), P("shard", "ctx", "tp"), P(), P(), P(), P()),
        check_vma=False,
    )
```

```python
import jax
import jax.numpy as jnp
from jax import lax
from jax.experimental import pallas as pl
from jax.experimental.pallas import tpu as pltpu
from jax.sharding import PartitionSpec as P

LEFT = 64
RIGHT = 8
NADAPT = 8
RANK = 16
HEAD = 64
LANES = 128
eps = 1e-05
BF = jnp.bfloat16
F32 = jnp.float32

CORE = [(0, 1), (1, 0), (2, 3), (3, 2)]
PAIR = [(0, 2), (2, 0), (1, 3), (3, 1)]
SIDE = [(0, 1), (1, 0)]
ACROSS = [(s * 4 + t, (1 - s) * 4 + (t ^ 2)) for s in range(2) for t in range(4)]


def block_at(block, core):
    return (block // 2) * 4 + (block % 2) * 2 + core


NEXT = [(block_at(n, k), block_at(n + 1, k)) for n in range(3) for k in range(2)]
BEFORE = [(block_at(n + 1, k), block_at(n, k)) for n in range(3) for k in range(2)]


def by_core(value):
    return lax.ppermute(value, "tp", CORE)


def by_pair(value):
    return lax.ppermute(value, "tp", PAIR)


def by_side(value):
    return lax.ppermute(value, "ctx", SIDE)


def across(value):
    return lax.ppermute(value, ("ctx", "tp"), ACROSS)


def wide_table(table):
    place = jnp.arange(4*LANES, dtype=jnp.int32)
    index = jnp.where(place < 3*LANES, jnp.clip(place - LEFT, 0, LEFT+RIGHT), 0)
    pick = (index[:, None] == jnp.arange(table.shape[0], dtype=jnp.int32)[None, :]).astype(BF)
    rows = jnp.dot(pick, table, preferred_element_type=F32).astype(BF)
    return jnp.concatenate([rows, rows], axis=1)

def load_blocks(b_ref, sources, target, sems, parts):
    copies=[]
    for j, source in enumerate(sources):
        rows = source.shape[0]; cols = source.shape[1]//parts
        for part in range(parts):
            copies.append(pltpu.make_async_copy(
                source.at[:, part*cols:(part+1)*cols],
                target.at[part, pl.ds(pl.multiple_of((b_ref[0] ^ j)*rows, rows), rows), :],
                sems.at[j*parts+part]))
    for c in copies: c.start()
    for c in copies: c.wait()

def window(r0, length):
    lo=max(r0-LANES,0); hi=min(r0+2*LANES,length)
    return lo,hi

def biased(s, near, p, rows, length):
    parts=[]
    for sub in range(rows//LANES):
        r0=p*rows+sub*LANES
        e=near[sub*LANES:(sub+1)*LANES]
        band=pltpu.roll(e, 0, 1, stride=1, stride_axis=0)
        lo,hi=window(r0,length)
        pieces=[]
        if lo>0: pieces.append(jnp.broadcast_to(e[:,0:1],(LANES,lo)))
        pieces.append(band[:, lo-r0+LANES:hi-r0+LANES])
        if hi<length: pieces.append(jnp.broadcast_to(e[:,2*LANES-1:2*LANES],(LANES,length-hi)))
        parts.append(jnp.concatenate(pieces,axis=1))
    return s+jnp.concatenate(parts,axis=0)


def fwd_kernel(b_ref, s0,s1,s2,s3, text_ref, o_ref, lse_ref, qkv, sems):
    dc=pl.program_id(0); k=pl.program_id(1)
    @pl.when((dc==0)&(k==0))
    def _(): load_blocks(b_ref,(s0,s1,s2,s3),qkv,sems,2)
    rows=o_ref.shape[1]; length=qkv.shape[1]
    own=(lax.broadcasted_iota(jnp.int32,(rows,LANES),1)//64)==k
    key=qkv[dc,:,LANES:2*LANES]; val=qkv[dc,:,2*LANES:]
    for p in range(length//rows):
        q=qkv[dc,p*rows:(p+1)*rows,0:LANES].astype(F32)*0.125
        q=jnp.where(own,q,0.0).astype(BF)
        s=biased(nt(q,key),nt(q,text_ref[...]),p,rows,length)
        top=jnp.max(s,axis=-1,keepdims=True)
        e=jnp.exp(s-top)
        tot=jnp.sum(e,axis=-1,keepdims=True)
        o=jnp.dot(e.astype(BF),val,preferred_element_type=F32)/tot
        o=o.astype(BF)
        slot=p^b_ref[0]
        @pl.when(k==0)
        def _(): o_ref[slot]=o
        @pl.when(k==1)
        def _(): o_ref[slot]=jnp.where(own,o,o_ref[slot])
        lse_ref[0,p*rows:(p+1)*rows,:]=top+jnp.log(tot)

def attend(b, slots, text):
    rows=slots[0].shape[0]; n=len(slots); length=rows*n
    anys=[pl.BlockSpec(memory_space=pl.ANY)]*n
    return pl.pallas_call(
        fwd_kernel,
        grid_spec=pltpu.PrefetchScalarGridSpec(
            num_scalar_prefetch=1, grid=(2,2),
            in_specs=anys+[pl.BlockSpec(text.shape,lambda d,k,b:(0,0))],
            out_specs=(pl.BlockSpec((n,rows,LANES),lambda d,k,b:(0,0,d)),
                       pl.BlockSpec((1,length,1),lambda d,k,b:(2*d+k,0,0))),
            scratch_shapes=[pltpu.VMEM((2,length,3*LANES),BF),pltpu.SemaphoreType.DMA((2*n,))]),
        out_shape=(jax.ShapeDtypeStruct((n,rows,2*LANES),BF),jax.ShapeDtypeStruct((4,length,1),F32)),
        compiler_params=pltpu.CompilerParams(vmem_limit_bytes=48<<20),
        name="attend",
        cost_estimate=pl.CostEstimate(flops=4*4*length*length*64,bytes_accessed=length*8*LANES*2,transcendentals=4*length*length),
    )(b,*slots,text)

def bwd_kernel(b_ref, s0,s1,s2,s3, g0,g1,g2,g3, text_ref, lse_ref, out_ref, qkv, gout, dq_acc, dk_acc, dv_acc, sems, gsems):
    dc=pl.program_id(0); k=pl.program_id(1)
    @pl.when((dc==0)&(k==0))
    def _():
        load_blocks(b_ref,(s0,s1,s2,s3),qkv,sems,2)
        load_blocks(b_ref,(g0,g1,g2,g3),gout,gsems,2)
    rows=out_ref.shape[1]; length=qkv.shape[1]
    own=(lax.broadcasted_iota(jnp.int32,(rows,LANES),1)//64)==k
    key=qkv[dc,:,LANES:2*LANES]; val=qkv[dc,:,2*LANES:]
    text=text_ref[...]
    turn=((lax.broadcasted_iota(jnp.int32,(LANES,LANES),0)+lax.broadcasted_iota(jnp.int32,(LANES,LANES),1))==LANES-1).astype(BF)
    @pl.when(k==0)
    def _():
        dk_acc[...]=jnp.zeros_like(dk_acc); dv_acc[...]=jnp.zeros_like(dv_acc)
    for p in range(length//rows):
        span=slice(p*rows,(p+1)*rows)
        q=qkv[dc,span,0:LANES].astype(F32)*0.125
        q=jnp.where(own,q,0.0).astype(BF)
        g=jnp.where(own,gout[dc,span,:].astype(F32),0.0).astype(BF)
        s=biased(nt(q,key),nt(q,text),p,rows,length)
        pr=jnp.exp(s-lse_ref[0,span,:])
        dp=nt(g,val)
        w=pr*dp
        ds=(w-pr*jnp.sum(w,axis=-1,keepdims=True)).astype(BF)
        dv_acc[...]+=tn(g,pr.astype(BF))
        dk_acc[...]+=tn(q,ds)
        dq=jnp.dot(ds,key,preferred_element_type=F32)
        extra=[]
        t_lo=text[0:1,:].astype(F32); t_hi=text[2*LANES-1:2*LANES,:].astype(F32)
        for sub in range(rows//LANES):
            r0=p*rows+sub*LANES
            lo,hi=window(r0,length)
            d=ds[sub*LANES:(sub+1)*LANES].astype(F32)
            pieces=[]
            if lo-r0+LANES>0: pieces.append(jnp.zeros((LANES,lo-r0+LANES),F32))
            pieces.append(d[:,lo:hi])
            pieces.append(jnp.zeros((LANES,4*LANES-(hi-r0+LANES)),F32))
            w=jnp.concatenate(pieces,axis=1)
            w=jnp.dot(turn,w.astype(BF),preferred_element_type=F32)
            w=pltpu.roll(w,3*LANES+1,1,stride=1,stride_axis=0)
            w=jnp.dot(turn,w.astype(BF),preferred_element_type=F32)
            x=jnp.dot(w.astype(BF),text,preferred_element_type=F32)
            if lo>0: x+=jnp.sum(d[:,:lo],axis=-1,keepdims=True)*t_lo
            if hi<length: x+=jnp.sum(d[:,hi:],axis=-1,keepdims=True)*t_hi
            extra.append(x)
        dq=(dq+jnp.concatenate(extra,axis=0))*0.125
        dq_acc[span,:]=jnp.where(own,dq,dq_acc[span,:])
    @pl.when(k==1)
    def _():
        for p in range(length//rows):
            slot=p^b_ref[0]; span=slice(p*rows,(p+1)*rows)
            out_ref[slot,:,0:LANES]=dq_acc[span,:].astype(BF)
            out_ref[slot,:,LANES:2*LANES]=dk_acc[:,span].T.astype(BF)
            out_ref[slot,:,2*LANES:]=dv_acc[:,span].T.astype(BF)

def attend_back(b, slots, grads, text, lse):
    rows=slots[0].shape[0]; n=len(slots); length=rows*n
    anys=[pl.BlockSpec(memory_space=pl.ANY)]*(2*n)
    return pl.pallas_call(
        bwd_kernel,
        grid_spec=pltpu.PrefetchScalarGridSpec(
            num_scalar_prefetch=1, grid=(2,2),
            in_specs=anys+[pl.BlockSpec(text.shape,lambda d,k,b:(0,0)),pl.BlockSpec((1,length,1),lambda d,k,b:(2*d+k,0,0))],
            out_specs=pl.BlockSpec((n,rows,3*LANES),lambda d,k,b:(0,0,d)),
            scratch_shapes=[pltpu.VMEM((2,length,3*LANES),BF),pltpu.VMEM((2,length,LANES),BF),
              pltpu.VMEM((length,LANES),F32),pltpu.VMEM((LANES,length),F32),pltpu.VMEM((LANES,length),F32),
              pltpu.SemaphoreType.DMA((2*n,)),pltpu.SemaphoreType.DMA((2*n,))]),
        out_shape=jax.ShapeDtypeStruct((n,rows,6*LANES),BF),
        compiler_params=pltpu.CompilerParams(vmem_limit_bytes=30<<20),
        name="attend_back",
        cost_estimate=pl.CostEstimate(flops=10*4*length*length*64,bytes_accessed=length*14*LANES*2,transcendentals=4*length*length),
    )(b,*slots,*grads,text,lse)


def nn(first, second):
    return jnp.dot(first, second, preferred_element_type=F32)


def nt(first, second):
    return lax.dot_general(first, second, (((1,), (1,)), ((), ())), preferred_element_type=F32)


def tn(first, second):
    return lax.dot_general(first, second, (((0,), (0,)), ((), ())), preferred_element_type=F32)


def normalize(value):
    mean = jnp.mean(value, axis=-1, keepdims=True)
    square = jnp.mean(value * value, axis=-1, keepdims=True)
    scale = lax.rsqrt(square - mean * mean + eps)
    return ((value - mean) * scale, scale)


def normalize_back(grad, normed, scale):
    mean = jnp.mean(grad, axis=-1, keepdims=True)
    cross = jnp.mean(grad * normed, axis=-1, keepdims=True)
    return scale * (grad - mean - normed * cross)


def swish_slope(value, sigma):
    return sigma + value * sigma * (1.0 - sigma)


def mask_row(adapter):
    lanes = lax.broadcasted_iota(jnp.int32, (1, NADAPT * RANK), 1)
    return (lanes // RANK == adapter).astype(F32)


def chosen_rows(adapter):
    shape = (RANK, NADAPT * RANK)
    lanes = lax.broadcasted_iota(jnp.int32, shape, 1)
    rows = lax.broadcasted_iota(jnp.int32, shape, 0)
    return (lanes == rows + adapter * RANK).astype(BF)


def compact(pick, value):
    return nt(pick, value).astype(BF)


class Fetches:
    def __init__(self, sems):
        self.sems = sems
        self.used = 0

    def __call__(self, source, target):
        copy = pltpu.make_async_copy(source, target, self.sems.at[self.used])
        self.used += 1
        copy.start()
        return copy


def wait_all(copies):
    for copy in copies:
        copy.wait()


def block_of(where, number):
    side, pair, core = number // 4, (number // 2) % 2, number % 2
    return ((where[0] ^ pair) * 2 + (where[1] ^ core)) * 2 + (where[2] ^ side)


def fetch_columns(fetch, where, source, target):
    found = []
    for number in range(8):
        start = pl.multiple_of(block_of(where, number) * LANES, LANES)
        place = pl.ds(number * LANES, LANES)
        found.append(fetch(source.at[:, pl.ds(start, LANES)], target.at[:, place]))
    return found


def fetch_rows(fetch, where, source, target):
    found = []
    for number in range(8):
        start = pl.multiple_of(block_of(where, number) * LANES, LANES)
        place = pl.ds(number * LANES, LANES)
        found.append(fetch(source.at[pl.ds(start, LANES), :], target.at[place, :]))
    return found


def store_absolute(where, out, first, value):
    rows = value.shape[0]
    for number in range(8):
        pair, side, half = number // 4, (number // 2) % 2, number % 2
        out[side ^ where[2], pair ^ where[0], half, first : first + rows, :] = value[
            :, number * LANES : (number + 1) * LANES
        ]


def store_relative(where, out, first, value, number):
    side, pair, core = number // 4, (number // 2) % 2, number % 2
    out[(where[1] ^ core) ^ where[2], pair, where[2] ^ side, first : first + value.shape[0], :] = value


def store_edge(out, value, flip_side):
    rows = value.shape[0]
    width = value.shape[1] // 4
    for side in range(2):
        for pair in range(2):
            start = (2 * side + pair) * width
            out[side ^ flip_side, 1 - pair] = value[:, start : start + width]


def read_edge(edge):
    return jnp.concatenate([edge[s, p] for s in range(2) for p in range(2)], axis=1)


VMEM_SPEC = pl.BlockSpec(memory_space=pltpu.VMEM)
ANY_SPEC = pl.BlockSpec(memory_space=pltpu.HBM)
SMEM_SPEC = pl.BlockSpec(memory_space=pltpu.SMEM)


def run(body, name, places, outs, scratch, operands, flops=0, room=44, out_specs=None):
    specs = [SMEM_SPEC] + [VMEM_SPEC if p == "v" else ANY_SPEC for p in places]
    moved = sum(o.size * o.dtype.itemsize for o in list(operands[1:]) + list(outs))
    return pl.pallas_call(
        body,
        name=name,
        in_specs=specs,
        out_specs=out_specs or [VMEM_SPEC] * len(outs),
        out_shape=outs,
        scratch_shapes=scratch,
        compiler_params=pltpu.CompilerParams(vmem_limit_bytes=room << 20),
        cost_estimate=pl.CostEstimate(
            flops=flops, bytes_accessed=min(moved, 16 << 20), transcendentals=0
        ),
    )(*operands)


def shape(dims, dtype):
    return jax.ShapeDtypeStruct(dims, dtype)


def fetch_ffn_adapters(fetch, where, which, column, up_ff, down_ff, p_in, q_in, p_out):
    found = []
    for number in range(4):
        side, core = number // 2, number % 2
        start = (2 * where[0] + (where[1] ^ core)) * (2 * column) + (where[2] ^ side) * column
        start = pl.multiple_of(start, column)
        place = pl.ds(number * column, column)
        found.append(fetch(up_ff.at[which, :, pl.ds(start, column)], q_in.at[:, place]))
        found.append(fetch(down_ff.at[which, pl.ds(start, column), :], p_out.at[place, :]))
    return found


def ffn_body(which, down_at, up_at, column, where, own, following, *refs):
    ins, outs, ups = refs[:4], refs[4:8], refs[8:12]
    down, down_ff, up, up_ff = ups
    part, send, pre_out, t_in_out, t_out_out = refs[12:17]
    rows, w_in, w_out, p_in, q_in, p_out, q_out, pre, active, sems = refs[17:]
    fetch = Fetches(sems)
    count = own.shape[0]
    small = [fetch(down.at[down_at], p_in), fetch(up.at[up_at], q_out)]
    small += fetch_ffn_adapters(fetch, where, which, column, up_ff, down_ff, p_in, q_in, p_out)
    first = [
        fetch(r.at[:, pl.ds(0, column)], w_in.at[:, pl.ds(n * column, column)])
        for n, r in enumerate(ins)
    ]
    second = [
        fetch(r.at[:, pl.ds(r.shape[1] - column, column)], w_out.at[:, pl.ds(n * column, column)])
        for n, r in enumerate(outs)
    ]
    mask = mask_row(where[3])
    rows[:count] = own[...]
    rows[count:] = following[...]
    wait_all(small)
    t_in = (nn(rows[...], p_in[...]) * mask).astype(BF)
    t_in_out[...] = t_in
    t_out = jnp.zeros(t_in.shape, F32)
    saved = []
    for n in range(4):
        span = slice(n * column, (n + 1) * column)
        first[n].wait()
        value = nn(rows[...], w_in[:, span]) + nn(t_in, q_in[:, span])
        pre[n] = value
        saved.append(fetch(pre.at[n], pre_out.at[n]))
        act = (value * jax.nn.sigmoid(value)).astype(BF)
        active[:, span] = act
        t_out = t_out + nn(act, p_out[span, :])
    t_out = (t_out * mask).astype(BF)
    t_out_out[...] = t_out
    wait_all(second)
    width = w_out.shape[0] // 2
    for n in range(2):
        span = slice(n * width, (n + 1) * width)
        total = nt(active[...], w_out[span, :]) + nn(t_out, q_out[:, span])
        part[:, span] = total[:count]
        send[:, span] = total[count:].astype(BF)
    wait_all(saved)


def ffn(which, down_at, up_at, where, own, following, w_in, w_out, adapters):
    count, width = own.shape
    column = adapters[3].shape[2] // 8
    hidden = 4 * column
    ranks = NADAPT * RANK

    def body(*refs):
        ffn_body(which, down_at, up_at, column, *refs)

    return run(
        body,
        "hidden_forward",
        "vv" + "a" * 12,
        [
            shape((count, width), F32),
            shape((count, width), BF),
            shape((4, 2 * count, column), F32),
            shape((2 * count, ranks), BF),
            shape((2 * count, ranks), BF),
        ],
        [
            pltpu.VMEM((2 * count, width), BF),
            pltpu.VMEM((width, hidden), BF),
            pltpu.VMEM((width, hidden), BF),
            pltpu.VMEM((width, ranks), BF),
            pltpu.VMEM((ranks, hidden), BF),
            pltpu.VMEM((hidden, ranks), BF),
            pltpu.VMEM((ranks, width), BF),
            pltpu.VMEM((4, 2 * count, column), F32),
            pltpu.VMEM((2 * count, hidden), BF),
            pltpu.SemaphoreType.DMA((22,)),
        ],
        [where, own, following, *w_in, *w_out, *adapters],
        flops=8 * count * width * hidden,
        out_specs=[VMEM_SPEC, VMEM_SPEC, ANY_SPEC, VMEM_SPEC, VMEM_SPEC],
    )


def ffn_back_body(which, down_at, up_at, column, where, own, following, u_own, u_next, t_in, t_out, *refs):
    pre_in = refs[0]
    ins, outs, ups = refs[1:5], refs[5:9], refs[9:13]
    down, down_ff, up, up_ff = ups
    part, send, grads = refs[13:16]
    full, rows, w_in, w_out, p_in, q_in, p_out, q_out, pre, active, slope, sems = refs[16:]
    fetch = Fetches(sems)
    count = own.shape[0]
    small = [fetch(down.at[down_at], p_in), fetch(up.at[up_at], q_out)]
    small += fetch_ffn_adapters(fetch, where, which, column, up_ff, down_ff, p_in, q_in, p_out)
    second = []
    kept = []
    for n, r in enumerate(outs):
        source = r.at[:, pl.ds(r.shape[1] - column, column)]
        second.append(fetch(source, w_out.at[:, pl.ds(n * column, column)]))
        kept.append(fetch(pre_in.at[n], pre.at[n]))
    first = [
        fetch(r.at[:, pl.ds(0, column)], w_in.at[:, pl.ds(n * column, column)])
        for n, r in enumerate(ins)
    ]
    mask = mask_row(where[3])
    pick = chosen_rows(where[3])
    full[:count] = own[...]
    full[count:] = following[...]
    rows[:count] = u_own[...]
    rows[count:] = u_next[...]
    wait_all(small)
    r_out = (nt(full[...], q_out[...]) * mask).astype(BF)
    c_out = compact(pick, r_out)
    c_t_in = compact(pick, t_in[...])
    r_in = jnp.zeros(r_out.shape, F32)
    for n in range(4):
        span = slice(n * column, (n + 1) * column)
        second[n].wait()
        kept[n].wait()
        grad = nn(full[...], w_out[:, span]) + nt(r_out, p_out[span, :])
        value = pre[n]
        sigma = jax.nn.sigmoid(value)
        act = (value * sigma).astype(BF)
        grad = (grad * swish_slope(value, sigma)).astype(BF)
        slope[:, span] = grad
        r_in = r_in + nt(grad, q_in[:, span])
        side, core = n // 2, n % 2
        near = (where[1] ^ core) ^ where[2]
        far = where[2] ^ side
        both = jnp.concatenate([nn(c_out, act), nn(c_t_in, grad)], axis=0)
        for piece in range(column // LANES):
            grads[near, 4 + far * (column // LANES) + piece] = both[
                :, piece * LANES : (piece + 1) * LANES
            ]
    r_in = (r_in * mask).astype(BF)
    wait_all(first)
    width = w_in.shape[0] // 2
    for n in range(2):
        span = slice(n * width, (n + 1) * width)
        total = nt(slope[...], w_in[span, :]) + nt(r_in, p_in[span, :])
        part[:, span] = total[:count]
        send[:, span] = total[count:].astype(BF)
    narrow = jnp.concatenate(
        [nn(compact(pick, r_in), rows[...]), nn(compact(pick, t_out[...]), full[...])], axis=0
    )
    for number in range(8):
        pair, side, half = number // 4, (number // 2) % 2, number % 2
        grads[side ^ where[2], 2 * (pair ^ where[0]) + half] = narrow[
            :, number * LANES : (number + 1) * LANES
        ]


def ffn_back(which, down_at, up_at, where, own, following, u_own, u_next, kept, w_in, w_out, adapters):
    pre, t_in, t_out = kept
    count, width = own.shape
    column = adapters[3].shape[2] // 8
    hidden = 4 * column
    ranks = NADAPT * RANK

    def body(*refs):
        ffn_back_body(which, down_at, up_at, column, *refs)

    return run(
        body,
        "hidden_backward",
        "vvvvvv" + "a" * 13,
        [
            shape((count, width), F32),
            shape((count, width), BF),
            shape((2, 4 + 2 * column // LANES, 2 * RANK, LANES), F32),
        ],
        [
            pltpu.VMEM((2 * count, width), BF),
            pltpu.VMEM((2 * count, width), BF),
            pltpu.VMEM((width, hidden), BF),
            pltpu.VMEM((width, hidden), BF),
            pltpu.VMEM((width, ranks), BF),
            pltpu.VMEM((ranks, hidden), BF),
            pltpu.VMEM((hidden, ranks), BF),
            pltpu.VMEM((ranks, width), BF),
            pltpu.VMEM((4, 2 * count, column), F32),
            pltpu.VMEM((2 * count, hidden), BF),
            pltpu.VMEM((2 * count, hidden), BF),
            pltpu.SemaphoreType.DMA((22,)),
        ],
        [where, own, following, u_own, u_next, t_in, t_out, pre, *w_in, *w_out, *adapters],
        flops=8 * count * width * hidden,
    )


def fetch_heads(fetch, where, pieces, up, wide):
    width = pieces[0].shape[0]
    three = 3 * LANES
    found = []
    for number, piece in enumerate(pieces):
        slot, core = number // 2, number % 2
        found.append(
            fetch(
                piece.at[:, pl.ds(0, three)],
                wide.at[slot, pl.ds(0, width), pl.ds(core * three, three)],
            )
        )
        start = pl.multiple_of(block_of(where, number) * LANES, LANES)
        for kind in range(3):
            found.append(
                fetch(
                    up.at[kind, :, pl.ds(start, LANES)],
                    wide.at[
                        slot,
                        pl.ds(width + kind * LANES, LANES),
                        pl.ds(core * three + kind * LANES, LANES),
                    ],
                )
            )
    return found


def clear_heads(wide, width):
    for kind in range(3):
        span = slice(width + kind * LANES, width + (kind + 1) * LANES)
        for core in range(2):
            for other in range(3):
                if other != kind:
                    at = (core * 3 + other) * LANES
                    for slot in range(4):
                        wide[slot, span, at : at + LANES] = jnp.zeros((LANES, LANES), BF)


def heads_body(where, resid, part, other, *refs):
    pieces = refs[:8]
    down, up = refs[8:10]
    first = refs[10]
    slots = refs[11:15]
    t_out = refs[15]
    wide, thin, sems = refs[16:]
    width = resid.shape[1]
    fetch = Fetches(sems)
    small = [
        fetch(down.at[1 + kind], thin.at[:, pl.ds(kind * LANES, LANES)]) for kind in range(3)
    ]
    large = fetch_heads(fetch, where, pieces, up, wide)
    clear_heads(wide, width)
    value = resid[...] + 0.5 * (part[...] + other[...].astype(F32))
    first[...] = value
    rows = normalize(value)[0].astype(BF)
    mask = jnp.concatenate([mask_row(where[3])] * 3, axis=1)
    wait_all(small)
    reduced = (nn(rows, thin[...]) * mask).astype(BF)
    t_out[...] = reduced
    both = jnp.concatenate([rows, reduced], axis=1)
    for slot in range(4):
        wait_all(large[slot * 8 : slot * 8 + 8])
        slots[slot][...] = nn(both, wide[slot]).astype(BF)


def heads_forward(where, resid, part, other, pieces, down, up):
    count, width = resid.shape
    three = 3 * LANES
    found = run(
        heads_body,
        "heads_forward",
        "vvv" + "a" * 10,
        [shape((count, width), F32)]
        + [shape((count, 2 * three), BF)] * 4
        + [shape((count, three), BF)],
        [
            pltpu.VMEM((4, width + three, 2 * three), BF),
            pltpu.VMEM((width, three), BF),
            pltpu.SemaphoreType.DMA((35,)),
        ],
        [where, resid, part, other, *pieces, down, up],
        flops=2 * count * width * 3 * width,
    )
    return (found[0], found[1:5], found[5])


def heads_back_body(where, grad, first, t_in, g0, g1, g2, g3, partial, convs, *refs):
    pieces = refs[:8]
    down, up = refs[8:10]
    result, half, grads = refs[10:13]
    wide, thin, sems = refs[13:]
    width = grad.shape[1]
    three = 3 * LANES
    fetch = Fetches(sems)
    small = [
        fetch(down.at[1 + kind], thin.at[:, pl.ds(kind * LANES, LANES)]) for kind in range(3)
    ]
    large = fetch_heads(fetch, where, pieces, up, wide)
    clear_heads(wide, width)
    normed, scale = normalize(first[...])
    rows = normed.astype(BF)
    pick = chosen_rows(where[3])
    mask = jnp.concatenate([mask_row(where[3])] * 3, axis=1)
    ranks = [compact(pick, t_in[:, k * LANES : (k + 1) * LANES]) for k in range(3)]
    total = None
    for slot, g in enumerate((g0, g1, g2, g3)):
        wait_all(large[slot * 8 : slot * 8 + 8])
        term = nt(g[...], wide[slot])
        total = term if total is None else total + term
        for core in range(2):
            for kind in range(3):
                at = core * three + kind * LANES
                store_relative(
                    where, grads, (4 + kind) * RANK, nn(ranks[kind], g[:, at : at + LANES]),
                    2 * slot + core,
                )
    reduced = (total[:, width:] * mask).astype(BF)
    wait_all(small)
    total = total[:, :width] + nt(reduced, thin[...])
    value = grad[...] + normalize_back(total, normed, scale)
    result[...] = value
    half[...] = (0.5 * value).astype(BF)
    for kind in range(3):
        found = nn(compact(pick, reduced[:, kind * LANES : (kind + 1) * LANES]), rows)
        store_absolute(where, grads, kind * RANK, found)
    for side in range(2):
        for pair in range(2):
            for piece in range(2):
                grads[side, pair, piece, 3 * RANK : 4 * RANK, :] = partial[
                    side, pair, piece, :RANK, :
                ]
                grads[side, pair, piece, 7 * RANK : 8 * RANK, :] = partial[
                    side, pair, piece, RANK:, :
                ]
                grads[side, pair, piece, 8 * RANK :, :] = convs[side, pair, piece]


def heads_back(where, grad, first, t_in, slots, partial, convs, pieces, down, up):
    count, width = grad.shape
    three = 3 * LANES
    return run(
        heads_back_body,
        "heads_backward",
        "v" * 9 + "a" * 10,
        [
            shape((count, width), F32),
            shape((count, width), BF),
            shape((2, 2, 2, 13 * RANK, LANES), F32),
        ],
        [
            pltpu.VMEM((4, width + three, 2 * three), BF),
            pltpu.VMEM((width, three), BF),
            pltpu.SemaphoreType.DMA((35,)),
        ],
        [where, grad, first, t_in, *slots, partial, convs, *pieces, down, up],
        flops=2 * count * width * 3 * width,
    )


def fetch_piece_columns(fetch, pieces, at, target):
    found = []
    for number, piece in enumerate(pieces):
        found.append(
            fetch(piece.at[:, pl.ds(at, LANES)], target.at[:, pl.ds(number * LANES, LANES)])
        )
    return found


def pair_body(where, first, m0, m1, m2, m3, *refs):
    heads, convs = refs[:8], refs[8:16]
    down, up = refs[16:18]
    second, value_out, gate_out, edge, t_mix_out, t_pair_out = refs[18:24]
    w_mix, w_value, w_gate, p_mix, q_mix, p_pair, q_value, q_gate, sems = refs[24:]
    fetch = Fetches(sems)
    mixing = fetch_rows(fetch, where, down.at[6], p_mix) + [fetch(up.at[5], q_mix)]
    mixing += fetch_piece_columns(fetch, heads, 3 * LANES, w_mix)
    pairs = [fetch(down.at[4], p_pair)]
    pairs += fetch_columns(fetch, where, up.at[3], q_value)
    pairs += fetch_columns(fetch, where, up.at[4], q_gate)
    pairs += fetch_piece_columns(fetch, convs, 0, w_value)
    gates = fetch_piece_columns(fetch, convs, LANES, w_gate)
    mask = mask_row(where[3])
    mixed = jnp.concatenate([m0[...], m1[...], m2[...], m3[...]], axis=1)
    wait_all(mixing)
    t_mix = (nn(mixed, p_mix[...]) * mask).astype(BF)
    t_mix_out[...] = t_mix
    value = first[...] + nt(mixed, w_mix[...]) + nn(t_mix, q_mix[...])
    second[...] = value
    rows = normalize(value)[0].astype(BF)
    wait_all(pairs)
    t_pair = (nn(rows, p_pair[...]) * mask).astype(BF)
    t_pair_out[...] = t_pair
    value = nn(rows, w_value[...]) + nn(t_pair, q_value[...])
    value_out[...] = value
    wait_all(gates)
    gate = nn(rows, w_gate[...]) + nn(t_pair, q_gate[...])
    gate_out[...] = gate
    last = value.shape[0] - edge.shape[2]
    store_edge(edge, value[last:] * jax.nn.sigmoid(gate[last:]), where[0])


def pair_forward(where, first, mixed, heads, convs, down, up):
    count, width = first.shape
    ranks = NADAPT * RANK
    square = pltpu.VMEM((width, width), BF)
    return run(
        pair_body,
        "pair_forward",
        "v" * 5 + "a" * 18,
        [
            shape((count, width), F32),
            shape((count, width), F32),
            shape((count, width), F32),
            shape((2, 2, 32, width // 4), F32),
            shape((count, ranks), BF),
            shape((count, ranks), BF),
        ],
        [
            square,
            square,
            square,
            pltpu.VMEM((width, ranks), BF),
            pltpu.VMEM((ranks, width), BF),
            pltpu.VMEM((width, ranks), BF),
            pltpu.VMEM((ranks, width), BF),
            pltpu.VMEM((ranks, width), BF),
            pltpu.SemaphoreType.DMA((50,)),
        ],
        [where, first, *mixed, *heads, *convs, down, up],
        flops=6 * count * width * width,
    )


def tap_sums(padded, taps, kernel, count, starts):
    found = []
    for number in range(padded.shape[0]):
        span = slice(number * LANES, (number + 1) * LANES)
        total = None
        for tap in range(taps):
            term = kernel[tap : tap + 1, span] * padded[number, starts[tap] : starts[tap] + count, :]
            total = term if total is None else total + term
        found.append(total)
    return jnp.concatenate(found, axis=1)


def conv_body(taps, where, second, value, gate, edge, kernel, *refs):
    convs = refs[:8]
    down, up = refs[8:10]
    conv_out, third, rows_out, t_out = refs[10:14]
    w_out, p_out, q_out, padded, sems = refs[14:]
    fetch = Fetches(sems)
    small = fetch_rows(fetch, where, down.at[7], p_out) + [fetch(up.at[6], q_out)]
    small += fetch_piece_columns(fetch, convs, 2 * LANES, w_out)
    count = second.shape[0]
    early = edge.shape[2]
    before = read_edge(edge)
    gated = value[...] * jax.nn.sigmoid(gate[...])
    for number in range(padded.shape[0]):
        span = slice(number * LANES, (number + 1) * LANES)
        padded[number, :early, :] = before[:, span]
        padded[number, early:, :] = gated[:, span]
    conv = tap_sums(padded, taps, kernel, count, [early - taps + 1 + k for k in range(taps)])
    conv_out[...] = conv
    normed = normalize(conv)[0]
    active = (normed * jax.nn.sigmoid(normed)).astype(BF)
    mask = mask_row(where[3])
    wait_all(small)
    reduced = (nn(active, p_out[...]) * mask).astype(BF)
    t_out[...] = reduced
    result = second[...] + nt(active, w_out[...]) + nn(reduced, q_out[...])
    third[...] = result
    rows_out[...] = normalize(result)[0].astype(BF)


def conv_forward(taps, where, second, value, gate, edge, kernel, convs, down, up):
    count, width = second.shape
    ranks = NADAPT * RANK

    def body(*refs):
        conv_body(taps, *refs)

    return run(
        body,
        "conv_forward",
        "v" * 5 + "a" * 10,
        [
            shape((count, width), F32),
            shape((count, width), F32),
            shape((count, width), BF),
            shape((count, ranks), BF),
        ],
        [
            pltpu.VMEM((width, width), BF),
            pltpu.VMEM((width, ranks), BF),
            pltpu.VMEM((ranks, width), BF),
            pltpu.VMEM((width // LANES, count + 32, LANES), F32),
            pltpu.SemaphoreType.DMA((17,)),
        ],
        [where, second, value, gate, edge, kernel, *convs, down, up],
        flops=2 * count * width * width,
    )


def conv_back_body(taps, where, grad, part, other, third, conv, t_in, *refs):
    convs = refs[:8]
    down, up = refs[8:10]
    result, grad_conv, edge, grads = refs[10:14]
    w_out, p_out, q_out, sems = refs[14:]
    fetch = Fetches(sems)
    small = fetch_rows(fetch, where, down.at[7], p_out) + [fetch(up.at[6], q_out)]
    small += fetch_piece_columns(fetch, convs, 2 * LANES, w_out)
    normed, scale = normalize(third[...])
    value = grad[...] + normalize_back(part[...] + other[...].astype(F32), normed, scale)
    result[...] = value
    full = value.astype(BF)
    mask = mask_row(where[3])
    pick = chosen_rows(where[3])
    wait_all(small)
    reduced = (nt(full, q_out[...]) * mask).astype(BF)
    active_grad = nn(full, w_out[...]) + nt(reduced, p_out[...])
    normed, scale = normalize(conv[...])
    sigma = jax.nn.sigmoid(normed)
    active = (normed * sigma).astype(BF)
    inner = normalize_back(active_grad * swish_slope(normed, sigma), normed, scale)
    grad_conv[...] = inner
    store_edge(edge, inner[: edge.shape[2]], 1 - where[0])
    store_absolute(where, grads, 0, nn(compact(pick, t_in[...]), full))
    found = nn(compact(pick, reduced), active)
    for number in range(8):
        store_relative(where, grads, RANK, found[:, number * LANES : (number + 1) * LANES], number)


def conv_back(taps, where, grad, part, other, third, conv, t_in, convs, down, up):
    count, width = grad.shape
    ranks = NADAPT * RANK

    def body(*refs):
        conv_back_body(taps, *refs)

    return run(
        body,
        "conv_backward",
        "v" * 6 + "a" * 10,
        [
            shape((count, width), F32),
            shape((count, width), F32),
            shape((2, 2, 32, width // 4), F32),
            shape((2, 2, 2, 2 * RANK, LANES), F32),
        ],
        [
            pltpu.VMEM((width, width), BF),
            pltpu.VMEM((width, ranks), BF),
            pltpu.VMEM((ranks, width), BF),
            pltpu.SemaphoreType.DMA((17,)),
        ],
        [where, grad, part, other, third, conv, t_in, *convs, down, up],
        flops=2 * count * width * width,
    )


def pair_back_body(
    taps, where, grad, grad_conv, edge, value, gate, kernel, second, t_pair, t_mix,
    m0, m1, m2, m3, partial, *refs
):
    heads, convs = refs[:8], refs[8:16]
    down, up = refs[16:18]
    result = refs[18]
    slots = refs[19:23]
    grads, mix_grads = refs[23:25]
    w_mix, w_value, w_gate, p_mix, q_mix, p_pair, q_value, q_gate, padded, sems = refs[25:]
    fetch = Fetches(sems)
    pairs = [fetch(down.at[4], p_pair)]
    pairs += fetch_columns(fetch, where, up.at[3], q_value)
    pairs += fetch_columns(fetch, where, up.at[4], q_gate)
    pairs += fetch_piece_columns(fetch, convs, 0, w_value)
    pairs += fetch_piece_columns(fetch, convs, LANES, w_gate)
    mixing = fetch_rows(fetch, where, down.at[6], p_mix) + [fetch(up.at[5], q_mix)]
    mixing += fetch_piece_columns(fetch, heads, 3 * LANES, w_mix)
    count = grad.shape[0]
    after = read_edge(edge)
    inner = grad_conv[...]
    for number in range(padded.shape[0]):
        span = slice(number * LANES, (number + 1) * LANES)
        padded[number, :count, :] = inner[:, span]
        padded[number, count:, :] = after[:, span]
    gated = tap_sums(padded, taps, kernel, count, [taps - 1 - k for k in range(taps)])
    sigma = jax.nn.sigmoid(gate[...])
    half = gated * sigma
    g_value = half.astype(BF)
    g_gate = (half * value[...] * (1.0 - sigma)).astype(BF)
    mask = mask_row(where[3])
    pick = chosen_rows(where[3])
    normed, scale = normalize(second[...])
    rows = normed.astype(BF)
    wait_all(pairs)
    reduced = ((nt(g_value, q_value[...]) + nt(g_gate, q_gate[...])) * mask).astype(BF)
    total = nt(g_value, w_value[...]) + nt(g_gate, w_gate[...]) + nt(reduced, p_pair[...])
    value_now = grad[...] + normalize_back(total, normed, scale)
    result[...] = value_now
    store_absolute(where, grads, 0, nn(compact(pick, reduced), rows))
    rank = compact(pick, t_pair[...])
    up_value = nn(rank, g_value)
    up_gate = nn(rank, g_gate)
    for number in range(8):
        span = slice(number * LANES, (number + 1) * LANES)
        store_relative(where, grads, 3 * RANK, up_value[:, span], number)
        store_relative(where, grads, 4 * RANK, up_gate[:, span], number)
    for side in range(2):
        for pair in range(2):
            for piece in range(2):
                grads[side, pair, piece, RANK : 3 * RANK, :] = partial[side, pair, piece]
    full = value_now.astype(BF)
    wait_all(mixing)
    reduced = (nt(full, q_mix[...]) * mask).astype(BF)
    mixed_grad = (nn(full, w_mix[...]) + nt(reduced, p_mix[...])).astype(BF)
    width = mixed_grad.shape[1] // 4
    for slot in range(4):
        slots[slot][...] = mixed_grad[:, slot * width : (slot + 1) * width]
    store_absolute(where, mix_grads, 0, nn(compact(pick, t_mix[...]), full))
    mixed = jnp.concatenate([m0[...], m1[...], m2[...], m3[...]], axis=1)
    found = nn(compact(pick, reduced), mixed)
    for number in range(8):
        span = slice(number * LANES, (number + 1) * LANES)
        store_relative(where, mix_grads, RANK, found[:, span], number)


def pair_back(
    taps, where, grad, grad_conv, edge, value, gate, kernel, second, t_pair, t_mix, mixed,
    partial, heads, convs, down, up
):
    count, width = grad.shape
    ranks = NADAPT * RANK
    square = pltpu.VMEM((width, width), BF)

    def body(*refs):
        pair_back_body(taps, *refs)

    found = run(
        body,
        "pair_backward",
        "v" * 14 + "a" * 18,
        [shape((count, width), F32)]
        + [shape((count, width // 4), BF)] * 4
        + [
            shape((2, 2, 2, 5 * RANK, LANES), F32),
            shape((2, 2, 2, 2 * RANK, LANES), F32),
        ],
        [
            square,
            square,
            square,
            pltpu.VMEM((width, ranks), BF),
            pltpu.VMEM((ranks, width), BF),
            pltpu.VMEM((width, ranks), BF),
            pltpu.VMEM((ranks, width), BF),
            pltpu.VMEM((ranks, width), BF),
            pltpu.VMEM((width // LANES, count + 32, LANES), F32),
            pltpu.SemaphoreType.DMA((50,)),
        ],
        [
            where, grad, grad_conv, edge, value, gate, kernel, second, t_pair, t_mix, *mixed,
            partial, *heads, *convs, down, up,
        ],
        flops=6 * count * width * width,
        room=52,
    )
    return (found[0], found[1:5], found[5], found[6])


def start_body(where, own, following, own_out, next_out):
    own_out[...] = normalize(own[...].astype(F32))[0].astype(BF)
    next_out[...] = normalize(following[...].astype(F32))[0].astype(BF)


def start_rows(where, own, following):
    count, width = own.shape
    return run(
        start_body, "start_rows", "vv", [shape((count, width), BF)] * 2, [], [where, own, following]
    )


def turn_body(where, third, part, other, cotangent, output, grad, half):
    fourth = third[...] + 0.5 * (part[...] + other[...].astype(F32))
    normed, scale = normalize(fourth)
    output[...] = normed.astype(BF)
    value = normalize_back(cotangent[...].astype(F32), normed, scale)
    grad[...] = value
    half[...] = (0.5 * value).astype(BF)


def turn(where, third, part, other, cotangent):
    count, width = third.shape
    return run(
        turn_body,
        "turn",
        "vvvv",
        [shape((count, width), BF), shape((count, width), F32), shape((count, width), BF)],
        [],
        [where, third, part, other, cotangent],
    )


def finish_body(where, grad, part, other, own, result):
    normed, scale = normalize(own[...].astype(F32))
    total = part[...] + other[...].astype(F32)
    result[...] = (grad[...] + normalize_back(total, normed, scale)).astype(BF)


def finish(where, grad, part, other, own):
    count, width = grad.shape
    return run(
        finish_body, "finish", "vvvv", [shape((count, width), BF)], [], [where, grad, part, other, own]
    )[0]


def expand_body(plan, spread, turned, found, *refs):
    kinds = sorted({kind for kind, _, _ in plan})
    outs = refs[-len(kinds) - len(plan) - 1 : -len(plan) - 1]
    held = refs[-len(plan) - 1 : -1]
    sems = refs[-1]
    copies = []
    for item, (kind, slot, starts) in enumerate(plan):
        column = len(starts) * LANES
        times = len(starts[0])
        for pair in range(2):
            for side in range(2):
                parts = []
                for rows in starts:
                    terms = [
                        found[:, side, pair ^ far, :, row : row + RANK, :].reshape(-1, LANES)
                        for far, row in enumerate(rows)
                    ]
                    parts.append(jnp.concatenate(terms, axis=0))
                value = jnp.concatenate(parts, axis=1)
                start = (2 * pair + side) * column
                if kind % 2 == 0:
                    whole = jnp.concatenate([spread[...]] * times, axis=0)
                    held[item][start : start + column, :] = tn(value, whole)
                else:
                    whole = jnp.concatenate([turned[...]] * times, axis=1)
                    held[item][:, start : start + column] = nn(whole, value)
        copy = pltpu.make_async_copy(held[item], outs[kinds.index(kind)].at[slot], sems.at[item])
        copy.start()
        copies.append(copy)
    wait_all(copies)


def expand_near_body(plan, near_count, where, spread, turned, *refs):
    pieces = refs[: 2 * near_count]
    kinds = len({kind for _, kind, _, _ in plan})
    outs = refs[-kinds - len(plan) - 1 : -len(plan) - 1]
    held = refs[-len(plan) - 1 : -1]
    sems = refs[-1]
    copies = []
    def rows_at(near, block, rows):
        return [pieces[2 * near + core][:, block, rows, :].reshape(-1, LANES) for core in range(2)]

    for item, (wide, kind, slot, group) in enumerate(plan):
        rows = slice(group * RANK, (group + 1) * RANK)
        blocks = [0, 1] if not wide else list(range(4, pieces[0].shape[1]))
        column = len(blocks) * LANES
        times = 1 if wide else 2
        for near in range(near_count):
            parts = []
            for n in blocks:
                found = rows_at(near, n, rows)
                if not wide:
                    found += rows_at(near ^ 1, n + 2, rows)
                parts.append(jnp.concatenate(found, axis=0))
            value = jnp.concatenate(parts, axis=1)
            pair, side = where[0] ^ (near % 2), where[2] ^ (near // 2)
            place = pl.ds(pl.multiple_of((2 * pair + side) * column, column), column)
            if kind % 2 == 0:
                held[item][place, :] = tn(value, jnp.concatenate([spread[...]] * times, axis=0))
            else:
                held[item][:, place] = nn(jnp.concatenate([turned[...]] * times, axis=1), value)
        at = sorted({k for _, k, _, _ in plan}).index(kind)
        copy = pltpu.make_async_copy(held[item], outs[at].at[slot], sems.at[item])
        copy.start()
        copies.append(copy)
    wait_all(copies)


def expand_near(plan, where, spread, turned, pieces, outs):
    kinds = sorted({kind for _, kind, _, _ in plan})
    held = [outs[kind].shape[1:] for _, kind, _, _ in plan]
    passed = [outs[k] for k in kinds]
    start = 3 + len(pieces)

    def body(*refs):
        expand_near_body(plan, len(pieces) // 2, *refs)

    result = pl.pallas_call(
        body,
        name="expand_near",
        in_specs=[SMEM_SPEC] + [VMEM_SPEC] * (2 + len(pieces)) + [ANY_SPEC] * len(passed),
        out_specs=[ANY_SPEC] * len(kinds),
        out_shape=[shape(outs[k].shape, F32) for k in kinds],
        scratch_shapes=[pltpu.VMEM(h, F32) for h in held]
        + [pltpu.SemaphoreType.DMA((len(plan),))],
        input_output_aliases={start + n: n for n in range(len(kinds))},
        compiler_params=pltpu.CompilerParams(vmem_limit_bytes=44 << 20),
        cost_estimate=pl.CostEstimate(flops=0, bytes_accessed=8 << 20, transcendentals=0),
    )(where, spread, turned, *pieces, *passed)
    outs = list(outs)
    for n, k in enumerate(kinds):
        outs[k] = result[n]
    return outs


def rows_of(base, blocks, rows, group, first=0):
    return [(base + n * rows + group * RANK,) for n in range(first, blocks)]


def expand(plan, spread, turned, found, outs):
    kinds = sorted({kind for kind, _, _ in plan})
    fresh = [isinstance(outs[k], jax.ShapeDtypeStruct) for k in kinds]
    held = [shape(outs[kind].shape[1:], F32) for kind, _, _ in plan]
    passed = [outs[k] for k, f in zip(kinds, fresh) if not f]
    aliases = {}
    for n, k in enumerate(kinds):
        if not fresh[n]:
            aliases[3 + len(aliases)] = n

    def body(*refs):
        expand_body(plan, *refs)

    result = pl.pallas_call(
        body,
        name="expand",
        in_specs=[VMEM_SPEC] * 3 + [ANY_SPEC] * len(passed),
        out_specs=[ANY_SPEC] * len(kinds),
        out_shape=[shape(outs[k].shape, F32) for k in kinds],
        scratch_shapes=[pltpu.VMEM(h.shape, F32) for h in held]
        + [pltpu.SemaphoreType.DMA((len(plan),))],
        input_output_aliases=aliases,
        compiler_params=pltpu.CompilerParams(vmem_limit_bytes=44 << 20),
        cost_estimate=pl.CostEstimate(flops=0, bytes_accessed=8 << 20, transcendentals=0),
    )(spread, turned, found, *passed)
    outs = list(outs)
    for n, k in enumerate(kinds):
        outs[k] = result[n]
    return outs


def join(own, other, bit, axis):
    return jnp.where(
        bit == 0,
        jnp.concatenate([own, other], axis=axis),
        jnp.concatenate([other, own], axis=axis),
    )


def part_of(value, index, count, axis):
    size = value.shape[axis] // count
    return lax.dynamic_slice_in_dim(value, index * size, size, axis)


class Place:
    def __init__(self):
        self.side = lax.axis_index("ctx")
        index = lax.axis_index("tp")
        self.pair = index // 2
        self.core = index % 2
        self.block = 2 * self.side + self.pair


def sequence_rows(value, place):
    own = lax.dynamic_index_in_dim(value, place.core, 0, keepdims=False)
    other = lax.dynamic_index_in_dim(value, 1 - place.core, 0, keepdims=False)
    return join(own, by_core(other), place.core, 1)


def own_rows(value, place):
    half = sequence_rows(value, place)
    mine = part_of(half, place.pair, 2, 0)
    theirs = part_of(half, 1 - place.pair, 2, 0)
    return join(mine, by_pair(theirs), place.pair, 1)


def all_rows(value, place):
    half = sequence_rows(value, place)
    full = join(half, by_pair(half), place.pair, 1)
    return part_of(full, place.pair, 2, 0), part_of(full, 1 - place.pair, 2, 0)


def feature_parts(value, place):
    mine = part_of(value, place.pair, 2, 1)
    theirs = part_of(value, 1 - place.pair, 2, 1)
    half = join(mine, by_pair(theirs), place.pair, 0)
    kept = part_of(half, place.core, 2, 1)[None]
    given = part_of(half, 1 - place.core, 2, 1)[None]
    return join(kept, by_core(given), place.core, 0)


def side_half(weight, place):
    return part_of(weight, place.side, 2, weight.ndim - 1)


def gathered(weight):
    return lax.all_gather(weight, "shard", axis=0, tiled=True)


def hidden_pieces(base):
    over = by_side(base)
    return [base, by_core(base), over, by_core(over)]


def whole_pieces(base):
    over = by_side(base)
    found = []
    for near in (base, over):
        far = by_pair(near)
        found += [near, by_core(near), far, by_core(far)]
    return found


def after(value, other):
    return lax.optimization_barrier((value, other))[0]


def line_order():
    count = lax.axis_size("shard")
    index = jnp.arange(count)
    return index if count > 8 else jnp.mod(lax.axis_index("shard") - index, count)


def around_shard(value):
    count = lax.axis_size("shard")
    if count > 8:
        return lax.all_gather(value, "shard", axis=0, tiled=False)
    found = [value]
    for shift in range(1, count):
        route = [(n, (n + shift) % count) for n in range(count)]
        found.append(lax.ppermute(value, "shard", route))
    return jnp.stack(found, axis=0)


def everywhere(value):
    flat = value.astype(BF).reshape(-1, LANES)
    found = lax.all_gather(flat, ("shard", "ctx", "tp"), axis=0, tiled=True)
    return found.reshape((-1, 2, 2, 2) + flat.shape)


def exchanged(slots):
    return [slots[0], by_pair(slots[1]), by_side(slots[2]), across(slots[3])]


def on_device(
    inputs,
    adapter_id,
    cotangent,
    ffn1_in,
    ffn1_out,
    query_w,
    key_w,
    value_w,
    out_w,
    conv_in_w,
    conv_kernel,
    conv_out_w,
    ffn2_in,
    ffn2_out,
    distance_table,
    adapt_down,
    adapt_down_ff,
    adapt_up,
    adapt_up_ff,
):
    place = Place()
    mine = lax.dynamic_index_in_dim(adapter_id, place.core, 0, keepdims=False)
    where = jnp.stack([place.pair, place.core, place.side, mine]).astype(jnp.int32)
    block = place.block.astype(jnp.int32)[None]
    adapters = (adapt_down, adapt_down_ff, adapt_up, adapt_up_ff)

    taps = conv_kernel.shape[0]
    core_kernel = jnp.concatenate([conv_kernel, by_core(conv_kernel)], axis=1)
    kernel = jnp.stack([core_kernel, by_pair(core_kernel)], axis=1).reshape(taps, 4, 2, -1)
    kernel = join(kernel[:, :, :1], kernel[:, :, 1:], place.side, 2)
    kernel = kernel.transpose(0, 2, 1, 3).reshape(taps, -1).astype(F32)

    ids = lax.all_gather(adapter_id, "shard", axis=0, tiled=True)
    eye = jnp.eye(RANK, dtype=BF)

    def spread_of(order):
        chosen = (order[:, None] == jnp.arange(NADAPT, dtype=jnp.int32)[None, :]).astype(BF)
        return (chosen[:, None, :, None] * eye[None, :, None, :]).reshape(-1, NADAPT * RANK)

    index = line_order()
    picked = index[:, None] == jnp.arange(index.shape[0])[None, :]
    near_ids = jnp.sum(jnp.where(picked[:, :, None], ids.reshape(1, -1, 2), 0), axis=1)
    near_ids = join(near_ids[:, :1], near_ids[:, 1:], place.core, 1).T.reshape(-1)
    spread, spread_near = spread_of(ids), spread_of(near_ids)
    turned, turned_near = spread.T, spread_near.T
    text = wide_table(distance_table)

    turning = own_rows(cotangent, place)
    settled = (kernel, text, spread, spread_near, turned, turned_near, turning)
    (kernel, text, spread, spread_near, turned, turned_near, turning) = lax.optimization_barrier(
        settled
    )

    base_in = gathered(side_half(ffn1_in, place))
    own, following = all_rows(inputs, place)
    rows_own, rows_next = start_rows(where, own, following)
    base_out = gathered(after(side_half(ffn1_out, place), (base_in, rows_own, rows_next)))
    in_side, in_core = by_side(base_in), by_core(base_in)
    local = jnp.concatenate(
        [side_half(w, place) for w in (query_w, key_w, value_w, out_w)], axis=1
    )
    base_heads = gathered(after(local, (base_out, in_side, in_core, turning, spread, kernel)))
    out_side, out_core = by_side(base_out), by_core(base_out)
    w1_in = [base_in, in_core, in_side, by_core(in_side)]
    pair_local = side_half(conv_in_w, place)
    local = jnp.concatenate(
        [pair_local[:, 0], pair_local[:, 1], side_half(conv_out_w, place)], axis=1
    )
    step = local.shape[1]
    local = jnp.concatenate([local, jnp.zeros_like(local[:, : step // 3])], axis=1)
    base_convs = gathered(after(local, (base_heads, out_side, out_core, w1_in[3])))
    w1_out = [base_out, out_core, out_side, by_core(out_side)]
    heads_side, heads_pair = by_side(base_heads), by_pair(base_heads)
    heads_core = by_core(base_heads)
    local = jnp.concatenate([side_half(w, place) for w in (ffn2_in, ffn2_out)], axis=1)
    part, send, pre, t_in, t_out = ffn(
        0, 0, 7, where, rows_own, rows_next, w1_in, w1_out, adapters
    )
    kept_one = (rows_own, rows_next, (pre, t_in, t_out))
    base_two = gathered(after(local, (base_convs, heads_side, heads_pair, heads_core, send)))
    other = by_pair(send)
    heads_far = by_side(heads_pair)
    heads = [base_heads, heads_core, heads_pair, by_core(heads_pair)]
    heads += [heads_side, by_core(heads_side), heads_far, by_core(after(heads_far, other))]
    base_convs = base_convs[:, :step]
    convs_pair = by_pair(after(base_convs, heads_pair))
    convs_side = by_side(after(base_convs, heads_far))

    first, slots, t_heads = heads_forward(
        where, own.astype(F32), part, other, heads, adapt_down, adapt_up
    )
    slots = exchanged(slots)
    convs_far = by_pair(after(convs_side, tuple(slots)))
    two_side = by_side(after(base_two, tuple(slots)))
    mixed, logs = attend(block, slots, text)
    convs = [base_convs, convs_pair, convs_side, convs_far]
    convs = [v for piece in convs for v in (piece, by_core(after(piece, mixed)))]
    mixed = exchanged([mixed[n] for n in range(4)])
    second, value, gate, edge, t_mix, t_pair = pair_forward(
        where, first, mixed, heads, convs, adapt_down, adapt_up
    )
    w2 = [base_two, by_core(after(base_two, mixed[0])), two_side, by_core(after(two_side, edge))]
    edge = lax.ppermute(edge, ("ctx", "tp"), NEXT)
    conv, third, rows_own, t_conv = conv_forward(
        taps, where, second, value, gate, edge, kernel, convs, adapt_down, adapt_up
    )
    rows_next = by_pair(rows_own)
    part, send, pre, t_in, t_out = ffn(1, 5, 8, where, rows_own, rows_next, w2, w2, adapters)
    kept_two = (rows_own, rows_next, (pre, t_in, t_out))

    output, grad, half = turn(where, third, part, by_pair(send), turning)
    part, send, sums_two = ffn_back(
        1, 5, 8, where, half, by_pair(half), *kept_two, w2, w2, adapters
    )
    grad, grad_conv, edge, partial = conv_back(
        taps, where, grad, part, by_pair(send), third, conv, t_conv, convs, adapt_down, adapt_up
    )
    came = after(by_side(after(sums_two[1], send)), grad_conv)
    sums_two = sums_two[0] + came
    edge = lax.ppermute(edge, ("ctx", "tp"), BEFORE)
    grad, grad_slots, conv_sums, partial = pair_back(
        taps, where, grad, grad_conv, edge, value, gate, kernel, second, t_pair, t_mix, mixed,
        partial, heads, convs, adapt_down, adapt_up,
    )
    found_two = everywhere(sums_two)
    grad_slots = exchanged(grad_slots)
    back = attend_back(block, slots, grad_slots, text, logs)
    output = feature_parts(output, place)
    back = exchanged([back[n] for n in range(4)])
    grad, half, head_sums = heads_back(
        after(where, output), grad, first, t_heads, back, partial, conv_sums, heads,
        adapt_down, adapt_up,
    )
    other_half = by_pair(half)
    head_sums = head_sums[0] + by_side(head_sums[1].astype(BF)).astype(F32)
    head_sums = head_sums[0] + by_pair(head_sums[1].astype(BF)).astype(F32)
    found_heads = everywhere(after(head_sums, other_half))
    outs = [shape(v.shape, F32) for v in (adapt_down, adapt_up, adapt_down_ff, adapt_up_ff)]
    ffn_blocks, ffn_rows = sums_two.shape[:2]
    plan = [
        (kind, slot, [(n * ffn_rows + g * RANK, (n + 2) * ffn_rows + g * RANK) for n in range(2)])
        for kind, slot, g in ((0, 5, 0), (1, 8, 1))
    ]
    plan += [
        (kind, 1, rows_of(0, ffn_blocks, ffn_rows, g, 4)) for kind, g in ((2, 0), (3, 1))
    ]
    outs = expand(plan, spread, turned, after(found_two, half), outs)
    part, send, sums_one = ffn_back(
        0, 0, 7, after(where, outs[0]), half, other_half, *kept_one, w1_in, w1_out, adapters
    )
    sums_one = sums_one[0] + by_side(sums_one[1].astype(BF)).astype(F32)
    line = around_shard(sums_one.astype(BF))
    pieces = [line, by_pair(line), by_side(line)]
    pieces.append(by_pair(pieces[2]))
    pieces = [v for piece in pieces for v in (piece, by_core(piece))]
    input_grad = finish(where, grad, part, by_pair(send), own)
    input_grad = feature_parts(input_grad, place).astype(F32)

    head_blocks, head_rows = head_sums.shape[:2]
    places = ((0, 1), (0, 2), (0, 3), (1, 5), (1, 0), (1, 1), (1, 2), (0, 6))
    places += ((0, 4), (1, 6), (0, 7), (1, 3), (1, 4))
    plan = [
        (kind, slot, rows_of(0, head_blocks, head_rows, g))
        for g, (kind, slot) in enumerate(places)
    ]
    outs = expand_near(
        [(False, 0, 0, 0), (False, 1, 7, 1), (True, 2, 0, 0), (True, 3, 0, 1)],
        where, spread_near, turned_near, pieces, outs,
    )
    outs = expand(plan, spread, turned, found_heads, outs)
    return (output, input_grad, outs[0], outs[2], outs[1], outs[3])


def solution(mesh):
    placed = (
        P("shard", "ctx", "tp"),
        P("shard"),
        P("shard", "ctx", "tp"),
        P("shard", "tp"),
        P("shard", "tp"),
        P("shard", "tp"),
        P("shard", "tp"),
        P("shard", "tp"),
        P("shard", "tp"),
        P("shard", None, "tp"),
        P(None, "tp"),
        P("shard", "tp"),
        P("shard", "tp"),
        P("shard", "tp"),
        P(),
        P(),
        P(),
        P(),
        P(),
    )
    return jax.shard_map(
        on_device,
        mesh=mesh,
        in_specs=placed,
        out_specs=(P("shard", "ctx", "tp"), P("shard", "ctx", "tp"), P(), P(), P(), P()),
        check_vma=False,
    )
```
